32 devices in a mesh: fsdp: 8 (over z, core), seq: 4 (over y, x).
Axes of the slice: x: 2, y: 2, z: 4, core: 2. Of those that a mesh axis runs over, the one named last changes fastest.
Arguments:
- hidden_in: bfloat16 [8192, 1536], P(('fsdp', 'seq')), may hold values from -12 to 12
- cotangent: bfloat16 [8192, 1536], P(('fsdp', 'seq')), may hold values from -6 to 6
- segment_ids: int32 [8, 1024], P('fsdp', 'seq'), may hold values from 0 to 3, never falling along the last dimension, each value on 1 to 512 neighbouring positions
- w_qkv: bfloat16 [1536, 3072], P('fsdp', 'seq'), may hold values from -1.5 to 1.5
- w_out: bfloat16 [1536, 1536], P('fsdp', 'seq'), may hold values from -0.625 to 0.625
- w_gate: bfloat16 [1536, 4096], P('fsdp', 'seq'), may hold values from -0.15625 to 0.15625
- w_up: bfloat16 [1536, 4096], P('fsdp', 'seq'), may hold values from -0.15625 to 0.15625
- w_down: bfloat16 [4096, 1536], P('fsdp', 'seq'), may hold values from -0.09375 to 0.09375
- gain_attn: bfloat16 [1536], P(('fsdp', 'seq')), may hold values from 0.099609375 to 1.8984375
- gain_mlp: bfloat16 [1536], P(('fsdp', 'seq')), may hold values from 0.099609375 to 1.8984375
Outputs:
- output: float32 [8192, 1536], P(('fsdp', 'seq'))
- d_input: float32 [8192, 1536], P(('fsdp', 'seq'))
- g_qkv: float32 [1536, 3072], P('fsdp', 'seq')
- g_out: float32 [1536, 1536], P('fsdp', 'seq')
- g_gate: float32 [1536, 4096], P('fsdp', 'seq')
- g_up: float32 [1536, 4096], P('fsdp', 'seq')
- g_down: float32 [4096, 1536], P('fsdp', 'seq')
- g_gain_attn: float32 [1536], P(('fsdp', 'seq'))
- g_gain_mlp: float32 [1536], P(('fsdp', 'seq'))
The draws below stay inside these ranges and needn't reach their ends.
Inputs may be any that keep to these rules, and one draw needn't show every extreme that they name: `segment_ids`: document numbers never fall along a row; a document has 1 to 512 tokens.
All inputs are finite; a program needn't handle non-finite values.
Results may differ from the reference program's by a relative error of at most 0.02.
Values may be sent and summed in bfloat16 or wider, within the bound.
A program may use at most 320 MiB of HBM per device.

```python
import math
import jax
import jax.numpy as jnp
import numpy as np
from jax import lax

D = 1536
H = 16
HEAD_DIM = 96
FF = 4096
DOCS = 4
QKV_COLS = 3072
LEN = 1024
TOKENS = 8192
N_FSDP = 8


def draw_hidden_in(key, part):
    key_rows, key_cols, key_noise = jax.random.split(jax.random.fold_in(key, 11), 3)
    row_scales = jnp.exp(jax.random.uniform(key_rows, (TOKENS, 1), jnp.float32, math.log(0.3), math.log(3.0)))
    col_scales = jnp.exp(jax.random.uniform(key_cols, (1, D), jnp.float32, math.log(0.5), math.log(2.0)))
    noise = jax.random.normal(key_noise, (TOKENS, D), jnp.float32)
    values = row_scales * noise * col_scales
    return jnp.clip(values, -12.0, 12.0).astype(jnp.bfloat16)


def draw_w_qkv(key, part):
    key_base = jax.random.fold_in(key, 23)
    base = jax.random.normal(key_base, (D, QKV_COLS), jnp.float32) / math.sqrt(D)
    return jnp.clip(base, -1.5, 1.5).astype(jnp.bfloat16)


def with_spikes(values, own_key, source, target, parts, factor):
    def block_of(axis_at):
        return (jnp.arange(values.shape[axis_at]) // (values.shape[axis_at] // parts)).reshape((-1,) + (1,) * (values.ndim - 1 - axis_at))

    one_side = jax.random.permutation(own_key, parts)[block_of(target)]
    other_side = (block_of(target) + parts // 2) % parts
    return jnp.where((block_of(source) == one_side) | (block_of(source) == other_side), factor * values, values)


def levels(key, extent, pieces, least, high):
    loudness = 1.0
    for dim, parts in pieces:
        steps = jax.random.uniform(jax.random.fold_in(jax.random.fold_in(key, 6), dim), (parts,), jnp.float32, least / len(pieces), high / len(pieces))
        loudness = loudness * jnp.repeat(jnp.exp(steps), extent[dim] // parts).reshape((-1,) + (1,) * (len(extent) - 1 - dim))
    return loudness


def profile(count, total, bound, slope):
    weights = [(1 << 20) // math.isqrt(grade ** slope) + 1 for grade in range(2, count + 1)]
    surplus, counts = total - bound - (count - 1), [1] * (count - 1)
    while surplus > 0:
        candidates = [i for i in range(count - 1) if counts[i] < bound]
        mass, budget = sum([weights[i] for i in candidates]), surplus
        for i in candidates:
            addition = min(bound - counts[i], max(1, budget * weights[i] // mass), surplus)
            counts[i] = counts[i] + addition
            surplus = surplus - addition
    return np.array([bound] + counts)


def ragged(own_key, number_of, total, most, lean):
    if number_of == 2:
        one = jax.random.randint(own_key, (), max(1, total - most), min(most, total - 1) + 1)
        return jnp.stack([one, total - one])
    lengths = jnp.asarray(profile(number_of, total, most, lean), jnp.int32)
    couples = (number_of - 1) // 2
    donor, taker = lengths[1:1 + 2 * couples:2], lengths[2:2 + 2 * couples:2]
    room = jnp.minimum(donor - 1, most - taker)
    passed = jax.random.randint(jax.random.fold_in(own_key, 1), (couples,), 0, 1 << 20) % (room + 1)
    lengths = lengths.at[1:1 + 2 * couples:2].set(donor - passed).at[2:2 + 2 * couples:2].set(taker + passed)
    return lengths[jax.random.permutation(jax.random.fold_in(own_key, 2), number_of)]


def bell_draw(stream_key, extent, spread, limit, pieces=(), held_as=jnp.bfloat16):
    array = spread * jax.random.normal(stream_key, extent, jnp.float32)
    if pieces:
        array = array * levels(stream_key, extent, pieces, -0.22, 0.18)
    return jnp.clip(array, -limit, limit).astype(held_as)


def heavy_noise(key, shape, spread, bound, shards, heavy, kind=jnp.bfloat16):
    drawn = spread * jax.random.normal(key, shape, jnp.float32)
    if shards:
        drawn = drawn * levels(key, shape, shards, -0.22, 0.18)
    return jnp.clip(with_spikes(drawn, jax.random.fold_in(key, 3), *heavy), -bound, bound).astype(kind)


def setup_inputs(seed: int = 0) -> dict:
    streams_of = jax.random.split(jax.random.key(seed), 11)
    hidden_in = draw_hidden_in(jax.random.fold_in(streams_of[10], 71), 0)
    cotangent = heavy_noise(streams_of[1], (TOKENS, D), 1.0, 6.0, ((0, 32),), (0, 1, 32, 2.75))
    segment_ids = jax.vmap(lambda own: jnp.searchsorted(jnp.cumsum(ragged(own, DOCS, LEN, LEN // 2, 2)), jnp.arange(LEN), side="right"))(jax.random.split(streams_of[2], N_FSDP)).reshape((N_FSDP, LEN)).astype(jnp.int32)
    w_qkv = draw_w_qkv(jax.random.fold_in(streams_of[10], 71), 0)
    w_out = bell_draw(streams_of[4], (H * HEAD_DIM, D), (H * HEAD_DIM // 16) ** -0.5, 0.625, ((0, 8), (1, 4)))
    w_gate = bell_draw(streams_of[5], (D, FF), D ** -0.5, 0.15625, ((0, 8), (1, 4)))
    w_up = bell_draw(streams_of[6], (D, FF), D ** -0.5, 0.15625, ((0, 8), (1, 4)))
    w_down = bell_draw(streams_of[7], (FF, D), FF ** -0.5, 0.09375, ((0, 8), (1, 4)))
    gain_attn = jnp.clip(1.0 + 0.18 * jax.random.normal(streams_of[8], (D,), jnp.float32), 0.099609375, 1.8984375).astype(jnp.bfloat16)
    gain_mlp = jnp.clip(1.0 + 0.18 * jax.random.normal(streams_of[9], (D,), jnp.float32), 0.099609375, 1.8984375).astype(jnp.bfloat16)
    return {"hidden_in": hidden_in, "cotangent": cotangent, "segment_ids": segment_ids, "w_qkv": w_qkv, "w_out": w_out, "w_gate": w_gate, "w_up": w_up, "w_down": w_down, "gain_attn": gain_attn, "gain_mlp": gain_mlp}


EPSILON = 1e-05
ROPE_BASE = 100000.0
NEGATIVE = -1e+30

def doc_positions(doc_ids):
    length = doc_ids.shape[0]
    tok_index = jnp.arange(length, dtype=jnp.int32)
    boundary = jnp.concatenate([jnp.ones((1,), dtype=jnp.bool_), doc_ids[1:] != doc_ids[:-1]])
    doc_start = lax.cummax(jnp.where(boundary, tok_index, jnp.zeros_like(tok_index)), axis=0)
    return tok_index - doc_start

def rope_tables(positions):
    half_dim = HEAD_DIM // 2
    freq_steps = jnp.arange(half_dim, dtype=jnp.float32)
    inverse = jnp.exp(freq_steps * (-2.0 * math.log(ROPE_BASE) / HEAD_DIM))
    angles = positions.astype(jnp.float32)[:, None] * inverse[None, :]
    return (jnp.cos(angles), jnp.sin(angles))

def rotate(block, cosine_table, sine_table):
    half_dim = block.shape[-1] // 2
    lower_part = block[..., :half_dim]
    upper_part = block[..., half_dim:]
    return jnp.concatenate([lower_part * cosine_table - upper_part * sine_table, upper_part * cosine_table + lower_part * sine_table], axis=-1)

def rotate_back(grad_in, cosine_table, sine_table):
    half_dim = grad_in.shape[-1] // 2
    lower_part = grad_in[..., :half_dim]
    upper_part = grad_in[..., half_dim:]
    return jnp.concatenate([lower_part * cosine_table + upper_part * sine_table, upper_part * cosine_table - lower_part * sine_table], axis=-1)

def inv_rms(values):
    return lax.rsqrt(lax.optimization_barrier(jnp.mean(values * values, axis=-1, keepdims=True)) + EPSILON)

def norm_back(grad_in, values, row_scale, gain_vec):
    weighted = grad_in * gain_vec
    d_values = row_scale * (weighted - values * (row_scale * row_scale) * lax.optimization_barrier(jnp.mean(weighted * values, axis=-1, keepdims=True)))
    d_gain = lax.optimization_barrier(jnp.sum(grad_in * values * row_scale, axis=0))
    return (d_values, d_gain)

def allowed_pairs(doc_ids):
    length = doc_ids.shape[0]
    tok_index = jnp.arange(length, dtype=jnp.int32)
    return (doc_ids[:, None] == doc_ids[None, :]) & (tok_index[None, :] <= tok_index[:, None])

def attend_full(group_item, doc_ids, score_scale):
    queries = group_item[:, :2].astype(jnp.float32)
    key_rows = group_item[:, 2].astype(jnp.float32)
    value_rows = group_item[:, 3].astype(jnp.float32)
    allowed = allowed_pairs(doc_ids)
    scores = jnp.einsum('qhd,kd->hqk', queries, key_rows) * score_scale
    scores = jnp.where(allowed[None], scores, NEGATIVE)
    row_max = lax.optimization_barrier(jnp.max(scores, axis=-1, keepdims=True))
    log_total = row_max + jnp.log(lax.optimization_barrier(jnp.sum(jnp.exp(scores - row_max), axis=-1, keepdims=True)))
    weights = jnp.where(allowed[None], jnp.exp(scores - log_total), 0.0).astype(jnp.bfloat16)
    weights = lax.optimization_barrier(weights)
    mixed_out = jnp.einsum('hqk,kd->qhd', weights.astype(jnp.float32), value_rows).astype(jnp.bfloat16)
    return (mixed_out, log_total[..., 0])

def attend_full_back(group_item, mixed_out, log_total, d_mixed, doc_ids, score_scale):
    queries = group_item[:, :2].astype(jnp.float32)
    key_rows = group_item[:, 2].astype(jnp.float32)
    value_rows = group_item[:, 3].astype(jnp.float32)
    allowed = allowed_pairs(doc_ids)
    scores = jnp.einsum('qhd,kd->hqk', queries, key_rows) * score_scale
    scores = jnp.where(allowed[None], scores, NEGATIVE)
    probabilities = jnp.where(allowed[None], jnp.exp(scores - log_total[:, :, None]), 0.0)
    weights = lax.optimization_barrier(probabilities.astype(jnp.bfloat16)).astype(jnp.float32)
    d_out_wide = d_mixed.astype(jnp.float32)
    d_values = jnp.einsum('hqk,qhd->kd', weights, d_out_wide)
    d_probs = jnp.einsum('qhd,kd->hqk', d_out_wide, value_rows)
    row_delta = lax.optimization_barrier(jnp.sum(d_out_wide * mixed_out.astype(jnp.float32), axis=-1))
    d_scores = (probabilities * (d_probs - jnp.transpose(row_delta)[:, :, None])).astype(jnp.bfloat16)
    d_scores = lax.optimization_barrier(d_scores).astype(jnp.float32)
    d_queries = jnp.einsum('hqk,kd->qhd', d_scores, key_rows) * score_scale
    d_keys = jnp.einsum('hqk,qhd->kd', d_scores, queries) * score_scale
    return (d_queries, d_keys, d_values)

def one_sequence(tok_in, cot_in, doc_ids, w_qkv, w_out, w_gate, w_up, w_down, gain_attn, gain_mlp):
    length = tok_in.shape[0]
    groups = w_qkv.shape[1] // (4 * HEAD_DIM)
    score_scale = 1.0 / math.sqrt(HEAD_DIM)
    cosine_table, sine_table = rope_tables(doc_positions(doc_ids))
    gain_one = gain_attn.astype(jnp.float32)
    gain_two = gain_mlp.astype(jnp.float32)
    values_in = tok_in.astype(jnp.float32)
    scale_one = inv_rms(values_in)
    normed_one = (values_in * scale_one * gain_one).astype(jnp.bfloat16)
    projected = jnp.dot(normed_one, w_qkv, preferred_element_type=jnp.float32).reshape(length, groups, 4, HEAD_DIM)
    packed = jnp.concatenate([rotate(projected[:, :, :3], cosine_table[:, None, None, :], sine_table[:, None, None, :]), projected[:, :, 3:]], axis=2).astype(jnp.bfloat16)
    by_group = jnp.moveaxis(packed, 1, 0)
    mixed_all, totals_all = lax.map(lambda group_item: attend_full(group_item, doc_ids, score_scale), by_group)
    attn_rows = jnp.moveaxis(mixed_all, 0, 1).reshape(length, groups * 2 * HEAD_DIM)
    middle = values_in + jnp.dot(attn_rows, w_out, preferred_element_type=jnp.float32)
    scale_two = inv_rms(middle)
    normed_two = (middle * scale_two * gain_two).astype(jnp.bfloat16)
    gate_pre = jnp.dot(normed_two, w_gate, preferred_element_type=jnp.float32)
    up_proj = jnp.dot(normed_two, w_up, preferred_element_type=jnp.float32)
    sigmoid_gate = jax.nn.sigmoid(gate_pre)
    activated = gate_pre * sigmoid_gate
    hidden_act = (activated * up_proj).astype(jnp.bfloat16)
    output = middle + jnp.dot(hidden_act, w_down, preferred_element_type=jnp.float32)
    cot_wide = cot_in.astype(jnp.float32)
    grad_down = jnp.dot(hidden_act.T, cot_in, preferred_element_type=jnp.float32)
    d_hidden = jnp.dot(cot_in, w_down.T, preferred_element_type=jnp.float32)
    d_gate = (d_hidden * up_proj * sigmoid_gate * (1.0 + gate_pre * (1.0 - sigmoid_gate))).astype(jnp.bfloat16)
    d_up = (d_hidden * activated).astype(jnp.bfloat16)
    grad_gate = jnp.dot(normed_two.T, d_gate, preferred_element_type=jnp.float32)
    grad_up = jnp.dot(normed_two.T, d_up, preferred_element_type=jnp.float32)
    d_normed_two = jnp.dot(d_gate, w_gate.T, preferred_element_type=jnp.float32) + jnp.dot(d_up, w_up.T, preferred_element_type=jnp.float32)
    d_middle, grad_gain_two = norm_back(d_normed_two, middle, scale_two, gain_two)
    d_middle = cot_wide + d_middle
    d_mid_low = d_middle.astype(jnp.bfloat16)
    grad_out = jnp.dot(attn_rows.T, d_mid_low, preferred_element_type=jnp.float32)
    d_attn = jnp.dot(d_mid_low, w_out.T, preferred_element_type=jnp.float32).astype(jnp.bfloat16)
    d_attn = jnp.moveaxis(d_attn.reshape(length, groups, 2, HEAD_DIM), 1, 0)

    def backward_group(operands):
        group_item, mixed_out, log_total, d_mixed = operands
        return attend_full_back(group_item, mixed_out, log_total, d_mixed, doc_ids, score_scale)
    d_queries, d_keys, d_values = lax.map(backward_group, (by_group, mixed_all, totals_all, d_attn))
    rotated_grad = rotate_back(jnp.concatenate([d_queries, d_keys[:, :, None]], axis=2), cosine_table[:, None, :], sine_table[:, None, :])
    d_packed = jnp.concatenate([rotated_grad, d_values[:, :, None]], axis=2).astype(jnp.bfloat16)
    d_packed = jnp.moveaxis(d_packed, 0, 1).reshape(length, groups * 4 * HEAD_DIM)
    grad_qkv = jnp.dot(normed_one.T, d_packed, preferred_element_type=jnp.float32)
    d_normed_one = jnp.dot(d_packed, w_qkv.T, preferred_element_type=jnp.float32)
    d_tokens, grad_gain_one = norm_back(d_normed_one, values_in, scale_one, gain_one)
    d_tokens = d_middle + d_tokens
    return (output, d_tokens, (grad_qkv, grad_out, grad_gate, grad_up, grad_down, grad_gain_one, grad_gain_two))

def reference(hidden_in, cotangent, segment_ids, w_qkv, w_out, w_gate, w_up, w_down, gain_attn, gain_mlp):
    seq_count = segment_ids.shape[0]
    length = segment_ids.shape[1]
    model_width = hidden_in.shape[1]
    tok_seqs = hidden_in.reshape(seq_count, length, model_width)
    cot_seqs = cotangent.reshape(seq_count, length, model_width)
    initial = (jnp.zeros(w_qkv.shape, jnp.float32), jnp.zeros(w_out.shape, jnp.float32), jnp.zeros(w_gate.shape, jnp.float32), jnp.zeros(w_up.shape, jnp.float32), jnp.zeros(w_down.shape, jnp.float32), jnp.zeros(gain_attn.shape, jnp.float32), jnp.zeros(gain_mlp.shape, jnp.float32))

    def step_one(running, inputs):
        tok_in, cot_in, doc_ids = inputs
        output, d_tokens, grads = one_sequence(tok_in, cot_in, doc_ids, w_qkv, w_out, w_gate, w_up, w_down, gain_attn, gain_mlp)
        return (tuple((total + piece for total, piece in zip(running, grads))), (output, d_tokens))
    grads, (outputs, d_inputs) = lax.scan(step_one, initial, (tok_seqs, cot_seqs, segment_ids))
    return (outputs.reshape(-1, model_width), d_inputs.reshape(-1, model_width), grads[0], grads[1], grads[2], grads[3], grads[4], grads[5], grads[6])
```

```python
import math

import jax
import jax.numpy as jnp
from jax import lax
from jax.sharding import PartitionSpec as P

HEAD_DIM = 96
EPSILON = 1e-05
ROPE_BASE = 100000.0
NEGATIVE = -1e30


def rope_tables(ids):
    length = ids.shape[0]
    first = jnp.sum((ids[None, :] < ids[:, None]).astype(jnp.int32), axis=1)
    positions = jnp.arange(length, dtype=jnp.int32) - first
    half_dim = HEAD_DIM // 2
    freq_steps = jnp.arange(half_dim, dtype=jnp.float32)
    inverse = jnp.exp(freq_steps * (-2.0 * math.log(ROPE_BASE) / HEAD_DIM))
    angles = positions.astype(jnp.float32)[:, None] * inverse[None, :]
    return (jnp.cos(angles), jnp.sin(angles))


def rotate(block, cosine_table, sine_table):
    half_dim = block.shape[-1] // 2
    lower, upper = block[..., :half_dim], block[..., half_dim:]
    return jnp.concatenate(
        [lower * cosine_table - upper * sine_table, upper * cosine_table + lower * sine_table],
        axis=-1,
    )


def inv_rms(values):
    return lax.rsqrt(jnp.mean(values * values, axis=-1, keepdims=True) + EPSILON)


def norm_back(grad_in, values, row_scale, gain_vec):
    weighted = grad_in * gain_vec
    d_values = row_scale * (
        weighted
        - values * (row_scale * row_scale) * jnp.mean(weighted * values, axis=-1, keepdims=True)
    )
    return (d_values, jnp.sum(grad_in * values * row_scale, axis=0))


def contract_rows(left, right):
    return lax.dot_general(
        left, right, (((0,), (0,)), ((), ())), preferred_element_type=jnp.float32
    )


def times(left, right):
    return jnp.dot(left, right, preferred_element_type=jnp.float32)


def times_trans(left, right):
    return lax.dot_general(
        left, right, (((1,), (1,)), ((), ())), preferred_element_type=jnp.float32
    )


def attend_forward(group, allowed, score_scale):
    queries, keys, vals = group[:, :2], group[:, 2], group[:, 3]
    scores = jnp.einsum("qhd,kd->hqk", queries, keys, preferred_element_type=jnp.float32)
    scores = jnp.where(allowed[None], scores * score_scale, NEGATIVE)
    row_max = jnp.max(scores, axis=-1, keepdims=True)
    lse = row_max + jnp.log(jnp.sum(jnp.exp(scores - row_max), axis=-1, keepdims=True))
    weights = jnp.where(allowed[None], jnp.exp(scores - lse), 0.0).astype(jnp.bfloat16)
    mixed = jnp.einsum("hqk,kd->qhd", weights, vals, preferred_element_type=jnp.float32)
    return mixed.astype(jnp.bfloat16), lse


def attend_backward(group, mixed, lse, d_mixed, allowed, score_scale):
    queries, keys, vals = group[:, :2], group[:, 2], group[:, 3]
    delta = jnp.sum(d_mixed.astype(jnp.float32) * mixed.astype(jnp.float32), axis=-1)
    scores = jnp.einsum("qhd,kd->hqk", queries, keys, preferred_element_type=jnp.float32)
    probs = jnp.where(allowed[None], jnp.exp(scores * score_scale - lse), 0.0)
    d_vals = jnp.einsum(
        "hqk,qhd->kd", probs.astype(jnp.bfloat16), d_mixed, preferred_element_type=jnp.float32
    )
    d_probs = jnp.einsum("qhd,kd->hqk", d_mixed, vals, preferred_element_type=jnp.float32)
    d_scores = (probs * (d_probs - jnp.transpose(delta)[:, :, None])).astype(jnp.bfloat16)
    d_q = jnp.einsum("hqk,kd->qhd", d_scores, keys, preferred_element_type=jnp.float32)
    d_k = jnp.einsum("hqk,qhd->kd", d_scores, queries, preferred_element_type=jnp.float32)
    return d_q * score_scale, d_k * score_scale, d_vals


def body(
    hidden_in, cotangent, segment_ids, w_qkv, w_out, w_gate, w_up, w_down, gain_attn, gain_mlp
):
    rows = hidden_in.shape[0]
    fsdp = lax.axis_size("fsdp")
    seq = lax.axis_size("seq")
    ratio = fsdp // seq
    scale = 1.0 / math.sqrt(HEAD_DIM)
    length = rows * seq
    moves = [
        (f * seq + s, ((f % ratio) * seq + s) * seq + f // ratio)
        for f in range(fsdp)
        for s in range(seq)
    ]
    back = [(there, here) for here, there in moves]

    def gather_rows(shard):
        height, width = shard.shape
        moved = lax.ppermute(shard, ("fsdp", "seq"), moves)
        blocks = lax.all_gather(moved, "fsdp", axis=0, tiled=False)
        blocks = blocks.reshape(ratio, seq, height, width)
        return jnp.transpose(blocks, (0, 2, 1, 3)).reshape(ratio * height, seq * width)

    def scatter_rows(grad):
        height, width = grad.shape[0] // ratio, grad.shape[1] // seq
        blocks = grad.astype(jnp.bfloat16).reshape(ratio, height, seq, width)
        blocks = jnp.transpose(blocks, (0, 2, 1, 3)).reshape(fsdp, height, width)
        own = lax.psum_scatter(blocks, "fsdp", scatter_dimension=0, tiled=False)
        return lax.ppermute(own, ("fsdp", "seq"), back).astype(jnp.float32)

    def gather_cols(shard):
        return lax.all_gather(shard, "fsdp", axis=0, tiled=True)

    def scatter_cols(grad):
        return lax.psum_scatter(
            grad.astype(jnp.bfloat16), "fsdp", scatter_dimension=0, tiled=True
        ).astype(jnp.float32)

    def gather_tokens(block):
        return lax.all_gather(block, "seq", axis=0, tiled=True)

    def scatter_tokens(partial):
        return lax.psum_scatter(
            partial.astype(jnp.bfloat16), "seq", scatter_dimension=0, tiled=True
        ).astype(jnp.float32)

    gains = lax.all_gather(
        jnp.stack([gain_attn, gain_mlp]), ("fsdp", "seq"), axis=1, tiled=True
    ).astype(jnp.float32)
    gain_one, gain_two = gains[0], gains[1]
    ids = lax.all_gather(segment_ids, "seq", axis=1, tiled=True)[0]
    hidden_all = gather_tokens(hidden_in)
    cot_all = gather_tokens(cotangent)
    cols_qkv = gather_cols(w_qkv)
    rows_out = gather_rows(w_out)
    cols_gate = gather_cols(w_gate)
    cols_up = gather_cols(w_up)
    rows_down = gather_rows(w_down)

    tok = jnp.arange(length, dtype=jnp.int32)
    allowed = (ids[:, None] == ids[None, :]) & (tok[None, :] <= tok[:, None])
    cosine, sine = rope_tables(ids)

    values_all = hidden_all.astype(jnp.float32)
    normed_one = (values_all * inv_rms(values_all) * gain_one).astype(jnp.bfloat16)
    groups = cols_qkv.shape[1] // (4 * HEAD_DIM)
    projected = times(normed_one, cols_qkv).reshape(length, groups, 4, HEAD_DIM)
    packed = jnp.concatenate(
        [
            rotate(projected[:, :, :3], cosine[:, None, None, :], sine[:, None, None, :]),
            projected[:, :, 3:],
        ],
        axis=2,
    ).astype(jnp.bfloat16)
    forward = [attend_forward(packed[:, g], allowed, scale) for g in range(groups)]
    attn = jnp.stack([mixed for mixed, _ in forward], axis=1).reshape(length, -1)

    values_in = hidden_in.astype(jnp.float32)
    middle = values_in + scatter_tokens(times(attn, rows_out))
    scale_two = inv_rms(middle)
    normed_two = gather_tokens((middle * scale_two * gain_two).astype(jnp.bfloat16))
    gate = times(normed_two, cols_gate)
    up = times(normed_two, cols_up)
    sig = jax.nn.sigmoid(gate)
    activated = gate * sig
    hid = (activated * up).astype(jnp.bfloat16)
    output = middle + scatter_tokens(times(hid, rows_down))
    g_down = scatter_rows(contract_rows(hid, cot_all))
    d_hid = times_trans(cot_all, rows_down)
    d_gate = (d_hid * up * sig * (1.0 + gate * (1.0 - sig))).astype(jnp.bfloat16)
    d_up = (d_hid * activated).astype(jnp.bfloat16)
    g_gate = scatter_cols(contract_rows(normed_two, d_gate))
    g_up = scatter_cols(contract_rows(normed_two, d_up))
    d_normed_two = scatter_tokens(times_trans(d_gate, cols_gate) + times_trans(d_up, cols_up))
    d_middle, part_two = norm_back(d_normed_two, middle, scale_two, gain_two)
    d_middle = cotangent.astype(jnp.float32) + d_middle
    d_low = gather_tokens(d_middle.astype(jnp.bfloat16))
    g_out = scatter_rows(contract_rows(attn, d_low))
    d_attn = times_trans(d_low, rows_out).astype(jnp.bfloat16)
    d_attn = d_attn.reshape(length, groups, 2, HEAD_DIM)
    pieces = []
    for g in range(groups):
        d_q, d_k, d_v = attend_backward(
            packed[:, g], forward[g][0], forward[g][1], d_attn[:, g], allowed, scale
        )
        turned = rotate(
            jnp.concatenate([d_q, d_k[:, None]], axis=1), cosine[:, None, :], -sine[:, None, :]
        )
        pieces.append(jnp.concatenate([turned, d_v[:, None]], axis=1))
    d_packed = jnp.stack(pieces, axis=1).reshape(length, -1).astype(jnp.bfloat16)
    g_qkv = scatter_cols(contract_rows(normed_one, d_packed))
    d_normed_one = scatter_tokens(times_trans(d_packed, cols_qkv))
    d_tokens, part_one = norm_back(d_normed_one, values_in, inv_rms(values_in), gain_one)
    d_tokens = d_middle + d_tokens
    g_gains = lax.psum_scatter(
        jnp.stack([part_one, part_two]), ("fsdp", "seq"), scatter_dimension=1, tiled=True
    )
    return (output, d_tokens, g_qkv, g_out, g_gate, g_up, g_down, g_gains[0], g_gains[1])


def solution(mesh):
    both = P(("fsdp", "seq"), None)
    split = P("fsdp", "seq")
    gain = P(("fsdp", "seq"))
    in_specs = (both, both, split, split, split, split, split, split, gain, gain)
    out_specs = (both, both, split, split, split, split, split, gain, gain)
    return jax.shard_map(body, mesh=mesh, in_specs=in_specs, out_specs=out_specs, check_vma=False)
```

```python
import functools
import math

import jax
import jax.numpy as jnp
from jax import lax
from jax.experimental import pallas as pl
from jax.experimental.pallas import tpu as pltpu
from jax.sharding import PartitionSpec as P

HEAD_DIM = 96
EPSILON = 1e-05
ROPE_BASE = 100000.0
NEGATIVE = -1e30
SCALE = 1.0 / math.sqrt(HEAD_DIM)
MESH = pl.DeviceIdType.MESH
BLOCK = 256
F32 = jnp.float32
BF16 = jnp.bfloat16
ANY = pl.BlockSpec(memory_space=pl.ANY)
VMEM = pl.BlockSpec(memory_space=pltpu.VMEM)


def dot(left, right):
    return jnp.dot(left, right, preferred_element_type=F32)


def dot_nt(left, right):
    return lax.dot_general(left, right, (((1,), (1,)), ((), ())), preferred_element_type=F32)


def dot_tn(left, right):
    return lax.dot_general(left, right, (((0,), (0,)), ((), ())), preferred_element_type=F32)


def shape(dims, kind):
    return jax.ShapeDtypeStruct(dims, kind)


def params(collective=None):
    return pltpu.CompilerParams(
        collective_id=collective,
        has_side_effects=collective is not None,
        vmem_limit_bytes=60 << 20,
    )


def cost(flops, moved):
    return pl.CostEstimate(flops=flops, bytes_accessed=moved, transcendentals=0)


def others(size):
    me = lax.axis_index("seq")
    if size == 4:
        low, high = lax.rem(me, 2), me // 2
        return [high * 2 + 1 - low, (1 - high) * 2 + low, (1 - high) * 2 + 1 - low]
    return [lax.rem(me + step, size) for step in range(1, size)]


def meet(size, axis="seq", ends=True):
    barrier = pltpu.get_barrier_semaphore()
    for peer in others(size):
        pl.semaphore_signal(barrier, inc=1, device_id={"seq": peer}, device_id_type=MESH)
    if ends:
        pl.semaphore_wait(barrier, size - 1)


def push(src, dst, sems, index, peer, axis="seq"):
    return pltpu.make_async_remote_copy(
        src_ref=src,
        dst_ref=dst,
        send_sem=sems[0].at[index],
        recv_sem=sems[1].at[index],
        device_id={axis: peer},
        device_id_type=MESH,
    )


def n_copies(size):
    return 6 if size == 4 else size - 1


class Gather:
    def __init__(self, size, own, whole, sems):
        self.size, self.own, self.whole, self.sems = size, own, whole, sems
        self.me = lax.axis_index("seq")
        self.peers = others(size)
        half = own.shape[0] // 2
        self.parts = [pl.ds(0, half), pl.ds(half, half)]

    def copy(self, index):
        me, own, whole, sems = self.me, self.own, self.whole, self.sems
        if self.size != 4:
            return push(own, whole.at[me], sems, index, self.peers[index])
        side, over, _ = self.peers
        one, two = self.parts
        src, dst, peer = [
            (own.at[one], whole.at[me, one], side),
            (own.at[two], whole.at[me, two], side),
            (own.at[two], whole.at[me, two], over),
            (own.at[one], whole.at[me, one], over),
            (whole.at[side, one], whole.at[side, one], over),
            (whole.at[over, two], whole.at[over, two], side),
        ][index]
        return push(src, dst, sems, index, peer)

    def start(self):
        for index in (0, 2, 1, 3) if self.size == 4 else range(self.size - 1):
            self.copy(index).start()

    def forward(self):
        if self.size == 4:
            for index in (0, 2):
                self.copy(index).wait_recv()
            self.copy(4).start()
            self.copy(5).start()

    def finish(self):
        for index in range(n_copies(self.size)):
            if self.size != 4 or index not in (0, 2):
                self.copy(index).wait_recv()
        for index in range(n_copies(self.size)):
            self.copy(index).wait_send()


def scatter_scratch(size, rows, width):
    if size == 4:
        held = [
            pltpu.VMEM((3, rows, width), BF16),
            pltpu.VMEM((2, rows // 2, width), BF16),
            pltpu.VMEM((2, rows, width), BF16),
        ]
    else:
        held = [
            pltpu.VMEM((size - 1, rows, width), BF16),
            pltpu.VMEM((1, 16, 128), BF16),
            pltpu.VMEM((size - 1, rows, width), BF16),
        ]
    return held + [pltpu.SemaphoreType.DMA((n_copies(size),))] * 2


class Scatter:
    def __init__(self, size, held, stage, got, sems):
        self.size, self.held, self.stage, self.got, self.sems = size, held, stage, got, sems
        self.peers = others(size)
        half = held.shape[1] // 2
        self.parts = [pl.ds(0, half), pl.ds(half, half)]

    def copy(self, index):
        held, stage, got, sems = self.held, self.stage, self.got, self.sems
        if self.size != 4:
            return push(held.at[index], got.at[index], sems, index, self.peers[index])
        side, over, _ = self.peers
        one, two = self.parts
        src, dst, peer = [
            (held.at[2, one], stage.at[0], side),
            (held.at[2, two], stage.at[1], over),
            (held.at[0, one], got.at[0, one], side),
            (held.at[1, two], got.at[1, two], over),
            (held.at[0, two], got.at[0, two], side),
            (held.at[1, one], got.at[1, one], over),
        ][index]
        return push(src, dst, sems, index, peer)

    def send(self, make):
        if self.size != 4:
            for k, peer in enumerate(self.peers):
                make(peer, self.held.at[k])
                self.copy(k).start()
            return
        make(self.peers[2], self.held.at[2])
        self.copy(0).start()
        self.copy(1).start()
        make(self.peers[0], self.held.at[0])
        self.copy(2).start()
        make(self.peers[1], self.held.at[1])
        self.copy(3).start()

    def forward(self):
        if self.size == 4:
            one, two = self.parts
            held, stage = self.held, self.stage
            self.copy(1).wait_recv()
            held[0, two] = (held[0, two].astype(F32) + stage[1].astype(F32)).astype(BF16)
            self.copy(4).start()
            self.copy(0).wait_recv()
            held[1, one] = (held[1, one].astype(F32) + stage[0].astype(F32)).astype(BF16)
            self.copy(5).start()

    def finish(self):
        for index in range(n_copies(self.size)):
            if self.size != 4 or index > 1:
                self.copy(index).wait_recv()
        for index in range(n_copies(self.size)):
            self.copy(index).wait_send()

    def terms(self, rows):
        total = self.got[0, rows].astype(F32)
        for k in range(1, self.got.shape[0]):
            total = total + self.got[k, rows].astype(F32)
        return total


def each(count, step, task):
    def run(index, carry):
        task(pl.multiple_of(index * step, step))
        return carry

    lax.fori_loop(0, count // step, run, 0)


def tile_of(width, most):
    tile = most
    while width % tile:
        tile //= 2
    return tile


def enter_kernel(seq, fsdp, hidden, ids, gains, hidden_all, ids_all, gains_all, *sems):
    block_sems, id_sems, gain_sems, wide_sems, local = (
        sems[0:2],
        sems[2:4],
        sems[4:6],
        sems[6:8],
        sems[8],
    )
    me, row = lax.axis_index("seq"), lax.axis_index("fsdp")
    barrier = pltpu.get_barrier_semaphore()
    for peer in others(seq):
        pl.semaphore_signal(barrier, inc=1, device_id={"seq": peer}, device_id_type=MESH)
    for step in range(1, fsdp):
        pl.semaphore_signal(
            barrier,
            inc=1,
            device_id={"fsdp": lax.rem(row + step, fsdp)},
            device_id_type=MESH,
        )
    pl.semaphore_wait(barrier, seq - 1 + fsdp - 1)
    whole = Gather(seq, hidden, hidden_all, block_sems)
    small = [push(ids, ids_all.at[me], id_sems, k, peer) for k, peer in enumerate(others(seq))]
    small += [
        push(gains, gains_all.at[row, me], gain_sems, k, peer)
        for k, peer in enumerate(others(seq))
    ]
    for copy in small:
        copy.start()
    whole.start()
    kept = [
        pltpu.make_async_copy(hidden, hidden_all.at[me], local.at[0]),
        pltpu.make_async_copy(ids, ids_all.at[me], local.at[1]),
        pltpu.make_async_copy(gains, gains_all.at[row, me], local.at[2]),
    ]
    for copy in kept:
        copy.start()
    for copy in small:
        copy.wait()
    for copy in kept:
        copy.wait()
    wide = [
        push(
            gains_all.at[row],
            gains_all.at[row],
            wide_sems,
            step - 1,
            lax.rem(row + step, fsdp),
            axis="fsdp",
        )
        for step in range(1, fsdp)
    ]
    for copy in wide:
        copy.start()
    whole.forward()
    for copy in wide:
        copy.wait()
    whole.finish()


def enter(seq, fsdp, hidden, ids, gains):
    rows, width = hidden.shape
    dma = pltpu.SemaphoreType.DMA
    return pl.pallas_call(
        functools.partial(enter_kernel, seq, fsdp),
        out_shape=(
            shape((seq, rows, width), BF16),
            shape((seq, 1, rows), jnp.int32),
            shape((fsdp, seq) + gains.shape, BF16),
        ),
        in_specs=[ANY] * 3,
        out_specs=(ANY,) * 3,
        scratch_shapes=[dma((n_copies(seq),))] * 2
        + [dma((seq - 1,))] * 4
        + [dma((fsdp - 1,))] * 2
        + [dma((3,))],
        compiler_params=params(0),
        name="enter",
    )(hidden, ids, gains)


def swap_halves(block):
    half = HEAD_DIM // 2
    return jnp.concatenate([block[:, half:], block[:, :half]], axis=1)


def mask_bias(ids_col, ids_row, start, low, high):
    span = high - low
    query = start + lax.broadcasted_iota(jnp.int32, (BLOCK, span), 0)
    key = low + lax.broadcasted_iota(jnp.int32, (BLOCK, span), 1)
    same = ids_col[pl.ds(start, BLOCK), :] == ids_row[:, low:high]
    bias = jnp.where(jnp.logical_and(same, key <= query), 0.0, NEGATIVE)
    return jnp.concatenate([bias, bias], axis=0)


def key_range(start, length):
    return max(0, start - length // 2), start + BLOCK


def attend_kernel(
    seq, hidden, gain, ids_col, ids_row, cosine, sine, w_qkv, cot, normed, packed, attn, lse,
    cot_all, *sems
):
    length = hidden.shape[0]
    groups = w_qkv.shape[1] // (4 * HEAD_DIM)
    meet(seq)
    whole = Gather(seq, cot, cot_all, sems[:2])
    whole.start()
    own = pltpu.make_async_copy(cot, cot_all.at[lax.axis_index("seq")], sems[2].at[0])
    own.start()

    def norm(at):
        rows = pl.ds(at, BLOCK)
        values = hidden[rows, :].astype(F32)
        scale = lax.rsqrt(jnp.mean(values * values, axis=-1, keepdims=True) + EPSILON)
        normed[rows, :] = (values * scale * gain[...]).astype(BF16)

    each(length, BLOCK, norm)
    for group in range(groups):

        def project(at, group=group):
            rows = pl.ds(at, 512)
            low = group * 4 * HEAD_DIM
            proj = dot(normed[rows, :], w_qkv[:, low : low + 4 * HEAD_DIM])
            for slot in range(4):
                part = proj[:, slot * HEAD_DIM : (slot + 1) * HEAD_DIM]
                if slot < 3:
                    part = part * cosine[rows, :] + swap_halves(part) * sine[rows, :]
                packed[group * 4 + slot, rows, :] = part.astype(BF16)

        each(length, 512, project)
    whole.forward()
    for start in range(0, length, BLOCK):
        low, high = key_range(start, length)
        rows = pl.ds(start, BLOCK)
        keys = pl.ds(low, high - low)
        bias = mask_bias(ids_col, ids_row, start, low, high)
        mixed, logs = [], []
        for group in range(groups):
            queries = jnp.concatenate(
                [packed[group * 4, rows, :], packed[group * 4 + 1, rows, :]], axis=0
            )
            scores = dot_nt(queries, packed[group * 4 + 2, keys, :]) * SCALE + bias
            most = jnp.max(scores, axis=-1, keepdims=True)
            grown = jnp.exp(scores - most)
            total = jnp.sum(grown, axis=-1, keepdims=True)
            weights = (grown * (1.0 / total)).astype(BF16)
            out = dot(weights, packed[group * 4 + 3, keys, :])
            log_total = most + jnp.log(total)
            mixed += [out[:BLOCK], out[BLOCK:]]
            logs += [log_total[:BLOCK], log_total[BLOCK:]]
        attn[rows, :] = jnp.concatenate(mixed, axis=1).astype(BF16)
        lane = lax.broadcasted_iota(jnp.int32, (BLOCK, 128), 1)
        stats = jnp.zeros((BLOCK, 128), F32)
        for head, log_total in enumerate(logs):
            stats = jnp.where(lane == head, log_total, stats)
        lse[rows, :] = stats
    whole.finish()
    own.wait()


def attend(seq, hidden_all, gain, ids_col, ids_row, cosine, sine, w_qkv, cot):
    length, width = hidden_all.shape
    groups = w_qkv.shape[1] // (4 * HEAD_DIM)
    dma = pltpu.SemaphoreType.DMA
    return pl.pallas_call(
        functools.partial(attend_kernel, seq),
        out_shape=(
            shape((length, width), BF16),
            shape((groups * 4, length, HEAD_DIM), BF16),
            shape((length, groups * 2 * HEAD_DIM), BF16),
            shape((length, 128), F32),
            shape((seq,) + cot.shape, BF16),
        ),
        in_specs=[VMEM] * 7 + [ANY],
        out_specs=(VMEM,) * 4 + (ANY,),
        scratch_shapes=[dma((n_copies(seq),))] * 2 + [dma((1,))],
        compiler_params=params(1),
        cost_estimate=cost(2 * length * width * w_qkv.shape[1] * 4, 20 << 20),
        name="attend",
    )(hidden_all, gain, ids_col, ids_row, cosine, sine, w_qkv, cot)


def join_blocks(blocks, seq, whole):
    ratio = blocks.shape[0] // seq
    height, width = blocks.shape[1:]
    for down in range(ratio):
        for across in range(seq):
            whole[down * height : (down + 1) * height, across * width : (across + 1) * width] = (
                blocks[down * seq + across]
            )


def middle_kernel(
    seq, attn, blocks, hidden, gain, middle, normed_all, w_out, held, stage, got, *sems
):
    rows, width = hidden.shape
    me = lax.axis_index("seq")
    tile = tile_of(width, 512)
    meet(seq, ends=False)
    join_blocks(blocks, seq, w_out)
    pl.semaphore_wait(pltpu.get_barrier_semaphore(), seq - 1)
    sums = Scatter(seq, held, stage, got, sems[:2])

    def term(device, ref):
        block = pl.ds(pl.multiple_of(device * rows, rows), rows)

        def part(at):
            ref[:, pl.ds(at, tile)] = dot(attn[block, :], w_out[:, pl.ds(at, tile)]).astype(BF16)

        each(width, tile, part)

    sums.send(term)
    block = pl.ds(pl.multiple_of(me * rows, rows), rows)

    def own(at):
        cols = pl.ds(at, tile)
        middle[:, cols] = hidden[:, cols].astype(F32) + dot(attn[block, :], w_out[:, cols])

    each(width, tile, own)
    sums.forward()
    sums.finish()

    def norm(at):
        part = pl.ds(at, 128)
        values = middle[part, :] + sums.terms(part)
        middle[part, :] = values
        scale = lax.rsqrt(jnp.mean(values * values, axis=-1, keepdims=True) + EPSILON)
        normed_all[me, part, :] = (values * scale * gain[...]).astype(BF16)

    each(rows, 128, norm)
    whole = Gather(seq, normed_all.at[me], normed_all, sems[2:4])
    whole.start()
    whole.forward()
    whole.finish()


def to_middle(seq, attn, blocks, hidden, gain):
    rows, width = hidden.shape
    dma = pltpu.SemaphoreType.DMA
    return pl.pallas_call(
        functools.partial(middle_kernel, seq),
        out_shape=(
            shape((rows, width), F32),
            shape((seq, rows, width), BF16),
            shape((attn.shape[1], width), BF16),
        ),
        in_specs=[VMEM] * 4,
        out_specs=(VMEM,) * 3,
        scratch_shapes=scatter_scratch(seq, rows, width) + [dma((n_copies(seq),))] * 2,
        compiler_params=params(2),
        cost_estimate=cost(60 << 30, 10 << 20),
        name="middle",
    )(attn, blocks, hidden, gain)


def feed_kernel(seq, normed, cot, w_gate, w_up, blocks, hid, d_gate, d_up, g_down, g_both, w_down):
    length = normed.shape[0]
    height = w_down.shape[0]
    for across in range(seq):
        width = blocks.shape[-1]
        w_down[:, across * width : (across + 1) * width] = blocks[0, across]

    def part(at):
        rows = pl.ds(at, 512)
        gate = dot(normed[rows, :], w_gate[...])
        up = dot(normed[rows, :], w_up[...])
        d_hid = dot_nt(cot[rows, :], w_down[...])
        sig = 1.0 / (1.0 + jnp.exp(-gate))
        active = gate * sig
        hid[rows, :] = (active * up).astype(BF16)
        d_gate[rows, :] = (d_hid * up * sig * (1.0 + gate * (1.0 - sig))).astype(BF16)
        d_up[rows, :] = (d_hid * active).astype(BF16)

    each(length, 512, part)
    for across in range(seq):
        width = blocks.shape[-1]
        cols = slice(across * width, (across + 1) * width)
        g_down[0, across] = dot_tn(hid[...], cot[:, cols]).astype(BF16)

    def grads(at):
        rows = pl.ds(at, 512)
        g_both[rows, :height] = dot_tn(normed[:, rows], d_gate[...]).astype(BF16)
        g_both[rows, height:] = dot_tn(normed[:, rows], d_up[...]).astype(BF16)

    each(normed.shape[1], 512, grads)


def feed(seq, normed_all, cot_all, w_gate, w_up, blocks):
    length, width = normed_all.shape
    inner = w_gate.shape[1]
    ratio = blocks.shape[0] // seq
    height, across = blocks.shape[1:]
    step = min(BLOCK, height)
    per = height // step
    blocks = blocks.reshape(ratio, seq, height, across)
    keep = pl.BlockSpec((length, width), lambda c: (0, 0), pipeline_mode=pl.Buffered(1))
    cols = pl.BlockSpec((width, step), lambda c: (0, c))
    by_col = pl.BlockSpec((length, step), lambda c: (0, c))
    by_row = pl.BlockSpec((1, seq, step, across), lambda c: (c // per, 0, c % per, 0))
    outs = pl.pallas_call(
        functools.partial(feed_kernel, seq),
        grid=(inner // step,),
        out_shape=(shape((length, inner), BF16),) * 3
        + (shape(blocks.shape, BF16), shape((width, 2 * inner), BF16)),
        in_specs=[keep, keep, cols, cols, by_row],
        out_specs=(by_col,) * 3
        + (by_row, pl.BlockSpec((width, 2 * step), lambda c: (0, c))),
        scratch_shapes=[pltpu.VMEM((step, width), BF16)],
        compiler_params=params(),
        cost_estimate=cost(12 * length * width * inner, 30 << 20),
        name="feed",
    )(normed_all, cot_all, w_gate, w_up, blocks)
    return outs, step


def back_kernel(
    seq, d_gate, d_up, w_gate, w_up, hid, blocks, middle, cot, gain, d_middle, d_low_all, d_gain,
    out_terms, held, stage, got, w_down, *sems
):
    rows, width = middle.shape
    me = lax.axis_index("seq")
    tile = tile_of(width, 512)
    meet(seq)
    sums = Scatter(seq, held, stage, got, sems[:2])

    def one(device, at):
        block = pl.ds(pl.multiple_of(device * rows, rows), rows)
        cols = pl.ds(at, tile)
        return dot_nt(d_gate[block, :], w_gate[cols, :]) + dot_nt(d_up[block, :], w_up[cols, :])

    def term(device, ref):
        def part(at):
            ref[:, pl.ds(at, tile)] = one(device, at).astype(BF16)

        each(width, tile, part)

    sums.send(term)

    def own(at):
        d_middle[:, pl.ds(at, tile)] = one(me, at)

    each(width, tile, own)
    sums.forward()
    join_blocks(blocks, seq, w_down)

    def outward(index, carry):
        block = pl.ds(pl.multiple_of(index * rows, rows), rows)
        def part(at):
            cols = pl.ds(at, tile)
            out_terms[index, :, cols] = dot(hid[block, :], w_down[:, cols]).astype(BF16)

        each(width, tile, part)
        return carry

    lax.fori_loop(0, seq, outward, 0)
    sums.finish()
    d_gain[...] = jnp.zeros_like(d_gain)

    def norm(at):
        part = pl.ds(at, 128)
        values = middle[part, :]
        grad = d_middle[part, :] + sums.terms(part)
        scale = lax.rsqrt(jnp.mean(values * values, axis=-1, keepdims=True) + EPSILON)
        weighted = grad * gain[...]
        inner = jnp.mean(weighted * values, axis=-1, keepdims=True)
        d_gain[...] += jnp.sum(grad * values * scale, axis=0, keepdims=True)
        total = cot[part, :].astype(F32) + scale * (weighted - values * (scale * scale) * inner)
        d_middle[part, :] = total
        d_low_all[me, part, :] = total.astype(BF16)

    each(rows, 128, norm)
    whole = Gather(seq, d_low_all.at[me], d_low_all, sems[2:4])
    whole.start()
    whole.forward()
    whole.finish()


def back(seq, d_gate, d_up, w_gate, w_up, hid, blocks, middle, cot, gain):
    rows, width = middle.shape
    dma = pltpu.SemaphoreType.DMA
    return pl.pallas_call(
        functools.partial(back_kernel, seq),
        out_shape=(
            shape((rows, width), F32),
            shape((seq, rows, width), BF16),
            shape((1, width), F32),
            shape((seq, rows, width), BF16),
        ),
        in_specs=[VMEM] * 9,
        out_specs=(VMEM,) * 4,
        scratch_shapes=scatter_scratch(seq, rows, width)[:3]
        + [pltpu.VMEM((hid.shape[1], width), BF16)]
        + [dma((n_copies(seq),))] * 4,
        compiler_params=params(3),
        cost_estimate=cost(60 << 30, 20 << 20),
        name="back",
    )(d_gate, d_up, w_gate, w_up, hid, blocks, middle, cot, gain)


def attend_back_kernel(
    seq, d_low, w_out, attn, packed, lse, ids_col, ids_row, cosine, sine, out_terms, middle,
    g_out, d_packed, output, held, stage, got, d_attn, d_keys, d_vals, *sems
):
    length = d_low.shape[0]
    rows_own = middle.shape[0]
    groups = packed.shape[0] // 4
    ratio = g_out.shape[0] // seq
    height, width = g_out.shape[1:]
    me = lax.axis_index("seq")
    meet(seq)
    sums = Scatter(seq, held, stage, got, sems[:2])

    def term(device, ref):
        ref[...] = out_terms[device]

    sums.send(term)

    def outer(at):
        rows = pl.ds(at, 512)
        d_attn[rows, :] = dot_nt(d_low[rows, :], w_out[...]).astype(BF16)

    each(length, 512, outer)
    for across in range(seq):
        part = dot_tn(attn[...], d_low[:, across * width : (across + 1) * width]).astype(BF16)
        for down in range(ratio):
            g_out[down * seq + across] = part[down * height : (down + 1) * height]
    sums.forward()
    d_keys[...] = jnp.zeros_like(d_keys)
    d_vals[...] = jnp.zeros_like(d_vals)
    stored = [[] for _ in range(groups)]
    for start in range(0, length, BLOCK):
        low, high = key_range(start, length)
        rows = pl.ds(start, BLOCK)
        keys = pl.ds(low, high - low)
        bias = mask_bias(ids_col, ids_row, start, low, high)
        for group in range(groups):
            base = group * 2 * HEAD_DIM
            queries = jnp.concatenate(
                [packed[group * 4, rows, :], packed[group * 4 + 1, rows, :]], axis=0
            )
            mixed = attn[rows, base : base + 2 * HEAD_DIM].astype(F32)
            d_wide = d_attn[rows, base : base + 2 * HEAD_DIM]
            product = mixed * d_wide.astype(F32)
            delta = jnp.concatenate(
                [
                    jnp.sum(product[:, :HEAD_DIM], axis=-1, keepdims=True),
                    jnp.sum(product[:, HEAD_DIM:], axis=-1, keepdims=True),
                ],
                axis=0,
            )
            d_out = jnp.concatenate([d_wide[:, :HEAD_DIM], d_wide[:, HEAD_DIM:]], axis=0)
            logs = jnp.concatenate(
                [
                    lse[rows, group * 2 : group * 2 + 1],
                    lse[rows, group * 2 + 1 : group * 2 + 2],
                ],
                axis=0,
            )
            key_rows = packed[group * 4 + 2, keys, :]
            scores = dot_nt(queries, key_rows) * SCALE + bias
            probs = jnp.exp(scores - logs)
            d_probs = dot_nt(d_out, packed[group * 4 + 3, keys, :])
            d_scores = (probs * (d_probs - delta)).astype(BF16)
            d_vals[group, keys, :] += dot_tn(probs.astype(BF16), d_out)
            d_keys[group, keys, :] += dot_tn(d_scores, queries) * SCALE
            d_query = dot(d_scores, key_rows) * SCALE
            turned = [
                part * cosine[rows, :] - swap_halves(part) * sine[rows, :]
                for part in (d_query[:BLOCK], d_query[BLOCK:])
            ]
            d_packed[rows, group * 4 * HEAD_DIM : group * 4 * HEAD_DIM + 2 * HEAD_DIM] = (
                jnp.concatenate(turned, axis=1).astype(BF16)
            )

    def last(at):
        rows = pl.ds(at, BLOCK)
        for group in range(groups):
            d_key = d_keys[group, rows, :]
            turned = d_key * cosine[rows, :] - swap_halves(d_key) * sine[rows, :]
            base = group * 4 * HEAD_DIM + 2 * HEAD_DIM
            d_packed[rows, base : base + 2 * HEAD_DIM] = jnp.concatenate(
                [turned, d_vals[group, rows, :]], axis=1
            ).astype(BF16)

    each(length, BLOCK, last)
    sums.finish()

    def total(at):
        part = pl.ds(at, 128)
        output[part, :] = middle[part, :] + out_terms[me, part, :].astype(F32) + sums.terms(part)

    each(rows_own, 128, total)


def attend_back(
    seq, fsdp, d_low_all, w_out, attn, packed, lse, ids_col, ids_row, cosine, sine, out_terms, middle
):
    rows, width = middle.shape
    length = d_low_all.shape[0]
    inner = attn.shape[1]
    groups = packed.shape[0] // 4
    height = inner // (fsdp // seq)
    return pl.pallas_call(
        functools.partial(attend_back_kernel, seq),
        out_shape=(
            shape((fsdp, height, width // seq), BF16),
            shape((length, groups * 4 * HEAD_DIM), BF16),
            shape((rows, width), F32),
        ),
        in_specs=[VMEM] * 11,
        out_specs=(VMEM,) * 3,
        scratch_shapes=scatter_scratch(seq, rows, width)[:3]
        + [pltpu.VMEM((length, inner), BF16)]
        + [pltpu.VMEM((groups, length, HEAD_DIM), F32)] * 2
        + [pltpu.SemaphoreType.DMA((n_copies(seq),))] * 2,
        compiler_params=params(4),
        cost_estimate=cost(30 << 30, 20 << 20),
        name="attend_back",
    )(d_low_all, w_out, attn, packed, lse, ids_col, ids_row, cosine, sine, out_terms, middle)


def leave_kernel(
    seq, d_packed, w_qkv, hidden, d_middle, gain, d_input, d_gain, held, stage, got, *sems
):
    rows, width = hidden.shape
    me = lax.axis_index("seq")
    tile = tile_of(width, 512)
    meet(seq)
    sums = Scatter(seq, held, stage, got, sems[:2])

    def one(device, at):
        block = pl.ds(pl.multiple_of(device * rows, rows), rows)
        return dot_nt(d_packed[block, :], w_qkv[pl.ds(at, tile), :])

    def term(device, ref):
        def part(at):
            ref[:, pl.ds(at, tile)] = one(device, at).astype(BF16)

        each(width, tile, part)

    sums.send(term)

    def own(at):
        d_input[:, pl.ds(at, tile)] = one(me, at)

    each(width, tile, own)
    sums.forward()
    sums.finish()
    d_gain[...] = jnp.zeros_like(d_gain)

    def norm(at):
        part = pl.ds(at, 128)
        values = hidden[part, :].astype(F32)
        grad = d_input[part, :] + sums.terms(part)
        scale = lax.rsqrt(jnp.mean(values * values, axis=-1, keepdims=True) + EPSILON)
        weighted = grad * gain[...]
        inner = jnp.mean(weighted * values, axis=-1, keepdims=True)
        d_gain[...] += jnp.sum(grad * values * scale, axis=0, keepdims=True)
        d_input[part, :] = d_middle[part, :] + scale * (
            weighted - values * (scale * scale) * inner
        )

    each(rows, 128, norm)


def leave(seq, d_packed, w_qkv, hidden, d_middle, gain):
    rows, width = hidden.shape
    return pl.pallas_call(
        functools.partial(leave_kernel, seq),
        out_shape=(shape((rows, width), F32), shape((1, width), F32)),
        in_specs=[VMEM] * 5,
        out_specs=(VMEM,) * 2,
        scratch_shapes=scatter_scratch(seq, rows, width),
        compiler_params=params(5),
        cost_estimate=cost(30 << 30, 10 << 20),
        name="leave",
    )(d_packed, w_qkv, hidden, d_middle, gain)


def rope_tables(ids):
    length = ids.shape[0]
    first = jnp.sum((ids[None, :] < ids[:, None]).astype(jnp.int32), axis=1)
    positions = jnp.arange(length, dtype=jnp.int32) - first
    half_dim = HEAD_DIM // 2
    freq_steps = jnp.arange(half_dim, dtype=F32)
    inverse = jnp.exp(freq_steps * (-2.0 * math.log(ROPE_BASE) / HEAD_DIM))
    angles = positions.astype(F32)[:, None] * inverse[None, :]
    cosine, sine = jnp.cos(angles), jnp.sin(angles)
    return (
        jnp.concatenate([cosine, cosine], axis=1),
        jnp.concatenate([-sine, sine], axis=1),
    )


def body(
    hidden_in, cotangent, segment_ids, w_qkv, w_out, w_gate, w_up, w_down, gain_attn, gain_mlp
):
    rows, width = hidden_in.shape
    fsdp = lax.axis_size("fsdp")
    seq = lax.axis_size("seq")
    ratio = fsdp // seq
    length = rows * seq
    moves = [
        (f * seq + s, ((f % ratio) * seq + s) * seq + f // ratio)
        for f in range(fsdp)
        for s in range(seq)
    ]
    home = [(there, here) for here, there in moves]

    def gather_cols(shard):
        return lax.all_gather(shard, "fsdp", axis=0, tiled=True)

    def gather_rows(shard):
        moved = lax.ppermute(shard, ("fsdp", "seq"), moves)
        return lax.all_gather(moved, "fsdp", axis=0, tiled=False)

    def scatter_cols(grad):
        return lax.psum_scatter(grad, "fsdp", scatter_dimension=0, tiled=True)

    def scatter_rows(blocks):
        own = lax.psum_scatter(blocks, "fsdp", scatter_dimension=0, tiled=False)
        return lax.ppermute(own, ("fsdp", "seq"), home).astype(F32)

    cols_qkv = gather_cols(w_qkv)
    blocks_out = gather_rows(w_out)
    cols_gate = gather_cols(w_gate)
    cols_up = gather_cols(w_up)
    blocks_down = gather_rows(w_down)

    hidden_all, ids_all, gains = enter(
        seq, fsdp, hidden_in, segment_ids, jnp.stack([gain_attn, gain_mlp])
    )
    gains = jnp.transpose(gains, (2, 0, 1, 3)).reshape(2, width).astype(F32)
    gain_one, gain_two = gains[:1], gains[1:]
    ids_row = ids_all.reshape(1, length)
    ids_col = ids_all.reshape(length, 1)
    cosine, sine = rope_tables(ids_all.reshape(length))

    normed_one, packed, attn, lse, cot_all = attend(
        seq, hidden_all.reshape(length, width), gain_one, ids_col, ids_row, cosine, sine,
        cols_qkv, cotangent,
    )
    cot_all = cot_all.reshape(length, width)
    middle, normed_two, rows_out = to_middle(seq, attn, blocks_out, hidden_in, gain_two)
    normed_two = normed_two.reshape(length, width)
    (hid, d_gate, d_up, g_down, g_both), step = feed(
        seq, normed_two, cot_all, cols_gate, cols_up, blocks_down
    )
    g_both = scatter_cols(g_both)
    g_down = scatter_rows(g_down.reshape(blocks_down.shape))
    d_middle, d_low_all, part_two, out_terms = back(
        seq, d_gate, d_up, cols_gate, cols_up, hid, blocks_down, middle, cotangent, gain_two
    )
    g_out, d_packed, output = attend_back(
        seq, fsdp, d_low_all.reshape(length, width), rows_out, attn, packed, lse, ids_col, ids_row,
        cosine, sine, out_terms, middle,
    )
    g_qkv = dot_tn(normed_one, d_packed).astype(BF16)
    g_out = scatter_rows(g_out)
    g_qkv = scatter_cols(g_qkv).astype(F32)
    d_tokens, part_one = leave(seq, d_packed, cols_qkv, hidden_in, d_middle, gain_one)
    totals = lax.psum(jnp.concatenate([part_one, part_two], axis=0), ("fsdp", "seq"))
    share = width // (fsdp * seq)
    at = (lax.axis_index("fsdp") * seq + lax.axis_index("seq")) * share
    g_gains = lax.dynamic_slice_in_dim(totals, at, share, 1)
    g_both = g_both.reshape(g_both.shape[0], -1, 2, step).astype(F32)
    g_gate = g_both[:, :, 0].reshape(g_both.shape[0], -1)
    g_up = g_both[:, :, 1].reshape(g_both.shape[0], -1)
    return (output, d_tokens, g_qkv, g_out, g_gate, g_up, g_down, g_gains[0], g_gains[1])


def solution(mesh):
    both = P(("fsdp", "seq"), None)
    split = P("fsdp", "seq")
    gain = P(("fsdp", "seq"))
    in_specs = (both, both, split, split, split, split, split, split, gain, gain)
    out_specs = (both, both, split, split, split, split, split, gain, gain)
    return jax.shard_map(body, mesh=mesh, in_specs=in_specs, out_specs=out_specs, check_vma=False)
```

```python
import functools
import math

import jax
import jax.numpy as jnp
from jax import lax
from jax.experimental import pallas as pl
from jax.experimental.pallas import tpu as pltpu
from jax.sharding import PartitionSpec as P

HEAD_DIM = 96
EPSILON = 1e-05
ROPE_BASE = 100000.0
NEGATIVE = -1e30
SCALE = 1.0 / math.sqrt(HEAD_DIM)
MESH = pl.DeviceIdType.MESH
BLOCK = 256
F32 = jnp.float32
BF16 = jnp.bfloat16
ANY = pl.BlockSpec(memory_space=pl.ANY)
VMEM = pl.BlockSpec(memory_space=pltpu.VMEM)


def dot(left, right):
    return jnp.dot(left, right, preferred_element_type=F32)


def dot_nt(left, right):
    return lax.dot_general(left, right, (((1,), (1,)), ((), ())), preferred_element_type=F32)


def dot_tn(left, right):
    return lax.dot_general(left, right, (((0,), (0,)), ((), ())), preferred_element_type=F32)


def shape(dims, kind):
    return jax.ShapeDtypeStruct(dims, kind)


def params(collective=None):
    return pltpu.CompilerParams(
        collective_id=collective,
        has_side_effects=collective is not None,
        vmem_limit_bytes=60 << 20,
    )


def cost(flops, moved):
    return pl.CostEstimate(flops=flops, bytes_accessed=moved, transcendentals=0)


def others(size):
    me = lax.axis_index("seq")
    if size == 4:
        low, high = lax.rem(me, 2), me // 2
        return [high * 2 + 1 - low, (1 - high) * 2 + low, (1 - high) * 2 + 1 - low]
    return [lax.rem(me + step, size) for step in range(1, size)]


def meet(seq, fsdp, pairs=(), ends=True):
    barrier = pltpu.get_barrier_semaphore()
    row = lax.axis_index("fsdp")
    for peer in others(seq):
        pl.semaphore_signal(barrier, inc=1, device_id={"seq": peer}, device_id_type=MESH)
    for step in range(1, fsdp):
        peer = lax.rem(row + step, fsdp)
        pl.semaphore_signal(barrier, inc=1, device_id={"fsdp": peer}, device_id_type=MESH)
    for there in pairs:

        @pl.when(away(there))
        def _(there=there):
            pl.semaphore_signal(
                barrier,
                inc=1,
                device_id={"fsdp": there[0], "seq": there[1]},
                device_id_type=MESH,
            )

    if pairs:

        @pl.when(away(pairs[0]))
        def _():
            pl.semaphore_wait(barrier, seq + fsdp - 2 + len(pairs))

        @pl.when(jnp.logical_not(away(pairs[0])))
        def _():
            pl.semaphore_wait(barrier, seq + fsdp - 2)
    elif ends:
        pl.semaphore_wait(barrier, seq + fsdp - 2)


def away(there):
    return jnp.logical_or(
        there[0] != lax.axis_index("fsdp"), there[1] != lax.axis_index("seq")
    )


def row_owner(seq, fsdp):
    row, me = lax.axis_index("fsdp"), lax.axis_index("seq")
    ratio = fsdp // seq
    to = (lax.rem(row, ratio) * seq + me, row // ratio)
    source = (me * ratio + row // seq, lax.rem(row, seq))
    return to, source


def push(src, dst, sems, index, peer, axis="seq", slot=None):
    return pltpu.make_async_remote_copy(
        src_ref=src,
        dst_ref=dst,
        send_sem=sems[0].at[index],
        recv_sem=sems[1].at[index if slot is None else slot],
        device_id={axis: peer},
        device_id_type=MESH,
    )


class Move:
    def __init__(self, src, dst, to, sems, index):
        self.local = pltpu.make_async_copy
        self.src, self.dst, self.to, self.sems, self.index = src, dst, to, sems, index

    def remote(self):
        return pltpu.make_async_remote_copy(
            src_ref=self.src,
            dst_ref=self.dst,
            send_sem=self.sems[0].at[self.index],
            recv_sem=self.sems[1].at[self.index],
            device_id={"fsdp": self.to[0], "seq": self.to[1]},
            device_id_type=MESH,
        )

    def within(self):
        return pltpu.make_async_copy(self.src, self.dst, self.sems[2].at[self.index])

    def start(self):
        @pl.when(away(self.to))
        def _():
            self.remote().start()

        @pl.when(jnp.logical_not(away(self.to)))
        def _():
            self.within().start()

    def finish(self):
        @pl.when(away(self.to))
        def _():
            self.remote().wait()

        @pl.when(jnp.logical_not(away(self.to)))
        def _():
            self.within().wait()


def chips(row):
    chip, core = row // 2, lax.rem(row, 2)
    pair = chip // 2
    mate = pair * 2 + 1 - lax.rem(chip, 2)
    first = (1 - pair) * 2
    return chip, core, mate, first, first + 1


def inner_chip(chip):
    return jnp.logical_or(chip == 1, chip == 2)


def line_scratch(fsdp):
    dma = pltpu.SemaphoreType.DMA
    return [dma((max(fsdp, 9),)), dma((max(fsdp, 8),)), dma((1,))]


class LineGather:
    def __init__(self, fsdp, own, whole, sems):
        self.fsdp, self.own, self.whole, self.sems = fsdp, own, whole, sems
        self.row = lax.axis_index("fsdp")
        if fsdp == 8:
            self.chip, self.core, self.mate, self.one, self.two = chips(self.row)
            self.near = 2 - self.chip // 2

    def at(self, chip):
        return chip * 2 + self.core

    def send(self, slot, index, peer, own=False):
        src = self.own if own else self.whole.at[slot]
        return push(src, self.whole.at[slot], self.sems, index, peer, "fsdp", slot)

    def arrive(self, slot):
        self.send(slot, 0, self.row).wait_recv()

    def local(self):
        return pltpu.make_async_copy(self.own, self.whole.at[self.row], self.sems[2].at[0])

    def sibling(self, chip, index):
        return self.send(self.at(chip), index, self.chip * 2 + 1 - self.core)

    def start(self):
        if self.fsdp != 8:
            for step in range(1, self.fsdp):
                peer = lax.rem(self.row + step, self.fsdp)
                self.send(self.row, step - 1, peer, own=True).start()
        else:
            self.send(self.row, 1, self.at(self.near), own=True).start()
            self.send(self.row, 0, self.at(self.mate), own=True).start()
            self.send(self.row, 2, self.chip * 2 + 1 - self.core, own=True).start()
        self.local().start()

    def pass_on(self, index, chip):
        self.arrive(self.at(chip))

        @pl.when(inner_chip(self.chip))
        def _():
            self.send(self.at(chip), index, self.at(self.mate)).start()

        self.sibling(chip, index + 3).start()

    def forward(self):
        if self.fsdp == 8:

            @pl.when(inner_chip(self.chip))
            def _():
                self.pass_on(3, self.one)
                self.pass_on(4, self.two)

    def finish(self):
        if self.fsdp != 8:
            for step in range(1, self.fsdp):
                self.arrive(lax.rem(self.row - step + self.fsdp, self.fsdp))
            for step in range(1, self.fsdp):
                self.send(self.row, step - 1, self.row, own=True).wait_send()
            self.local().wait()
            return
        self.arrive(self.at(self.mate))
        self.sibling(self.mate, 5).start()

        @pl.when(jnp.logical_not(inner_chip(self.chip)))
        def _():
            self.pass_on(3, self.one)
            self.pass_on(4, self.two)

        for chip in range(4):
            self.arrive(chip * 2 + 1 - self.core)
        self.local().wait()
        for index in range(3):
            self.send(self.row, index, self.row, own=True).wait_send()
        for index, chip in ((5, self.mate), (6, self.one), (7, self.two)):
            self.sibling(chip, index).wait_send()

        @pl.when(inner_chip(self.chip))
        def _():
            self.send(self.at(self.one), 3, self.row).wait_send()
            self.send(self.at(self.two), 4, self.row).wait_send()


def reduce_scratch(fsdp, height, width):
    if fsdp == 8:
        bufs = [pltpu.VMEM((4, height, width), BF16)] * 2
    else:
        bufs = [pltpu.VMEM((1, 16, 128), BF16), pltpu.VMEM((fsdp - 1, height, width), BF16)]
    return bufs + line_scratch(fsdp)


class LineReduce:
    def __init__(self, fsdp, grad, pair, got, *sems):
        self.fsdp, self.grad, self.pair, self.got, self.sems = fsdp, grad, pair, got, sems
        self.row = lax.axis_index("fsdp")
        if fsdp == 8:
            self.chip, self.core, self.mate, self.one, self.two = chips(self.row)
            self.roles = [self.one, self.two, self.mate, self.chip]

    def rows(self, task):
        height = self.grad.shape[1]
        step = 64
        while height % step:
            step //= 2
        each(height, step, lambda at: task(pl.ds(at, step)))

    def across(self, role):
        other = 1 - self.core
        return push(
            self.grad.at[self.roles[role] * 2 + other],
            self.pair.at[role],
            self.sems,
            role,
            self.chip * 2 + other,
            "fsdp",
        )

    def to_mate(self, role):
        slot = (1, 2, 0)[role]
        return push(
            self.pair.at[role],
            self.got.at[slot],
            self.sems,
            4 + slot,
            self.mate * 2 + self.core,
            "fsdp",
        )

    def to_other(self, role):
        return push(
            self.pair.at[role],
            self.got.at[3],
            self.sems,
            7 + role,
            self.roles[role] * 2 + self.core,
            "fsdp",
            7,
        )

    def direct(self, step):
        peer = lax.rem(self.row + step, self.fsdp)
        return push(
            self.grad.at[peer], self.got.at[step - 1], self.sems, step - 1, peer, "fsdp"
        )

    def start(self):
        if self.fsdp != 8:
            for step in range(1, self.fsdp):
                self.direct(step).start()
        else:
            for role in range(4):
                self.across(role).start()

    def pairs(self):
        if self.fsdp != 8:
            return
        for role in range(3):
            self.across(role).wait_recv()
            mine = self.roles[role] * 2 + self.core

            def add(part, role=role, mine=mine):
                self.pair[role, part] = (
                    self.pair[role, part].astype(F32) + self.grad[mine, part].astype(F32)
                ).astype(BF16)

            self.rows(add)
            if role < 2:

                @pl.when(jnp.logical_not(inner_chip(self.chip)))
                def _(role=role):
                    self.to_mate(role).start()
            else:
                self.to_mate(role).start()

    def forward(self):
        if self.fsdp != 8:
            return

        @pl.when(inner_chip(self.chip))
        def _():
            for role in range(2):
                self.to_mate(role).wait_recv()

                def add(part, role=role):
                    self.pair[role, part] = (
                        self.pair[role, part].astype(F32) + self.got[role + 1, part].astype(F32)
                    ).astype(BF16)

                self.rows(add)
                self.to_other(role).start()

    def finish(self, out):
        if self.fsdp != 8:
            for step in range(1, self.fsdp):
                self.direct(step).wait_recv()

            def total(part):
                value = self.grad[self.row, part].astype(F32)
                for step in range(1, self.fsdp):
                    value = value + self.got[step - 1, part].astype(F32)
                out[part, :] = value.astype(out.dtype)

            self.rows(total)
            for step in range(1, self.fsdp):
                self.direct(step).wait_send()
            return
        self.across(3).wait_recv()
        self.to_mate(2).wait_recv()
        self.to_other(0).wait_recv()

        def total(part):
            out[part, :] = (
                self.grad[self.row, part].astype(F32)
                + self.pair[3, part].astype(F32)
                + self.got[0, part].astype(F32)
                + self.got[3, part].astype(F32)
            ).astype(out.dtype)

        self.rows(total)
        for role in range(4):
            self.across(role).wait_send()
        self.to_mate(2).wait_send()

        @pl.when(inner_chip(self.chip))
        def _():
            self.to_other(0).wait_send()
            self.to_other(1).wait_send()

        @pl.when(jnp.logical_not(inner_chip(self.chip)))
        def _():
            self.to_mate(0).wait_send()
            self.to_mate(1).wait_send()


def n_copies(size):
    return 6 if size == 4 else size - 1


class Gather:
    def __init__(self, size, own, whole, sems):
        self.size, self.own, self.whole, self.sems = size, own, whole, sems
        self.me = lax.axis_index("seq")
        self.peers = others(size)
        half = own.shape[0] // 2
        self.parts = [pl.ds(0, half), pl.ds(half, half)]

    def copy(self, index):
        me, own, whole, sems = self.me, self.own, self.whole, self.sems
        if self.size != 4:
            return push(own, whole.at[me], sems, index, self.peers[index])
        side, over, _ = self.peers
        one, two = self.parts
        src, dst, peer = [
            (own.at[one], whole.at[me, one], side),
            (own.at[two], whole.at[me, two], side),
            (own.at[two], whole.at[me, two], over),
            (own.at[one], whole.at[me, one], over),
            (whole.at[side, one], whole.at[side, one], over),
            (whole.at[over, two], whole.at[over, two], side),
        ][index]
        return push(src, dst, sems, index, peer)

    def start(self):
        for index in (0, 2, 1, 3) if self.size == 4 else range(self.size - 1):
            self.copy(index).start()

    def forward(self):
        if self.size == 4:
            for index in (0, 2):
                self.copy(index).wait_recv()
            self.copy(4).start()
            self.copy(5).start()

    def finish(self, task=None):
        if self.size == 4:
            order = [(self.peers[0], (1,)), (self.peers[1], (3,)), (self.peers[2], (4, 5))]
        else:
            order = [
                (lax.rem(self.me - k - 1 + self.size, self.size), (k,))
                for k in range(self.size - 1)
            ]
        for device, parts in order:
            for index in parts:
                self.copy(index).wait_recv()
            if task is not None:
                task(device)
        for index in range(n_copies(self.size)):
            self.copy(index).wait_send()


def scatter_scratch(size, rows, width):
    if size == 4:
        held = [
            pltpu.VMEM((3, rows, width), BF16),
            pltpu.VMEM((2, rows // 2, width), BF16),
            pltpu.VMEM((2, rows, width), BF16),
        ]
    else:
        held = [
            pltpu.VMEM((size - 1, rows, width), BF16),
            pltpu.VMEM((1, 16, 128), BF16),
            pltpu.VMEM((size - 1, rows, width), BF16),
        ]
    return held + [pltpu.SemaphoreType.DMA((n_copies(size),))] * 2


class Scatter:
    def __init__(self, size, held, stage, got, sems):
        self.size, self.held, self.stage, self.got, self.sems = size, held, stage, got, sems
        self.peers = others(size)
        half = held.shape[1] // 2
        self.parts = [pl.ds(0, half), pl.ds(half, half)]

    def copy(self, index):
        held, stage, got, sems = self.held, self.stage, self.got, self.sems
        if self.size != 4:
            return push(held.at[index], got.at[index], sems, index, self.peers[index])
        side, over, _ = self.peers
        one, two = self.parts
        src, dst, peer = [
            (held.at[2, one], stage.at[0], side),
            (held.at[2, two], stage.at[1], over),
            (held.at[0, one], got.at[0, one], side),
            (held.at[1, two], got.at[1, two], over),
            (held.at[0, two], got.at[0, two], side),
            (held.at[1, one], got.at[1, one], over),
        ][index]
        return push(src, dst, sems, index, peer)

    def send(self, make, hooks=()):
        hooks = list(hooks)
        order = [(2, (0, 1)), (0, (2,)), (1, (3,))]
        if self.size != 4:
            order = [(k, (k,)) for k in range(self.size - 1)]
        for place, sends in order:
            make(self.peers[place], self.held.at[place])
            for index in sends:
                self.copy(index).start()
            if hooks:
                hooks.pop(0)()
        for hook in hooks:
            hook()

    def forward(self):
        if self.size == 4:
            one, two = self.parts
            held, stage = self.held, self.stage
            self.copy(1).wait_recv()
            held[0, two] = (held[0, two].astype(F32) + stage[1].astype(F32)).astype(BF16)
            self.copy(4).start()
            self.copy(0).wait_recv()
            held[1, one] = (held[1, one].astype(F32) + stage[0].astype(F32)).astype(BF16)
            self.copy(5).start()

    def finish(self):
        for index in range(n_copies(self.size)):
            if self.size != 4 or index > 1:
                self.copy(index).wait_recv()
        for index in range(n_copies(self.size)):
            self.copy(index).wait_send()

    def terms(self, rows):
        total = self.got[0, rows].astype(F32)
        for k in range(1, self.got.shape[0]):
            total = total + self.got[k, rows].astype(F32)
        return total


def each(count, step, task):
    def run(index, carry):
        task(pl.multiple_of(index * step, step))
        return carry

    lax.fori_loop(0, count // step, run, 0)


def tile_of(width, most):
    tile = most
    while width % tile:
        tile //= 2
    return tile


def enter_kernel(
    seq, fsdp, hidden, ids, gain_one, gain_two, w_qkv, w_out, w_down, normed, ids_row, ids_col,
    cosine, sine, gains, cols_qkv, moved_out, moved_down, raw, ids_all, gain_own, gain_parts,
    *sems
):
    block_sems, id_sems, gain_sems, wide_sems = sems[0:2], sems[2:4], sems[4:6], sems[6:8]
    line_sems, move_sems, local = sems[8:11], sems[11:14], sems[14]
    rows = hidden.shape[0]
    length = rows * seq
    me, row = lax.axis_index("seq"), lax.axis_index("fsdp")
    to, source = row_owner(seq, fsdp)
    share = gain_one.shape[1]
    gain_own[0:1, :] = gain_one[...].astype(F32)
    gain_own[1:2, :] = gain_two[...].astype(F32)
    gain_parts[row, me] = gain_own[...]
    ids_all[me] = ids[...]
    meet(seq, fsdp, (to, source))
    whole = Gather(seq, hidden, raw, block_sems)
    line = LineGather(fsdp, w_qkv, cols_qkv, line_sems)
    moves = [
        Move(w_out, moved_out, to, move_sems, 0),
        Move(w_down, moved_down, to, move_sems, 1),
    ]
    id_copies = [
        push(ids, ids_all.at[me], id_sems, k, peer) for k, peer in enumerate(others(seq))
    ]
    gain_copies = [
        push(gain_own, gain_parts.at[row, me], gain_sems, k, peer)
        for k, peer in enumerate(others(seq))
    ]
    for copy in id_copies + gain_copies:
        copy.start()
    line.start()
    whole.start()
    for move in moves:
        move.start()
    mine = pltpu.make_async_copy(hidden, raw.at[me], local.at[0])
    mine.start()
    for copy in gain_copies:
        copy.wait()
    wide = [
        push(
            gain_parts.at[row],
            gain_parts.at[row],
            wide_sems,
            step - 1,
            lax.rem(row + step, fsdp),
            "fsdp",
        )
        for step in range(1, fsdp)
    ]
    for copy in wide:
        copy.start()
    for copy in id_copies:
        copy.wait()
    for k in range(seq):
        for at in range(0, rows, 128):
            piece = ids_all[k, :, at : at + 128]
            ids_row[:, k * rows + at : k * rows + at + 128] = piece
            turned = jnp.transpose(jnp.broadcast_to(piece, (128, 128)))
            ids_col[k * rows + at : k * rows + at + 128, :] = turned[:, :1]
    half = HEAD_DIM // 2
    step = lax.broadcasted_iota(jnp.int32, (1, half), 1).astype(F32)
    inverse = jnp.exp(step * (-2.0 * math.log(ROPE_BASE) / HEAD_DIM))

    def table(at):
        part = pl.ds(at, BLOCK)
        first = jnp.sum(
            (ids_row[...] < ids_col[part, :]).astype(jnp.int32).astype(F32),
            axis=-1,
            keepdims=True,
        )
        place = (at + lax.broadcasted_iota(jnp.int32, (BLOCK, 1), 0)).astype(F32) - first
        angles = place * inverse
        cos, sin = jnp.cos(angles), jnp.sin(angles)
        cosine[part, :] = jnp.concatenate([cos, cos], axis=1)
        sine[part, :] = jnp.concatenate([-sin, sin], axis=1)

    each(length, BLOCK, table)
    for copy in wide:
        copy.wait()
    for r in range(fsdp):
        for k in range(seq):
            at = (r * seq + k) * share
            gains[:, at : at + share] = gain_parts[r, k]
    whole.forward()
    line.forward()
    mine.wait()

    def norm(device):
        base = pl.multiple_of(device * rows, rows)

        def part(at):
            values = raw[device, pl.ds(at, 128), :].astype(F32)
            scale = lax.rsqrt(jnp.mean(values * values, axis=-1, keepdims=True) + EPSILON)
            normed[pl.ds(base + at, 128), :] = (values * scale * gains[0:1, :]).astype(BF16)

        each(rows, 128, part)

    norm(me)
    whole.finish(norm)
    line.finish()
    for move in moves:
        move.finish()


def enter(seq, fsdp, hidden, ids, gain_one, gain_two, w_qkv, w_out, w_down):
    rows, width = hidden.shape
    length = rows * seq
    dma = pltpu.SemaphoreType.DMA
    share = gain_one.shape[1]
    return pl.pallas_call(
        functools.partial(enter_kernel, seq, fsdp),
        out_shape=(
            shape((length, width), BF16),
            shape((1, length), jnp.int32),
            shape((length, 1), jnp.int32),
            shape((length, HEAD_DIM), F32),
            shape((length, HEAD_DIM), F32),
            shape((2, width), F32),
            shape((fsdp,) + w_qkv.shape, BF16),
            shape(w_out.shape, BF16),
            shape(w_down.shape, BF16),
        ),
        in_specs=[ANY] + [VMEM] * 3 + [ANY] * 3,
        out_specs=(VMEM,) * 6 + (ANY,) * 3,
        scratch_shapes=[
            pltpu.VMEM((seq, rows, width), BF16),
            pltpu.VMEM((seq, 1, rows), jnp.int32),
            pltpu.VMEM((2, share), F32),
            pltpu.VMEM((fsdp, seq, 2, share), F32),
        ]
        + [dma((n_copies(seq),))] * 2
        + [dma((seq - 1,))] * 4
        + [dma((fsdp - 1,))] * 2
        + line_scratch(fsdp)
        + [dma((2,))] * 3
        + [dma((1,))],
        compiler_params=params(0),
        name="enter",
    )(hidden, ids, gain_one, gain_two, w_qkv, w_out, w_down)


def swap_halves(block):
    half = HEAD_DIM // 2
    return jnp.concatenate([block[:, half:], block[:, :half]], axis=1)


def mask_bias(ids_col, ids_row, start, low, high):
    span = high - low
    query = start + lax.broadcasted_iota(jnp.int32, (BLOCK, span), 0)
    key = low + lax.broadcasted_iota(jnp.int32, (BLOCK, span), 1)
    same = ids_col[pl.ds(start, BLOCK), :] == ids_row[:, low:high]
    bias = jnp.where(jnp.logical_and(same, key <= query), 0.0, NEGATIVE)
    return jnp.concatenate([bias, bias], axis=0)


def key_range(start, length):
    return max(0, start - length // 2), start + BLOCK


def attend_kernel(
    seq, fsdp, normed, ids_col, ids_row, cosine, sine, w_qkv, cot, w_out, w_gate, packed, attn,
    lse, cot_all, blocks_out, cols_gate, *sems
):
    length = normed.shape[0]
    groups = w_qkv.shape[1] // (4 * HEAD_DIM)
    meet(seq, fsdp)
    whole = Gather(seq, cot, cot_all, sems[:2])
    lines = [
        LineGather(fsdp, w_out, blocks_out, sems[3:6]),
        LineGather(fsdp, w_gate, cols_gate, sems[6:9]),
    ]
    for exchange in lines:
        exchange.start()
    whole.start()
    own = pltpu.make_async_copy(cot, cot_all.at[lax.axis_index("seq")], sems[2].at[0])
    own.start()
    for group in range(groups):

        def project(at, group=group):
            rows = pl.ds(at, 512)
            low = group * 4 * HEAD_DIM
            proj = dot(normed[rows, :], w_qkv[:, low : low + 4 * HEAD_DIM])
            for slot in range(4):
                part = proj[:, slot * HEAD_DIM : (slot + 1) * HEAD_DIM]
                if slot < 3:
                    part = part * cosine[rows, :] + swap_halves(part) * sine[rows, :]
                packed[group * 4 + slot, rows, :] = part.astype(BF16)

        each(length, 512, project)
    for start in range(0, length, BLOCK):
        low, high = key_range(start, length)
        rows = pl.ds(start, BLOCK)
        keys = pl.ds(low, high - low)
        bias = mask_bias(ids_col, ids_row, start, low, high)
        mixed, logs = [], []
        for group in range(groups):
            queries = jnp.concatenate(
                [packed[group * 4, rows, :], packed[group * 4 + 1, rows, :]], axis=0
            )
            scores = dot_nt(queries, packed[group * 4 + 2, keys, :]) * SCALE + bias
            most = jnp.max(scores, axis=-1, keepdims=True)
            grown = jnp.exp(scores - most)
            total = jnp.sum(grown, axis=-1, keepdims=True)
            weights = (grown * (1.0 / total)).astype(BF16)
            out = dot(weights, packed[group * 4 + 3, keys, :])
            log_total = most + jnp.log(total)
            mixed += [out[:BLOCK], out[BLOCK:]]
            logs += [log_total[:BLOCK], log_total[BLOCK:]]
        attn[rows, :] = jnp.concatenate(mixed, axis=1).astype(BF16)
        lane = lax.broadcasted_iota(jnp.int32, (BLOCK, 128), 1)
        stats = jnp.zeros((BLOCK, 128), F32)
        for head, log_total in enumerate(logs):
            stats = jnp.where(lane == head, log_total, stats)
        lse[rows, :] = stats
        if start == BLOCK:
            whole.forward()
            lines[0].forward()
        if start == 2 * BLOCK:
            lines[1].forward()
    whole.finish()
    own.wait()
    for exchange in lines:
        exchange.finish()


def attend(seq, fsdp, normed, ids_col, ids_row, cosine, sine, w_qkv, cot, w_out, w_gate):
    length, width = normed.shape
    groups = w_qkv.shape[1] // (4 * HEAD_DIM)
    dma = pltpu.SemaphoreType.DMA
    return pl.pallas_call(
        functools.partial(attend_kernel, seq, fsdp),
        out_shape=(
            shape((groups * 4, length, HEAD_DIM), BF16),
            shape((length, groups * 2 * HEAD_DIM), BF16),
            shape((length, 128), F32),
            shape((seq,) + cot.shape, BF16),
            shape((fsdp,) + w_out.shape, BF16),
            shape((fsdp,) + w_gate.shape, BF16),
        ),
        in_specs=[VMEM] * 6 + [ANY] * 3,
        out_specs=(VMEM,) * 3 + (ANY,) * 3,
        scratch_shapes=[dma((n_copies(seq),))] * 2
        + [dma((1,))]
        + line_scratch(fsdp) * 2,
        compiler_params=params(1),
        name="attend",
    )(normed, ids_col, ids_row, cosine, sine, w_qkv, cot, w_out, w_gate)


def join_blocks(blocks, seq, whole):
    ratio = blocks.shape[0] // seq
    height, width = blocks.shape[1:]
    for down in range(ratio):
        for across in range(seq):
            whole[down * height : (down + 1) * height, across * width : (across + 1) * width] = (
                blocks[down * seq + across]
            )


def middle_kernel(
    seq, fsdp, attn, blocks, hidden, gain, w_up, w_down, middle, normed_all, w_out, cols_up,
    blocks_down, held, stage, got, *sems
):
    rows, width = hidden.shape
    me = lax.axis_index("seq")
    tile = tile_of(width, 512)
    meet(seq, fsdp, ends=False)
    join_blocks(blocks, seq, w_out)
    pl.semaphore_wait(pltpu.get_barrier_semaphore(), seq + fsdp - 2)
    lines = [
        LineGather(fsdp, w_up, cols_up, sems[4:7]),
        LineGather(fsdp, w_down, blocks_down, sems[7:10]),
    ]
    for exchange in lines:
        exchange.start()
    sums = Scatter(seq, held, stage, got, sems[:2])

    def term(device, ref):
        block = pl.ds(pl.multiple_of(device * rows, rows), rows)

        def part(at):
            ref[:, pl.ds(at, tile)] = dot(attn[block, :], w_out[:, pl.ds(at, tile)]).astype(BF16)

        each(width, tile, part)

    sums.send(term)
    block = pl.ds(pl.multiple_of(me * rows, rows), rows)

    def own(at):
        cols = pl.ds(at, tile)
        middle[:, cols] = hidden[:, cols].astype(F32) + dot(attn[block, :], w_out[:, cols])

    each(width, tile, own)
    sums.forward()
    lines[0].forward()
    sums.finish()

    def norm(at):
        part = pl.ds(at, 128)
        values = middle[part, :] + sums.terms(part)
        middle[part, :] = values
        scale = lax.rsqrt(jnp.mean(values * values, axis=-1, keepdims=True) + EPSILON)
        normed_all[me, part, :] = (values * scale * gain[1:2, :]).astype(BF16)

    each(rows, 128, norm)
    whole = Gather(seq, normed_all.at[me], normed_all, sems[2:4])
    whole.start()
    whole.forward()
    lines[1].forward()
    whole.finish()
    for exchange in lines:
        exchange.finish()


def to_middle(seq, fsdp, attn, blocks, hidden, gain, w_up, w_down):
    rows, width = hidden.shape
    dma = pltpu.SemaphoreType.DMA
    return pl.pallas_call(
        functools.partial(middle_kernel, seq, fsdp),
        out_shape=(
            shape((rows, width), F32),
            shape((seq, rows, width), BF16),
            shape((attn.shape[1], width), BF16),
            shape((fsdp,) + w_up.shape, BF16),
            shape((fsdp,) + w_down.shape, BF16),
        ),
        in_specs=[VMEM] * 4 + [ANY] * 2,
        out_specs=(VMEM,) * 3 + (ANY,) * 2,
        scratch_shapes=scatter_scratch(seq, rows, width)
        + [dma((n_copies(seq),))] * 2
        + line_scratch(fsdp) * 2,
        compiler_params=params(2),
        name="middle",
    )(attn, blocks, hidden, gain, w_up, w_down)


def feed_kernel(
    seq, normed, cot, w_gate, w_up, blocks, hid, d_gate, d_up, g_down, g_gate, g_up, w_down
):
    length = normed.shape[0]
    for across in range(seq):
        width = blocks.shape[-1]
        w_down[:, across * width : (across + 1) * width] = blocks[0, across]

    def part(at):
        rows = pl.ds(at, 512)
        gate = dot(normed[rows, :], w_gate[...])
        up = dot(normed[rows, :], w_up[...])
        d_hid = dot_nt(cot[rows, :], w_down[...])
        sig = 1.0 / (1.0 + jnp.exp(-gate))
        active = gate * sig
        hid[rows, :] = (active * up).astype(BF16)
        d_gate[rows, :] = (d_hid * up * sig * (1.0 + gate * (1.0 - sig))).astype(BF16)
        d_up[rows, :] = (d_hid * active).astype(BF16)

    each(length, 512, part)
    for across in range(seq):
        width = blocks.shape[-1]
        cols = slice(across * width, (across + 1) * width)
        g_down[0, across] = dot_tn(hid[...], cot[:, cols]).astype(BF16)

    def grads(at):
        rows = pl.ds(at, 512)
        g_gate[rows, :] = dot_tn(normed[:, rows], d_gate[...]).astype(BF16)
        g_up[rows, :] = dot_tn(normed[:, rows], d_up[...]).astype(BF16)

    each(normed.shape[1], 512, grads)


def feed(seq, normed_all, cot_all, w_gate, w_up, blocks):
    length, width = normed_all.shape
    inner = w_gate.shape[1]
    ratio = blocks.shape[0] // seq
    height, across = blocks.shape[1:]
    step = min(BLOCK, height)
    per = height // step
    blocks = blocks.reshape(ratio, seq, height, across)
    keep = pl.BlockSpec((length, width), lambda c: (0, 0), pipeline_mode=pl.Buffered(1))
    cols = pl.BlockSpec((width, step), lambda c: (0, c))
    by_col = pl.BlockSpec((length, step), lambda c: (0, c))
    by_row = pl.BlockSpec((1, seq, step, across), lambda c: (c // per, 0, c % per, 0))
    return pl.pallas_call(
        functools.partial(feed_kernel, seq),
        grid=(inner // step,),
        out_shape=(shape((length, inner), BF16),) * 3
        + (shape(blocks.shape, BF16),)
        + (shape((width, inner), BF16),) * 2,
        in_specs=[keep, keep, cols, cols, by_row],
        out_specs=(by_col,) * 3
        + (by_row, cols, cols),
        scratch_shapes=[pltpu.VMEM((step, width), BF16)],
        compiler_params=params(),
        cost_estimate=cost(12 * length * width * inner, 30 << 20),
        name="feed",
    )(normed_all, cot_all, w_gate, w_up, blocks)


def back_kernel(
    seq, fsdp, d_gate, d_up, w_gate, w_up, hid, blocks, middle, cot, gain, g_gate, g_up, d_middle,
    d_low_all, d_gain, out_terms, own_gate, own_up, held, stage, got, w_down, *rest
):
    sems = rest[:4]
    size = len(reduce_scratch(fsdp, 16, 128))
    lines = [
        LineReduce(fsdp, g_gate, *rest[4 : 4 + size]),
        LineReduce(fsdp, g_up, *rest[4 + size :]),
    ]
    rows, width = middle.shape
    me = lax.axis_index("seq")
    tile = tile_of(width, 512)
    meet(seq, fsdp)
    for exchange in lines:
        exchange.start()
    sums = Scatter(seq, held, stage, got, sems[:2])

    def one(device, at):
        block = pl.ds(pl.multiple_of(device * rows, rows), rows)
        cols = pl.ds(at, tile)
        return dot_nt(d_gate[block, :], w_gate[cols, :]) + dot_nt(d_up[block, :], w_up[cols, :])

    def term(device, ref):
        def part(at):
            ref[:, pl.ds(at, tile)] = one(device, at).astype(BF16)

        each(width, tile, part)

    sums.send(term, [lines[0].pairs, lines[1].pairs])

    def own(at):
        d_middle[:, pl.ds(at, tile)] = one(me, at)

    each(width, tile, own)
    sums.forward()
    join_blocks(blocks, seq, w_down)

    def outward(index, carry=0):
        block = pl.ds(pl.multiple_of(index * rows, rows), rows)

        def part(at):
            cols = pl.ds(at, tile)
            out_terms[index, :, cols] = dot(hid[block, :], w_down[:, cols]).astype(BF16)

        each(width, tile, part)
        return carry

    lax.fori_loop(0, seq, outward, 0)
    lines[0].forward()
    sums.finish()
    d_gain[...] = jnp.zeros_like(d_gain)

    def norm(at):
        part = pl.ds(at, 128)
        values = middle[part, :]
        grad = d_middle[part, :] + sums.terms(part)
        scale = lax.rsqrt(jnp.mean(values * values, axis=-1, keepdims=True) + EPSILON)
        weighted = grad * gain[1:2, :]
        inner = jnp.mean(weighted * values, axis=-1, keepdims=True)
        d_gain[...] += jnp.sum(grad * values * scale, axis=0, keepdims=True)
        total = cot[part, :].astype(F32) + scale * (weighted - values * (scale * scale) * inner)
        d_middle[part, :] = total
        d_low_all[me, part, :] = total.astype(BF16)

    each(rows, 128, norm)
    whole = Gather(seq, d_low_all.at[me], d_low_all, sems[2:4])
    whole.start()
    whole.forward()
    lines[1].forward()
    lines[0].finish(own_gate)
    whole.finish()
    lines[1].finish(own_up)


def back(seq, fsdp, d_gate, d_up, w_gate, w_up, hid, blocks, middle, cot, gain, g_gate, g_up):
    rows, width = middle.shape
    dma = pltpu.SemaphoreType.DMA
    block = g_gate.shape[1:]
    return pl.pallas_call(
        functools.partial(back_kernel, seq, fsdp),
        out_shape=(
            shape((rows, width), F32),
            shape((seq, rows, width), BF16),
            shape((1, width), F32),
            shape((seq, rows, width), BF16),
            shape(block, F32),
            shape(block, F32),
        ),
        in_specs=[VMEM] * 11,
        out_specs=(VMEM,) * 6,
        scratch_shapes=scatter_scratch(seq, rows, width)[:3]
        + [pltpu.VMEM((hid.shape[1], width), BF16)]
        + [dma((n_copies(seq),))] * 4
        + reduce_scratch(fsdp, *block) * 2,
        compiler_params=params(3),
        name="back",
    )(d_gate, d_up, w_gate, w_up, hid, blocks, middle, cot, gain, g_gate, g_up)


def attend_back_kernel(
    seq, fsdp, d_low, w_out, attn, packed, lse, ids_col, ids_row, cosine, sine, out_terms, middle,
    normed, g_down, d_packed, output, g_qkv, own_down, own_out, held, stage, got, d_attn, d_keys,
    d_vals, g_out, *rest
):
    sems = rest[:2]
    size = len(reduce_scratch(fsdp, 16, 128))
    lines = [
        LineReduce(fsdp, g_down, *rest[2 : 2 + size]),
        LineReduce(fsdp, g_out, *rest[2 + size :]),
    ]
    length = d_low.shape[0]
    rows_own = middle.shape[0]
    groups = packed.shape[0] // 4
    ratio = fsdp // seq
    height, width = g_out.shape[1:]
    me = lax.axis_index("seq")
    meet(seq, fsdp)
    lines[0].start()
    sums = Scatter(seq, held, stage, got, sems[:2])

    def term(device, ref):
        ref[...] = out_terms[device]

    sums.send(term, [lines[0].pairs])

    def outer(at):
        rows = pl.ds(at, 512)
        d_attn[rows, :] = dot_nt(d_low[rows, :], w_out[...]).astype(BF16)

    each(length, 512, outer)
    for across in range(seq):
        part = dot_tn(attn[...], d_low[:, across * width : (across + 1) * width]).astype(BF16)
        for down in range(ratio):
            g_out[down * seq + across] = part[down * height : (down + 1) * height]
    lines[1].start()
    sums.forward()
    d_keys[...] = jnp.zeros_like(d_keys)
    d_vals[...] = jnp.zeros_like(d_vals)
    for start in range(0, length, BLOCK):
        low, high = key_range(start, length)
        rows = pl.ds(start, BLOCK)
        keys = pl.ds(low, high - low)
        bias = mask_bias(ids_col, ids_row, start, low, high)
        for group in range(groups):
            base = group * 2 * HEAD_DIM
            queries = jnp.concatenate(
                [packed[group * 4, rows, :], packed[group * 4 + 1, rows, :]], axis=0
            )
            mixed = attn[rows, base : base + 2 * HEAD_DIM].astype(F32)
            d_wide = d_attn[rows, base : base + 2 * HEAD_DIM]
            product = mixed * d_wide.astype(F32)
            delta = jnp.concatenate(
                [
                    jnp.sum(product[:, :HEAD_DIM], axis=-1, keepdims=True),
                    jnp.sum(product[:, HEAD_DIM:], axis=-1, keepdims=True),
                ],
                axis=0,
            )
            d_out = jnp.concatenate([d_wide[:, :HEAD_DIM], d_wide[:, HEAD_DIM:]], axis=0)
            logs = jnp.concatenate(
                [
                    lse[rows, group * 2 : group * 2 + 1],
                    lse[rows, group * 2 + 1 : group * 2 + 2],
                ],
                axis=0,
            )
            key_rows = packed[group * 4 + 2, keys, :]
            scores = dot_nt(queries, key_rows) * SCALE + bias
            probs = jnp.exp(scores - logs)
            d_probs = dot_nt(d_out, packed[group * 4 + 3, keys, :])
            d_scores = (probs * (d_probs - delta)).astype(BF16)
            d_vals[group, keys, :] += dot_tn(probs.astype(BF16), d_out)
            d_keys[group, keys, :] += dot_tn(d_scores, queries) * SCALE
            d_query = dot(d_scores, key_rows) * SCALE
            turned = [
                part * cosine[rows, :] - swap_halves(part) * sine[rows, :]
                for part in (d_query[:BLOCK], d_query[BLOCK:])
            ]
            d_packed[rows, group * 4 * HEAD_DIM : group * 4 * HEAD_DIM + 2 * HEAD_DIM] = (
                jnp.concatenate(turned, axis=1).astype(BF16)
            )
        if start == 0:
            lines[1].pairs()
        if start == BLOCK:
            lines[0].forward()
        if start == 2 * BLOCK:
            lines[1].forward()

    def last(at):
        rows = pl.ds(at, BLOCK)
        for group in range(groups):
            d_key = d_keys[group, rows, :]
            turned = d_key * cosine[rows, :] - swap_halves(d_key) * sine[rows, :]
            base = group * 4 * HEAD_DIM + 2 * HEAD_DIM
            d_packed[rows, base : base + 2 * HEAD_DIM] = jnp.concatenate(
                [turned, d_vals[group, rows, :]], axis=1
            ).astype(BF16)

    each(length, BLOCK, last)
    tall = tile_of(normed.shape[1], 512)

    def weight(at):
        part = pl.ds(at, tall)
        g_qkv[part, :] = dot_tn(normed[:, part], d_packed[...]).astype(BF16)

    each(normed.shape[1], tall, weight)
    sums.finish()

    def total(at):
        part = pl.ds(at, 128)
        output[part, :] = middle[part, :] + out_terms[me, part, :].astype(F32) + sums.terms(part)

    each(rows_own, 128, total)
    lines[0].finish(own_down)
    lines[1].finish(own_out)


def attend_back(
    seq, fsdp, d_low_all, w_out, attn, packed, lse, ids_col, ids_row, cosine, sine, out_terms,
    middle, normed, g_down
):
    rows, width = middle.shape
    length = d_low_all.shape[0]
    inner = attn.shape[1]
    groups = packed.shape[0] // 4
    height = inner // (fsdp // seq)
    return pl.pallas_call(
        functools.partial(attend_back_kernel, seq, fsdp),
        out_shape=(
            shape((length, groups * 4 * HEAD_DIM), BF16),
            shape((rows, width), F32),
            shape((width, groups * 4 * HEAD_DIM), BF16),
            shape(g_down.shape[1:], BF16),
            shape((height, width // seq), BF16),
        ),
        in_specs=[VMEM] * 13,
        out_specs=(VMEM,) * 5,
        scratch_shapes=scatter_scratch(seq, rows, width)[:3]
        + [pltpu.VMEM((length, inner), BF16)]
        + [pltpu.VMEM((groups, length, HEAD_DIM), F32)] * 2
        + [pltpu.VMEM((fsdp, height, width // seq), BF16)]
        + [pltpu.SemaphoreType.DMA((n_copies(seq),))] * 2
        + reduce_scratch(fsdp, *g_down.shape[1:])
        + reduce_scratch(fsdp, height, width // seq),
        compiler_params=params(4),
        name="attend_back",
    )(
        d_low_all, w_out, attn, packed, lse, ids_col, ids_row, cosine, sine, out_terms, middle,
        normed, g_down,
    )


def leave_kernel(
    seq, fsdp, d_packed, w_qkv, hidden, d_middle, gain, gain_two, g_qkv, own_down, own_out,
    d_input, own_qkv, g_down, g_out, g_gain_one, g_gain_two, held, stage, got, home_down, home_out,
    parts, seq_parts, sums_own, fsdp_parts, *rest
):
    sems, part_sems, move_sems = rest[:2], rest[2:6], rest[6:9]
    line = LineReduce(fsdp, g_qkv, *rest[9:])
    rows, width = hidden.shape
    me, row = lax.axis_index("seq"), lax.axis_index("fsdp")
    tile = tile_of(width, 512)
    source, to = row_owner(seq, fsdp)
    meet(seq, fsdp, (to, source))
    line.start()
    moves = [
        Move(own_down, home_down, to, move_sems, 0),
        Move(own_out, home_out, to, move_sems, 1),
    ]
    for move in moves:
        move.start()
    sums = Scatter(seq, held, stage, got, sems)

    def one(device, at):
        block = pl.ds(pl.multiple_of(device * rows, rows), rows)
        return dot_nt(d_packed[block, :], w_qkv[pl.ds(at, tile), :])

    def term(device, ref):
        def part(at):
            ref[:, pl.ds(at, tile)] = one(device, at).astype(BF16)

        each(width, tile, part)

    sums.send(term, [line.pairs])

    def own(at):
        d_input[:, pl.ds(at, tile)] = one(me, at)

    each(width, tile, own)
    sums.forward()
    line.forward()
    for move in moves:
        move.finish()
    g_down[...] = home_down[...].astype(F32)
    g_out[...] = home_out[...].astype(F32)
    parts[0:1, :] = jnp.zeros((1, width), F32)
    parts[1:2, :] = gain_two[...]
    sums.finish()

    def norm(at):
        part = pl.ds(at, 128)
        values = hidden[part, :].astype(F32)
        grad = d_input[part, :] + sums.terms(part)
        scale = lax.rsqrt(jnp.mean(values * values, axis=-1, keepdims=True) + EPSILON)
        weighted = grad * gain[0:1, :]
        inner = jnp.mean(weighted * values, axis=-1, keepdims=True)
        parts[0:1, :] += jnp.sum(grad * values * scale, axis=0, keepdims=True)
        d_input[part, :] = d_middle[part, :] + scale * (
            weighted - values * (scale * scale) * inner
        )

    each(rows, 128, norm)
    first = [
        push(parts, seq_parts.at[k], part_sems[:2], k, peer)
        for k, peer in enumerate(others(seq))
    ]
    for copy in first:
        copy.start()
    line.finish(own_qkv)
    for copy in first:
        copy.wait()
    total = parts[...]
    for k in range(seq - 1):
        total = total + seq_parts[k]
    sums_own[...] = total
    second = [
        push(
            sums_own,
            fsdp_parts.at[step - 1],
            part_sems[2:],
            step - 1,
            lax.rem(row + step, fsdp),
            "fsdp",
        )
        for step in range(1, fsdp)
    ]
    for copy in second:
        copy.start()
    for copy in second:
        copy.wait()
    for step in range(1, fsdp):
        total = total + fsdp_parts[step - 1]
    share = g_gain_one.shape[1]
    turned = pltpu.roll(
        jnp.broadcast_to(total[:, None, :], (2, 8, width)).reshape(16, width),
        lax.rem(width - (row * seq + me) * share, width),
        1,
    )
    g_gain_one[...] = turned[0:1, :share]
    g_gain_two[...] = turned[8:9, :share]


def leave(
    seq, fsdp, d_packed, w_qkv, hidden, d_middle, gain, gain_two, g_qkv, own_down, own_out
):
    rows, width = hidden.shape
    dma = pltpu.SemaphoreType.DMA
    share = width // (seq * fsdp)
    return pl.pallas_call(
        functools.partial(leave_kernel, seq, fsdp),
        out_shape=(
            shape((rows, width), F32),
            shape(g_qkv.shape[1:], F32),
            shape(own_down.shape, F32),
            shape(own_out.shape, F32),
            shape((1, share), F32),
            shape((1, share), F32),
        ),
        in_specs=[VMEM] * 9,
        out_specs=(VMEM,) * 6,
        scratch_shapes=scatter_scratch(seq, rows, width)[:3]
        + [
            pltpu.VMEM(own_down.shape, BF16),
            pltpu.VMEM(own_out.shape, BF16),
            pltpu.VMEM((2, width), F32),
            pltpu.VMEM((seq - 1, 2, width), F32),
            pltpu.VMEM((2, width), F32),
            pltpu.VMEM((fsdp - 1, 2, width), F32),
        ]
        + [dma((n_copies(seq),))] * 2
        + [dma((seq - 1,))] * 2
        + [dma((fsdp - 1,))] * 2
        + [dma((2,))] * 3
        + reduce_scratch(fsdp, *g_qkv.shape[1:]),
        compiler_params=params(5),
        name="leave",
    )(d_packed, w_qkv, hidden, d_middle, gain, gain_two, g_qkv, own_down, own_out)


def body(
    hidden_in, cotangent, segment_ids, w_qkv, w_out, w_gate, w_up, w_down, gain_attn, gain_mlp
):
    rows, width = hidden_in.shape
    fsdp = lax.axis_size("fsdp")
    seq = lax.axis_size("seq")
    length = rows * seq

    normed_one, ids_row, ids_col, cosine, sine, gains, cols_qkv, moved_out, moved_down = enter(
        seq, fsdp, hidden_in, segment_ids, gain_attn.reshape(1, -1), gain_mlp.reshape(1, -1),
        w_qkv, w_out, w_down,
    )
    cols_qkv = cols_qkv.reshape(width, -1)
    packed, attn, lse, cot_all, blocks_out, cols_gate = attend(
        seq, fsdp, normed_one, ids_col, ids_row, cosine, sine, cols_qkv, cotangent, moved_out,
        w_gate,
    )
    cot_all = cot_all.reshape(length, width)
    cols_gate = cols_gate.reshape(width, -1)
    middle, normed_two, rows_out, cols_up, blocks_down = to_middle(
        seq, fsdp, attn, blocks_out, hidden_in, gains, w_up, moved_down
    )
    cols_up = cols_up.reshape(width, -1)
    hid, d_gate, d_up, g_down, g_gate, g_up = feed(
        seq, normed_two.reshape(length, width), cot_all, cols_gate, cols_up, blocks_down
    )
    d_middle, d_low_all, part_two, out_terms, g_gate, g_up = back(
        seq, fsdp, d_gate, d_up, cols_gate, cols_up, hid, blocks_down, middle, cotangent, gains,
        g_gate.reshape((fsdp,) + w_gate.shape), g_up.reshape((fsdp,) + w_up.shape),
    )
    d_packed, output, g_qkv, own_down, own_out = attend_back(
        seq, fsdp, d_low_all.reshape(length, width), rows_out, attn, packed, lse, ids_col, ids_row,
        cosine, sine, out_terms, middle, normed_one, g_down.reshape(blocks_down.shape),
    )
    d_input, g_qkv, g_down, g_out, g_gain_one, g_gain_two = leave(
        seq, fsdp, d_packed, cols_qkv, hidden_in, d_middle, gains, part_two,
        g_qkv.reshape((fsdp,) + w_qkv.shape), own_down, own_out,
    )
    return (
        output, d_input, g_qkv, g_out, g_gate, g_up, g_down, g_gain_one.reshape(-1),
        g_gain_two.reshape(-1),
    )


def solution(mesh):
    both = P(("fsdp", "seq"), None)
    split = P("fsdp", "seq")
    gain = P(("fsdp", "seq"))
    in_specs = (both, both, split, split, split, split, split, split, gain, gain)
    out_specs = (both, both, split, split, split, split, split, gain, gain)
    return jax.shard_map(body, mesh=mesh, in_specs=in_specs, out_specs=out_specs, check_vma=False)
```

```python
import functools
import math

import jax
import jax.numpy as jnp
from jax import lax
from jax.experimental import pallas as pl
from jax.experimental.pallas import tpu as pltpu
from jax.sharding import PartitionSpec as P

HEAD_DIM = 96
EPSILON = 1e-05
ROPE_BASE = 100000.0
NEGATIVE = -1e30
SCALE = 1.0 / math.sqrt(HEAD_DIM)
MESH = pl.DeviceIdType.MESH
BLOCK = 256
F32 = jnp.float32
BF16 = jnp.bfloat16
ANY = pl.BlockSpec(memory_space=pl.ANY)
VMEM = pl.BlockSpec(memory_space=pltpu.VMEM)


def dot(left, right):
    return jnp.dot(left, right, preferred_element_type=F32)


def dot_nt(left, right):
    return lax.dot_general(left, right, (((1,), (1,)), ((), ())), preferred_element_type=F32)


def dot_tn(left, right):
    return lax.dot_general(left, right, (((0,), (0,)), ((), ())), preferred_element_type=F32)


def shape(dims, kind):
    return jax.ShapeDtypeStruct(dims, kind)


def params(collective=None):
    return pltpu.CompilerParams(
        collective_id=collective,
        has_side_effects=collective is not None,
        vmem_limit_bytes=60 << 20,
    )


def cost(flops, moved):
    return pl.CostEstimate(flops=flops, bytes_accessed=moved, transcendentals=0)


def others(size):
    me = lax.axis_index("seq")
    if size == 4:
        low, high = lax.rem(me, 2), me // 2
        return [high * 2 + 1 - low, (1 - high) * 2 + low, (1 - high) * 2 + 1 - low]
    return [lax.rem(me + step, size) for step in range(1, size)]


def meet(seq, fsdp, pairs=(), ends=True):
    barrier = pltpu.get_barrier_semaphore()
    row = lax.axis_index("fsdp")
    for peer in others(seq):
        pl.semaphore_signal(barrier, inc=1, device_id={"seq": peer}, device_id_type=MESH)
    for step in range(1, fsdp):
        peer = lax.rem(row + step, fsdp)
        pl.semaphore_signal(barrier, inc=1, device_id={"fsdp": peer}, device_id_type=MESH)
    for there in pairs:

        @pl.when(away(there))
        def _(there=there):
            pl.semaphore_signal(
                barrier,
                inc=1,
                device_id={"fsdp": there[0], "seq": there[1]},
                device_id_type=MESH,
            )

    if pairs:

        @pl.when(away(pairs[0]))
        def _():
            pl.semaphore_wait(barrier, seq + fsdp - 2 + len(pairs))

        @pl.when(jnp.logical_not(away(pairs[0])))
        def _():
            pl.semaphore_wait(barrier, seq + fsdp - 2)
    elif ends:
        pl.semaphore_wait(barrier, seq + fsdp - 2)


def away(there):
    return jnp.logical_or(
        there[0] != lax.axis_index("fsdp"), there[1] != lax.axis_index("seq")
    )


def row_owner(seq, fsdp):
    row, me = lax.axis_index("fsdp"), lax.axis_index("seq")
    ratio = fsdp // seq
    to = (lax.rem(row, ratio) * seq + me, row // ratio)
    source = (me * ratio + row // seq, lax.rem(row, seq))
    return to, source


def push(src, dst, sems, index, peer, axis="seq", slot=None):
    return pltpu.make_async_remote_copy(
        src_ref=src,
        dst_ref=dst,
        send_sem=sems[0].at[index],
        recv_sem=sems[1].at[index if slot is None else slot],
        device_id={axis: peer},
        device_id_type=MESH,
    )


class Move:
    def __init__(self, src, dst, to, sems, index):
        self.local = pltpu.make_async_copy
        self.src, self.dst, self.to, self.sems, self.index = src, dst, to, sems, index

    def remote(self):
        return pltpu.make_async_remote_copy(
            src_ref=self.src,
            dst_ref=self.dst,
            send_sem=self.sems[0].at[self.index],
            recv_sem=self.sems[1].at[self.index],
            device_id={"fsdp": self.to[0], "seq": self.to[1]},
            device_id_type=MESH,
        )

    def within(self):
        return pltpu.make_async_copy(self.src, self.dst, self.sems[2].at[self.index])

    def start(self):
        @pl.when(away(self.to))
        def _():
            self.remote().start()

        @pl.when(jnp.logical_not(away(self.to)))
        def _():
            self.within().start()

    def finish(self):
        @pl.when(away(self.to))
        def _():
            self.remote().wait()

        @pl.when(jnp.logical_not(away(self.to)))
        def _():
            self.within().wait()


class Home:
    def __init__(self, seq, fsdp, own, mid, out, sems):
        self.seq, self.fsdp, self.ratio = seq, fsdp, fsdp // seq
        self.own, self.mid, self.out, self.sems = own, mid, out, sems
        self.me, self.row = lax.axis_index("seq"), lax.axis_index("fsdp")
        self.stop = lax.rem(self.row, seq)
        self.base = self.row // seq

    def plane_copy(self):
        return push(self.own, self.mid.at[self.me], self.sems, 0, self.stop, "seq", self.me)

    def plane_local(self):
        return pltpu.make_async_copy(self.own, self.mid.at[self.me], self.sems[2].at[0])

    def start_plane(self):
        @pl.when(self.me != self.stop)
        def _():
            self.plane_copy().start()

        @pl.when(self.me == self.stop)
        def _():
            self.plane_local().start()

    def finish_plane(self):
        @pl.when(self.me != self.stop)
        def _():
            self.plane_copy().wait_send()

        @pl.when(self.me == self.stop)
        def _():
            self.plane_local().wait()
            for step in range(1, self.seq):
                peer = lax.rem(self.me + step, self.seq)
                push(self.own, self.mid.at[peer], self.sems, 0, peer, "seq", peer).wait_recv()

    def line_local(self, k):
        return pltpu.make_async_copy(self.mid.at[k], self.out, self.sems[2].at[0])

    def each_line(self, remote, local):
        @pl.when(self.me == self.stop)
        def _():
            for k in range(self.seq):
                row = k * self.ratio + self.base

                @pl.when(row != self.row)
                def _(k=k, row=row):
                    remote(push(self.mid.at[k], self.out, self.sems, k, row, "fsdp", self.seq))

                @pl.when(row == self.row)
                def _(k=k):
                    local(self.line_local(k))

    def start_line(self):
        self.each_line(lambda copy: copy.start(), lambda copy: copy.start())

    def finish_line(self):
        source = lax.rem(self.row, self.ratio) * self.seq + self.me

        @pl.when(source != self.row)
        def _():
            push(self.mid.at[0], self.out, self.sems, 0, source, "fsdp", self.seq).wait_recv()

        self.each_line(lambda copy: copy.wait_send(), lambda copy: copy.wait())


def home_sems(seq):
    dma = pltpu.SemaphoreType.DMA
    return [dma((seq,)), dma((seq + 1,)), dma((1,))]


def chips(row):
    chip, core = row // 2, lax.rem(row, 2)
    pair = chip // 2
    mate = pair * 2 + 1 - lax.rem(chip, 2)
    first = (1 - pair) * 2
    return chip, core, mate, first, first + 1


def inner_chip(chip):
    return jnp.logical_or(chip == 1, chip == 2)


def line_scratch(fsdp):
    dma = pltpu.SemaphoreType.DMA
    return [dma((max(fsdp, 9),)), dma((max(fsdp, 8),)), dma((1,))]


class LineGather:
    def __init__(self, fsdp, own, whole, sems, part=None):
        self.fsdp, self.own, self.whole, self.sems = fsdp, own, whole, sems
        if part is not None:
            self.own, self.whole = own.at[part], whole.at[:, part]
        self.row = lax.axis_index("fsdp")
        if fsdp == 8:
            self.chip, self.core, self.mate, self.one, self.two = chips(self.row)
            self.near = 2 - self.chip // 2

    def at(self, chip):
        return chip * 2 + self.core

    def send(self, slot, index, peer, own=False):
        src = self.own if own else self.whole.at[slot]
        return push(src, self.whole.at[slot], self.sems, index, peer, "fsdp", slot)

    def arrive(self, slot):
        self.send(slot, 0, self.row).wait_recv()

    def local(self):
        return pltpu.make_async_copy(self.own, self.whole.at[self.row], self.sems[2].at[0])

    def sibling(self, chip, index):
        return self.send(self.at(chip), index, self.chip * 2 + 1 - self.core)

    def start(self):
        if self.fsdp != 8:
            for step in range(1, self.fsdp):
                peer = lax.rem(self.row + step, self.fsdp)
                self.send(self.row, step - 1, peer, own=True).start()
        else:
            self.send(self.row, 1, self.at(self.near), own=True).start()
            self.send(self.row, 0, self.at(self.mate), own=True).start()
            self.send(self.row, 2, self.chip * 2 + 1 - self.core, own=True).start()
        self.local().start()

    def pass_on(self, index, chip):
        self.arrive(self.at(chip))

        @pl.when(inner_chip(self.chip))
        def _():
            self.send(self.at(chip), index, self.at(self.mate)).start()

        self.sibling(chip, index + 3).start()

    def forward(self):
        if self.fsdp == 8:

            @pl.when(inner_chip(self.chip))
            def _():
                self.pass_on(3, self.one)
                self.pass_on(4, self.two)

    def finish(self):
        if self.fsdp != 8:
            for step in range(1, self.fsdp):
                self.arrive(lax.rem(self.row - step + self.fsdp, self.fsdp))
            for step in range(1, self.fsdp):
                self.send(self.row, step - 1, self.row, own=True).wait_send()
            self.local().wait()
            return
        self.arrive(self.at(self.mate))
        self.sibling(self.mate, 5).start()

        @pl.when(jnp.logical_not(inner_chip(self.chip)))
        def _():
            self.pass_on(3, self.one)
            self.pass_on(4, self.two)

        for chip in range(4):
            self.arrive(chip * 2 + 1 - self.core)
        self.local().wait()
        for index in range(3):
            self.send(self.row, index, self.row, own=True).wait_send()
        for index, chip in ((5, self.mate), (6, self.one), (7, self.two)):
            self.sibling(chip, index).wait_send()

        @pl.when(inner_chip(self.chip))
        def _():
            self.send(self.at(self.one), 3, self.row).wait_send()
            self.send(self.at(self.two), 4, self.row).wait_send()


def reduce_scratch(fsdp, height, width):
    if fsdp == 8:
        bufs = [pltpu.VMEM((4, height, width), BF16)] * 2
    else:
        bufs = [pltpu.VMEM((1, 16, 128), BF16), pltpu.VMEM((fsdp - 1, height, width), BF16)]
    return bufs + line_scratch(fsdp)


class LineReduce:
    def __init__(self, fsdp, grad, pair, got, *sems):
        self.fsdp, self.grad, self.pair, self.got, self.sems = fsdp, grad, pair, got, sems
        self.row = lax.axis_index("fsdp")
        if fsdp == 8:
            self.chip, self.core, self.mate, self.one, self.two = chips(self.row)
            self.roles = [self.one, self.two, self.mate, self.chip]

    def rows(self, task):
        height = self.grad.shape[1]
        step = 64
        while height % step:
            step //= 2
        each(height, step, lambda at: task(pl.ds(at, step)))

    def across(self, role):
        other = 1 - self.core
        return push(
            self.grad.at[self.roles[role] * 2 + other],
            self.pair.at[role],
            self.sems,
            role,
            self.chip * 2 + other,
            "fsdp",
        )

    def to_mate(self, role):
        slot = (1, 2, 0)[role]
        return push(
            self.pair.at[role],
            self.got.at[slot],
            self.sems,
            4 + slot,
            self.mate * 2 + self.core,
            "fsdp",
        )

    def to_other(self, role):
        return push(
            self.pair.at[role],
            self.got.at[3],
            self.sems,
            7 + role,
            self.roles[role] * 2 + self.core,
            "fsdp",
            7,
        )

    def direct(self, step):
        peer = lax.rem(self.row + step, self.fsdp)
        return push(
            self.grad.at[peer], self.got.at[step - 1], self.sems, step - 1, peer, "fsdp"
        )

    def start(self):
        if self.fsdp != 8:
            for step in range(1, self.fsdp):
                self.direct(step).start()
        else:
            for role in range(4):
                self.across(role).start()

    def pairs(self):
        if self.fsdp != 8:
            return
        for role in range(3):
            self.across(role).wait_recv()
            mine = self.roles[role] * 2 + self.core

            def add(part, role=role, mine=mine):
                self.pair[role, part] = (
                    self.pair[role, part].astype(F32) + self.grad[mine, part].astype(F32)
                ).astype(BF16)

            self.rows(add)
            if role < 2:

                @pl.when(jnp.logical_not(inner_chip(self.chip)))
                def _(role=role):
                    self.to_mate(role).start()
            else:
                self.to_mate(role).start()

    def forward(self, roles=(0, 1)):
        if self.fsdp != 8:
            return

        @pl.when(inner_chip(self.chip))
        def _():
            for role in roles:
                self.to_mate(role).wait_recv()

                def add(part, role=role):
                    self.pair[role, part] = (
                        self.pair[role, part].astype(F32) + self.got[role + 1, part].astype(F32)
                    ).astype(BF16)

                self.rows(add)
                self.to_other(role).start()

    def finish(self, out):
        if self.fsdp != 8:
            for step in range(1, self.fsdp):
                self.direct(step).wait_recv()

            def total(part):
                value = self.grad[self.row, part].astype(F32)
                for step in range(1, self.fsdp):
                    value = value + self.got[step - 1, part].astype(F32)
                out[part, :] = value.astype(out.dtype)

            self.rows(total)
            for step in range(1, self.fsdp):
                self.direct(step).wait_send()
            return
        self.across(3).wait_recv()
        self.to_mate(2).wait_recv()
        self.to_other(0).wait_recv()

        def total(part):
            out[part, :] = (
                self.grad[self.row, part].astype(F32)
                + self.pair[3, part].astype(F32)
                + self.got[0, part].astype(F32)
                + self.got[3, part].astype(F32)
            ).astype(out.dtype)

        self.rows(total)
        for role in range(4):
            self.across(role).wait_send()
        self.to_mate(2).wait_send()

        @pl.when(inner_chip(self.chip))
        def _():
            self.to_other(0).wait_send()
            self.to_other(1).wait_send()

        @pl.when(jnp.logical_not(inner_chip(self.chip)))
        def _():
            self.to_mate(0).wait_send()
            self.to_mate(1).wait_send()


def n_copies(size):
    return 6 if size == 4 else size - 1


class Gather:
    def __init__(self, size, own, whole, sems):
        self.size, self.own, self.whole, self.sems = size, own, whole, sems
        self.me = lax.axis_index("seq")
        self.peers = others(size)
        half = own.shape[0] // 2
        self.parts = [pl.ds(0, half), pl.ds(half, half)]

    def copy(self, index):
        me, own, whole, sems = self.me, self.own, self.whole, self.sems
        if self.size != 4:
            return push(own, whole.at[me], sems, index, self.peers[index])
        side, over, _ = self.peers
        one, two = self.parts
        src, dst, peer = [
            (own.at[one], whole.at[me, one], side),
            (own.at[two], whole.at[me, two], side),
            (own.at[two], whole.at[me, two], over),
            (own.at[one], whole.at[me, one], over),
            (whole.at[side, one], whole.at[side, one], over),
            (whole.at[over, two], whole.at[over, two], side),
        ][index]
        return push(src, dst, sems, index, peer)

    def start(self):
        for index in (0, 2, 1, 3) if self.size == 4 else range(self.size - 1):
            self.copy(index).start()

    def forward(self):
        if self.size == 4:
            for index in (0, 2):
                self.copy(index).wait_recv()
            self.copy(4).start()
            self.copy(5).start()

    def finish(self, task=None):
        if self.size == 4:
            order = [(self.peers[0], (1,)), (self.peers[1], (3,)), (self.peers[2], (4, 5))]
        else:
            order = [
                (lax.rem(self.me - k - 1 + self.size, self.size), (k,))
                for k in range(self.size - 1)
            ]
        for device, parts in order:
            for index in parts:
                self.copy(index).wait_recv()
            if task is not None:
                task(device)
        for index in range(n_copies(self.size)):
            self.copy(index).wait_send()


def scatter_scratch(size, rows, width):
    small = size == 4
    return [
        pltpu.VMEM((size, rows, width), BF16),
        pltpu.VMEM((2, rows // 2, width) if small else (1, 16, 128), BF16),
        pltpu.VMEM((2 if small else size - 1, rows, width), BF16),
    ] + [pltpu.SemaphoreType.DMA((n_copies(size),))] * 2


class Scatter:
    def __init__(self, size, held, stage, got, sems):
        self.size, self.held, self.stage, self.got, self.sems = size, held, stage, got, sems
        self.me = lax.axis_index("seq")
        self.peers = others(size)
        half = held.shape[1] // 2
        self.parts = [pl.ds(0, half), pl.ds(half, half)]

    def copy(self, index):
        held, stage, got, sems = self.held, self.stage, self.got, self.sems
        if self.size != 4:
            peer = self.peers[index]
            return push(held.at[peer], got.at[index], sems, index, peer)
        side, over, far = self.peers
        one, two = self.parts
        src, dst, peer = [
            (held.at[far, one], stage.at[0], side),
            (held.at[far, two], stage.at[1], over),
            (held.at[side, one], got.at[0, one], side),
            (held.at[over, two], got.at[1, two], over),
            (held.at[side, two], got.at[0, two], side),
            (held.at[over, one], got.at[1, one], over),
        ][index]
        return push(src, dst, sems, index, peer)

    def sends(self):
        if self.size == 4:
            return [(2, (0, 1)), (0, (2,)), (1, (3,))]
        return [(k, (k,)) for k in range(self.size - 1)]

    def ready(self, device):
        for place, indices in self.sends():

            @pl.when(self.peers[place] == device)
            def _(indices=indices):
                for index in indices:
                    self.copy(index).start()

    def send(self, make, hooks=()):
        hooks = list(hooks)
        for place, indices in self.sends():
            make(self.peers[place], self.held.at[self.peers[place]])
            for index in indices:
                self.copy(index).start()
            run_hook(hooks)
        while hooks:
            run_hook(hooks)

    def forward(self):
        if self.size == 4:
            side, over, _ = self.peers
            one, two = self.parts
            held, stage = self.held, self.stage
            self.copy(1).wait_recv()
            held[side, two] = (held[side, two].astype(F32) + stage[1].astype(F32)).astype(BF16)
            self.copy(4).start()
            self.copy(0).wait_recv()
            held[over, one] = (held[over, one].astype(F32) + stage[0].astype(F32)).astype(BF16)
            self.copy(5).start()

    def finish(self):
        for index in range(n_copies(self.size)):
            if self.size != 4 or index > 1:
                self.copy(index).wait_recv()
        for index in range(n_copies(self.size)):
            self.copy(index).wait_send()

    def terms(self, rows):
        total = self.got[0, rows].astype(F32)
        for k in range(1, self.got.shape[0]):
            total = total + self.got[k, rows].astype(F32)
        return total


def run_hook(hooks):
    if hooks:
        hook = hooks.pop(0)
        if hook is not None:
            hook()


def each(count, step, task):
    def run(index, carry):
        task(pl.multiple_of(index * step, step))
        return carry

    lax.fori_loop(0, count // step, run, 0)


class Load:
    def __init__(self, src, dst, sem):
        self.dst, self.waited = dst, False
        self.copy = pltpu.make_async_copy(src, dst, sem)
        self.copy.start()

    def get(self):
        if not self.waited:
            self.waited = True
            self.copy.wait()
        return self.dst


def loads(srcs, dsts, sems):
    return [Load(src, dst, sems.at[k]) for k, (src, dst) in enumerate(zip(srcs, dsts))]


def load_scratch(arrays):
    return [pltpu.VMEM(array.shape, array.dtype) for array in arrays] + [
        pltpu.SemaphoreType.DMA((len(arrays),))
    ]


def tile_of(width, most):
    tile = most
    while width % tile:
        tile //= 2
    return tile


def swap_halves(block):
    half = HEAD_DIM // 2
    return jnp.concatenate([block[:, half:], block[:, :half]], axis=1)


def inv_rms(values):
    return lax.rsqrt(jnp.mean(values * values, axis=-1, keepdims=True) + EPSILON)


def mask_bias(ids_col, ids_row, start, low, span):
    query = start + lax.broadcasted_iota(jnp.int32, (BLOCK, span), 0)
    key = low + lax.broadcasted_iota(jnp.int32, (BLOCK, span), 1)
    same = ids_col[pl.ds(start, BLOCK), :] == ids_row[:, pl.ds(low, span)]
    bias = jnp.where(jnp.logical_and(same, key <= query), 0.0, NEGATIVE)
    return jnp.concatenate([bias, bias], axis=0)


def join_blocks(blocks, seq, whole):
    ratio = blocks.shape[0] // seq
    height, width = blocks.shape[1:]
    for down in range(ratio):
        for across in range(seq):
            whole[down * height : (down + 1) * height, across * width : (across + 1) * width] = (
                blocks[down * seq + across]
            )


def forward_kernel(
    seq, fsdp, hidden, w_qkv, w_out, w_gate, w_up, w_down, cot, ids, gain_one, gain_two, normed,
    ids_row, ids_col, cosine, sine, gains, packed, attn, lse, middle, own_normed, rows_out,
    cols_qkv, cols_gate, cols_up, moved_out, moved_down, cot_all, raw, ids_all, gain_own,
    gain_parts, blocks_out, held, stage, got, *sems
):
    def take(count):
        nonlocal sems
        taken, sems = sems[:count], sems[count:]
        return taken

    rows, width = hidden.shape
    length = rows * seq
    groups = w_qkv.shape[1] // (4 * HEAD_DIM)
    me, row = lax.axis_index("seq"), lax.axis_index("fsdp")
    to, source = row_owner(seq, fsdp)
    share = gain_one.shape[1]
    tile = tile_of(width, 512)
    gain_own[0:1, :] = gain_one[...].astype(F32)
    gain_own[1:2, :] = gain_two[...].astype(F32)
    gain_parts[row, me] = gain_own[...]
    ids_all[me] = ids[...]
    meet(seq, fsdp, (to, source))
    local = take(1)[0]
    whole = Gather(seq, hidden, raw, take(2))
    cots = Gather(seq, cot, cot_all, take(2))
    sums = Scatter(seq, held, stage, got, take(2))
    half = w_gate.shape[0] // 2
    one, two = pl.ds(0, half), pl.ds(half, half)
    line_qkv = LineGather(fsdp, w_qkv, cols_qkv, take(3))
    line_out = LineGather(fsdp, moved_out, blocks_out, take(3))
    line_gate = [
        LineGather(fsdp, w_gate, cols_gate, take(3), part) for part in (one, two)
    ]
    line_up = [LineGather(fsdp, w_up, cols_up, take(3), part) for part in (one, two)]
    move_out = Move(w_out, moved_out, to, take(3), 0)
    move_down = Move(w_down, moved_down, to, take(3), 0)
    id_sems, gain_sems, wide_sems = take(2), take(2), take(2)
    id_copies = [
        push(ids, ids_all.at[me], id_sems, k, peer) for k, peer in enumerate(others(seq))
    ]
    gain_copies = [
        push(gain_own, gain_parts.at[row, me], gain_sems, k, peer)
        for k, peer in enumerate(others(seq))
    ]
    for copy in id_copies + gain_copies:
        copy.start()
    line_qkv.start()
    whole.start()
    move_out.start()
    mine = pltpu.make_async_copy(hidden, raw.at[me], local.at[0])
    mine.start()
    for copy in gain_copies:
        copy.wait()
    wide = [
        push(
            gain_parts.at[row],
            gain_parts.at[row],
            wide_sems,
            step - 1,
            lax.rem(row + step, fsdp),
            "fsdp",
        )
        for step in range(1, fsdp)
    ]
    for copy in wide:
        copy.start()
    for copy in id_copies:
        copy.wait()
    for k in range(seq):
        for at in range(0, rows, 128):
            piece = ids_all[k, :, at : at + 128]
            ids_row[:, k * rows + at : k * rows + at + 128] = piece
            turned = jnp.transpose(jnp.broadcast_to(piece, (128, 128)))
            ids_col[k * rows + at : k * rows + at + 128, :] = turned[:, :1]
    order = lax.broadcasted_iota(jnp.int32, (1, HEAD_DIM // 2), 1).astype(F32)
    inverse = jnp.exp(order * (-2.0 * math.log(ROPE_BASE) / HEAD_DIM))

    def table(at):
        part = pl.ds(at, BLOCK)
        first = jnp.sum(
            (ids_row[...] < ids_col[part, :]).astype(jnp.int32).astype(F32),
            axis=-1,
            keepdims=True,
        )
        place = (at + lax.broadcasted_iota(jnp.int32, (BLOCK, 1), 0)).astype(F32) - first
        angles = place * inverse
        cos, sin = jnp.cos(angles), jnp.sin(angles)
        cosine[part, :] = jnp.concatenate([cos, cos], axis=1)
        sine[part, :] = jnp.concatenate([-sin, sin], axis=1)

    each(length, BLOCK, table)
    for copy in wide:
        copy.wait()
    for r in range(fsdp):
        for k in range(seq):
            at = (r * seq + k) * share
            gains[:, at : at + share] = gain_parts[r, k]
    whole.forward()
    line_qkv.forward()
    mine.wait()

    def norm(device):
        base = pl.multiple_of(device * rows, rows)

        def part(at):
            values = raw[device, pl.ds(at, 128), :].astype(F32)
            normed[pl.ds(base + at, 128), :] = (
                values * inv_rms(values) * gains[0:1, :]
            ).astype(BF16)

        each(rows, 128, part)

    norm(me)
    move_out.finish()
    line_out.start()
    for line in line_gate:
        line.start()
    whole.finish(norm)
    cots.start()
    kept = pltpu.make_async_copy(cot, cot_all.at[me], local.at[0])
    kept.start()
    move_down.start()
    line_qkv.finish()
    for group in range(groups):

        def project(at, group=group):
            part = pl.ds(at, 512)
            low = group * 4 * HEAD_DIM
            weight = cols_qkv[:, :, low : low + 4 * HEAD_DIM].reshape(width, 4 * HEAD_DIM)
            proj = dot(normed[part, :], weight)
            for slot in range(4):
                piece = proj[:, slot * HEAD_DIM : (slot + 1) * HEAD_DIM]
                if slot < 3:
                    piece = piece * cosine[part, :] + swap_halves(piece) * sine[part, :]
                packed[group * 4 + slot, part, :] = piece.astype(BF16)

        each(length, 512, project)
    line_out.forward()
    hooks = [
        line_gate[0].forward,
        cots.forward,
        line_out.finish,
        line_gate[1].forward,
        line_up[0].start,
        line_up[1].start,
        None,
        line_up[0].forward,
    ]
    for index in range(seq):
        start = index * BLOCK
        low = max(0, start - length // 2)
        span = start + BLOCK - low
        part, keys = pl.ds(start, BLOCK), pl.ds(low, span)
        bias = mask_bias(ids_col, ids_row, start, low, span)
        mixed, logs = [], []
        for group in range(groups):
            queries = jnp.concatenate(
                [packed[group * 4, part, :], packed[group * 4 + 1, part, :]], axis=0
            )
            scores = dot_nt(queries, packed[group * 4 + 2, keys, :]) * SCALE + bias
            most = jnp.max(scores, axis=-1, keepdims=True)
            grown = jnp.exp(scores - most)
            total = jnp.sum(grown, axis=-1, keepdims=True)
            weights = (grown * (1.0 / total)).astype(BF16)
            out = dot(weights, packed[group * 4 + 3, keys, :])
            log_total = most + jnp.log(total)
            mixed += [out[:BLOCK], out[BLOCK:]]
            logs += [log_total[:BLOCK], log_total[BLOCK:]]
            if index:
                run_hook(hooks)
        attn[part, :] = jnp.concatenate(mixed, axis=1).astype(BF16)
        lane = lax.broadcasted_iota(jnp.int32, (BLOCK, 128), 1)
        stats = jnp.zeros((BLOCK, 128), F32)
        for head, log_total in enumerate(logs):
            stats = jnp.where(lane == head, log_total, stats)
        lse[part, :] = stats
        if index == 0:
            run_hook(hooks)
            run_hook(hooks)
            run_hook(hooks)
            join_blocks(blocks_out, seq, rows_out)

        def onward(at, part=part, index=index):
            cols = pl.ds(at, tile)
            term = dot(attn[part, :], rows_out[:, cols])

            @pl.when(me == index)
            def _():
                middle[:, cols] = raw[me, :, cols].astype(F32) + term

            @pl.when(me != index)
            def _():
                held[index, :, cols] = term.astype(BF16)

        each(width, tile, onward)
        sums.ready(index)
    while hooks:
        run_hook(hooks)
    sums.forward()
    cots.finish()
    kept.wait()
    line_gate[0].finish()
    line_gate[1].finish()
    line_up[1].forward()
    sums.finish()

    def second(at):
        part = pl.ds(at, 128)
        values = middle[part, :] + sums.terms(part)
        middle[part, :] = values
        own_normed[part, :] = (values * inv_rms(values) * gains[1:2, :]).astype(BF16)

    each(rows, 128, second)
    line_up[0].finish()
    line_up[1].finish()
    move_down.finish()


def forward(seq, fsdp, hidden, w_qkv, w_out, w_gate, w_up, w_down, cot, ids, gain_one, gain_two):
    rows, width = hidden.shape
    length = rows * seq
    dma = pltpu.SemaphoreType.DMA
    share = gain_one.shape[1]
    groups = w_qkv.shape[1] // (4 * HEAD_DIM)
    inner = groups * 2 * HEAD_DIM
    return pl.pallas_call(
        functools.partial(forward_kernel, seq, fsdp),
        out_shape=(
            shape((length, width), BF16),
            shape((1, length), jnp.int32),
            shape((length, 1), jnp.int32),
            shape((length, HEAD_DIM), F32),
            shape((length, HEAD_DIM), F32),
            shape((2, width), F32),
            shape((groups * 4, length, HEAD_DIM), BF16),
            shape((length, inner), BF16),
            shape((length, 128), F32),
            shape((rows, width), F32),
            shape((rows, width), BF16),
            shape((inner, width), BF16),
            shape((fsdp,) + w_qkv.shape, BF16),
            shape((fsdp,) + w_gate.shape, BF16),
            shape((fsdp,) + w_up.shape, BF16),
            shape(w_out.shape, BF16),
            shape(w_down.shape, BF16),
            shape((seq, rows, width), BF16),
        ),
        in_specs=[ANY] * 7 + [VMEM] * 3,
        out_specs=(VMEM,) * 13 + (ANY,) * 5,
        scratch_shapes=[
            pltpu.VMEM((seq, rows, width), BF16),
            pltpu.VMEM((seq, 1, rows), jnp.int32),
            pltpu.VMEM((2, share), F32),
            pltpu.VMEM((fsdp, seq, 2, share), F32),
            pltpu.VMEM((fsdp,) + w_out.shape, BF16),
        ]
        + scatter_scratch(seq, rows, width)[:3]
        + [dma((1,))]
        + [dma((n_copies(seq),))] * 6
        + line_scratch(fsdp) * 6
        + [dma((1,))] * 6
        + [dma((seq - 1,))] * 4
        + [dma((fsdp - 1,))] * 2,
        compiler_params=params(0),
        name="forward",
    )(hidden, w_qkv, w_out, w_gate, w_up, w_down, cot, ids, gain_one, gain_two)


def feed_kernel(
    seq, fsdp, own_normed, cot_all, w_gate, w_up, middle, w_down, gains, d_middle, own_low, d_gain,
    own_down, out_terms, g_gate, g_up, normed, whole_down, blocks, gate, up, hid, d_gate, d_up,
    held, stage, got, grad_tiles, out_tiles, *rest
):
    arrays, rest = rest[:5], rest[5:]
    rows, width = middle.shape
    length = rows * seq
    inner = gate.shape[1]
    me = lax.axis_index("seq")
    tile = tile_of(width, 512)
    wide = tile_of(inner, 512)
    w_gate, w_up, cot, middle = loads((w_gate, w_up, cot_all, middle), arrays[:4], arrays[4])
    meet(seq, fsdp)
    local, tile_sems = rest[0], rest[1]
    whole = Gather(seq, own_normed, normed, rest[2:4])
    sums = Scatter(seq, held, stage, got, rest[4:6])
    half = w_down.shape[0] // 2
    line_down = [
        LineGather(fsdp, w_down, blocks, rest[6:9], pl.ds(0, half)),
        LineGather(fsdp, w_down, blocks, rest[9:12], pl.ds(half, half)),
    ]
    line = LineReduce(fsdp, blocks, *rest[12:])
    for exchange in line_down:
        exchange.start()
    whole.start()
    mine = pltpu.make_async_copy(own_normed, normed.at[me], local.at[0])
    mine.start()
    w_gate, w_up = w_gate.get(), w_up.get()
    mine.wait()

    def block_of(device):
        return pl.ds(pl.multiple_of(device * rows, rows), rows)

    def first(device):
        block = block_of(device)

        def part(at):
            cols = pl.ds(at, wide)
            gate_part = dot(normed[device], w_gate[:, cols])
            up_part = dot(normed[device], w_up[:, cols])
            gate[block, cols] = gate_part
            up[block, cols] = up_part
            hid[block, cols] = (gate_part / (1.0 + jnp.exp(-gate_part)) * up_part).astype(BF16)

        each(inner, wide, part)

    first(me)
    whole.forward()
    hooks = [line_down[0].forward, line_down[1].forward]

    def arrived(device):
        first(device)
        run_hook(hooks)

    whole.finish(arrived)
    while hooks:
        run_hook(hooks)
    cot, middle = cot.get(), middle.get()
    for exchange in line_down:
        exchange.finish()
    join_blocks(blocks, seq, whole_down)

    def second(device, out):
        block = block_of(device)

        def part(at):
            cols = pl.ds(at, wide)
            d_hid = dot_nt(cot[block, :], whole_down[cols, :])
            gate_part = gate[block, cols]
            sig = 1.0 / (1.0 + jnp.exp(-gate_part))
            d_gate[block, cols] = (
                d_hid * up[block, cols] * sig * (1.0 + gate_part * (1.0 - sig))
            ).astype(BF16)
            d_up[block, cols] = (d_hid * (gate_part * sig)).astype(BF16)

        each(inner, wide, part)

        def term(at):
            cols = pl.ds(at, tile)
            total = dot_nt(d_gate[block, :], w_gate[cols, :]) + dot_nt(
                d_up[block, :], w_up[cols, :]
            )
            out[:, cols] = total.astype(out.dtype)

        each(width, tile, term)

    def down_grad():
        height, across = blocks.shape[1:]
        for k in range(seq):
            for down in range(fsdp // seq):
                blocks[down * seq + k] = dot_tn(
                    hid[:, down * height : (down + 1) * height],
                    cot[:, k * across : (k + 1) * across],
                ).astype(BF16)
        line.start()

    sums.send(second, [None, down_grad])
    second(me, d_middle)
    line.pairs()
    sums.forward()

    def tile_out(index, slot, grads):
        at = index * wide_rows
        return pltpu.make_async_copy(
            grad_tiles.at[slot], grads.at[pl.ds(at, wide_rows)], tile_sems.at[slot]
        )

    wide_rows = grad_tiles.shape[1]
    count = width // wide_rows
    done = []
    jobs = [(d_gate, g_gate, k) for k in range(count)] + [(d_up, g_up, k) for k in range(count)]
    for number, (left, grads, index) in enumerate(jobs):
        slot = number % 2
        if number >= 2:
            done[number - 2].wait()
        for k in range(seq):
            spot = slice(index * wide_rows, (index + 1) * wide_rows)
            part = dot_tn(normed[k, :, spot], left[k * rows : (k + 1) * rows, :])
            if k == 0:
                total = part
            else:
                total = total + part
        grad_tiles[slot] = total.astype(BF16)
        done.append(tile_out(index, slot, grads))
        done[-1].start()
        if number == 1:
            line.forward((0,))
        if number == 4:
            line.forward((1,))
    for copy in done[-2:]:
        copy.wait()
    done = []
    for index in range(seq):
        slot = index % 2
        if index >= 2:
            done[index - 2].wait()

        def part(at, index=index, slot=slot):
            cols = pl.ds(at, tile)
            out_tiles[slot, :, cols] = dot(
                hid[index * rows : (index + 1) * rows, :], whole_down[:, cols]
            ).astype(BF16)

        each(width, tile, part)
        done.append(
            pltpu.make_async_copy(out_tiles.at[slot], out_terms.at[index], tile_sems.at[slot])
        )
        done[-1].start()
    for copy in done[-2:]:
        copy.wait()
    sums.finish()
    d_gain[...] = jnp.zeros_like(d_gain)
    base = pl.multiple_of(me * rows, rows)

    def norm(at):
        part = pl.ds(at, 128)
        values = middle[part, :]
        grad = d_middle[part, :] + sums.terms(part)
        scale = inv_rms(values)
        weighted = grad * gains[1:2, :]
        mean = jnp.mean(weighted * values, axis=-1, keepdims=True)
        d_gain[...] += jnp.sum(grad * values * scale, axis=0, keepdims=True)
        total = cot[pl.ds(base + at, 128), :].astype(F32) + scale * (
            weighted - values * (scale * scale) * mean
        )
        d_middle[part, :] = total
        own_low[part, :] = total.astype(BF16)

    each(rows, 128, norm)
    line.finish(own_down)


def feed(seq, fsdp, own_normed, cot_all, w_gate, w_up, middle, w_down, gains):
    rows, width = middle.shape
    length = rows * seq
    inner = w_gate.shape[1]
    dma = pltpu.SemaphoreType.DMA
    return pl.pallas_call(
        functools.partial(feed_kernel, seq, fsdp),
        out_shape=(
            shape((rows, width), F32),
            shape((rows, width), BF16),
            shape((1, width), F32),
            shape(w_down.shape, BF16),
            shape((seq, rows, width), BF16),
            shape((width, inner), BF16),
            shape((width, inner), BF16),
        ),
        in_specs=[ANY] * 6 + [VMEM],
        out_specs=(VMEM,) * 4 + (ANY,) * 3,
        scratch_shapes=[
            pltpu.VMEM((seq, rows, width), BF16),
            pltpu.VMEM((inner, width), BF16),
            pltpu.VMEM((fsdp,) + w_down.shape, BF16),
            pltpu.VMEM((length, inner), F32),
            pltpu.VMEM((length, inner), F32),
            pltpu.VMEM((length, inner), BF16),
            pltpu.VMEM((length, inner), BF16),
            pltpu.VMEM((length, inner), BF16),
        ]
        + scatter_scratch(seq, rows, width)[:3]
        + [pltpu.VMEM((2, min(512, inner // 2), inner), BF16), pltpu.VMEM((2, rows, width), BF16)]
        + load_scratch((w_gate, w_up, cot_all, middle))
        + [dma((1,)), dma((2,))]
        + [dma((n_copies(seq),))] * 4
        + line_scratch(fsdp) * 2
        + reduce_scratch(fsdp, *w_down.shape),
        compiler_params=params(1),
        name="feed",
    )(own_normed, cot_all, w_gate, w_up, middle, w_down, gains)


def attend_back_kernel(
    seq, fsdp, own_low, g_gate, w_out, attn, packed, lse, cosine, sine, out_terms, normed, middle,
    ids_col, ids_row, own_down, d_packed, output, g_qkv, own_gate, own_out, mid_down, held, stage,
    got, d_low, d_keys, d_vals, g_out, *rest
):
    arrays, rest = rest[:9], rest[9:]
    size = len(reduce_scratch(fsdp, 16, 128))
    rows, width = own_low.shape
    length = rows * seq
    groups = packed.shape[0] // 4
    ratio = fsdp // seq
    height, across = g_out.shape[1:]
    tall = tile_of(width, 512)
    local = rest[0]
    g_gate, w_out, attn, packed, lse, cosine, sine, normed = loads(
        (g_gate, w_out, attn, packed, lse, cosine, sine, normed), arrays[:8], arrays[8]
    )
    terms = Load(out_terms, held, local.at[1])
    middle = Load(middle, output, local.at[2])
    me = lax.axis_index("seq")
    meet(seq, fsdp)
    whole = Gather(seq, own_low, d_low, rest[1:3])
    sums = Scatter(seq, held, stage, got, rest[3:5])
    home = Home(seq, fsdp, own_down, mid_down, None, rest[5:8])
    lines = [
        LineReduce(fsdp, g_gate.get(), *rest[8 : 8 + size]),
        LineReduce(fsdp, g_out, *rest[8 + size :]),
    ]
    whole.start()
    mine = pltpu.make_async_copy(own_low, d_low.at[me], local.at[0])
    mine.start()
    lines[0].start()
    w_out, attn, packed, lse = w_out.get(), attn.get(), packed.get(), lse.get()
    cosine, sine = cosine.get(), sine.get()
    d_keys[...] = jnp.zeros_like(d_keys)
    d_vals[...] = jnp.zeros_like(d_vals)
    lines[0].pairs()
    mine.wait()
    span = length // 2 + BLOCK
    hooks = [
        whole.forward,
        functools.partial(lines[0].forward, (0,)),
        None,
        functools.partial(lines[0].forward, (1,)),
    ]

    def attend(device):
        start = pl.multiple_of(device * BLOCK, BLOCK)
        low = pl.multiple_of(jnp.maximum(start - length // 2, 0), BLOCK)
        part, keys = pl.ds(start, BLOCK), pl.ds(low, span)
        d_attn = dot_nt(d_low[device], w_out[...]).astype(BF16)
        bias = mask_bias(ids_col, ids_row, start, low, span)
        for group in range(groups):
            base = group * 2 * HEAD_DIM
            queries = jnp.concatenate(
                [packed[group * 4, part, :], packed[group * 4 + 1, part, :]], axis=0
            )
            d_wide = d_attn[:, base : base + 2 * HEAD_DIM]
            product = attn[part, base : base + 2 * HEAD_DIM].astype(F32) * d_wide.astype(F32)
            delta = jnp.concatenate(
                [
                    jnp.sum(product[:, :HEAD_DIM], axis=-1, keepdims=True),
                    jnp.sum(product[:, HEAD_DIM:], axis=-1, keepdims=True),
                ],
                axis=0,
            )
            d_out = jnp.concatenate([d_wide[:, :HEAD_DIM], d_wide[:, HEAD_DIM:]], axis=0)
            logs = jnp.concatenate(
                [
                    lse[part, group * 2 : group * 2 + 1],
                    lse[part, group * 2 + 1 : group * 2 + 2],
                ],
                axis=0,
            )
            key_rows = packed[group * 4 + 2, keys, :]
            scores = dot_nt(queries, key_rows) * SCALE + bias
            probs = jnp.exp(scores - logs)
            d_probs = dot_nt(d_out, packed[group * 4 + 3, keys, :])
            d_scores = (probs * (d_probs - delta)).astype(BF16)
            d_vals[group, keys, :] += dot_tn(probs.astype(BF16), d_out)
            d_keys[group, keys, :] += dot_tn(d_scores, queries) * SCALE
            d_query = dot(d_scores, key_rows) * SCALE
            turned = [
                piece * cosine[part, :] - swap_halves(piece) * sine[part, :]
                for piece in (d_query[:BLOCK], d_query[BLOCK:])
            ]
            d_packed[part, group * 4 * HEAD_DIM : group * 4 * HEAD_DIM + 2 * HEAD_DIM] = (
                jnp.concatenate(turned, axis=1).astype(BF16)
            )
            run_hook(hooks)

    attend(me)
    whole.finish(attend)
    while hooks:
        run_hook(hooks)
    sums.send(lambda device, ref: terms.get())
    home.start_plane()
    for k in range(seq):
        for index in range(seq):
            part = dot_tn(
                attn[index * rows : (index + 1) * rows, :],
                d_low[index, :, k * across : (k + 1) * across],
            )
            total = part if index == 0 else total + part
        total = total.astype(BF16)
        for down in range(ratio):
            g_out[down * seq + k] = total[down * height : (down + 1) * height]
    lines[1].start()

    def last(at):
        part = pl.ds(at, BLOCK)
        for group in range(groups):
            d_key = d_keys[group, part, :]
            turned = d_key * cosine[part, :] - swap_halves(d_key) * sine[part, :]
            base = group * 4 * HEAD_DIM + 2 * HEAD_DIM
            d_packed[part, base : base + 2 * HEAD_DIM] = jnp.concatenate(
                [turned, d_vals[group, part, :]], axis=1
            ).astype(BF16)

    each(length, BLOCK, last)
    lines[1].pairs()
    normed = normed.get()

    def weight(at):
        part = pl.ds(at, tall)
        g_qkv[part, :] = dot_tn(normed[:, part], d_packed[...]).astype(BF16)

    each(width, tall, weight)
    sums.forward()
    lines[0].finish(own_gate)
    lines[1].forward()
    sums.finish()
    middle.get()

    def total_of(at):
        part = pl.ds(at, 128)
        output[part, :] = output[part, :] + held[me, part, :].astype(F32) + sums.terms(part)

    each(rows, 128, total_of)
    lines[1].finish(own_out)
    home.finish_plane()


def attend_back(
    seq, fsdp, own_low, g_gate, w_out, attn, packed, lse, cosine, sine, out_terms, normed, middle,
    ids_col, ids_row, own_down
):
    rows, width = own_low.shape
    length = rows * seq
    inner = attn.shape[1]
    groups = packed.shape[0] // 4
    height = inner // (fsdp // seq)
    dma = pltpu.SemaphoreType.DMA
    return pl.pallas_call(
        functools.partial(attend_back_kernel, seq, fsdp),
        out_shape=(
            shape((length, groups * 4 * HEAD_DIM), BF16),
            shape((rows, width), F32),
            shape((width, groups * 4 * HEAD_DIM), BF16),
            shape(g_gate.shape[1:], F32),
            shape((height, width // seq), BF16),
            shape((seq,) + own_down.shape, BF16),
        ),
        in_specs=[ANY] * 11 + [VMEM] * 2 + [ANY],
        out_specs=(VMEM,) * 5 + (ANY,),
        scratch_shapes=scatter_scratch(seq, rows, width)[:3]
        + [pltpu.VMEM((seq, rows, width), BF16)]
        + [pltpu.VMEM((groups, length, HEAD_DIM), F32)] * 2
        + [pltpu.VMEM((fsdp, height, width // seq), BF16)]
        + load_scratch((g_gate, w_out, attn, packed, lse, cosine, sine, normed))
        + [dma((3,))]
        + [dma((n_copies(seq),))] * 4
        + home_sems(seq)
        + reduce_scratch(fsdp, *g_gate.shape[1:])
        + reduce_scratch(fsdp, height, width // seq),
        compiler_params=params(2),
        name="attend_back",
    )(
        own_low, g_gate, w_out, attn, packed, lse, cosine, sine, out_terms, normed, middle, ids_col,
        ids_row, own_down,
    )


def leave_kernel(
    seq, fsdp, g_up, g_qkv, d_packed, w_qkv, hidden, d_middle, own_out, mid_down, gain, gain_two,
    d_input, own_qkv, own_up, g_down, g_out, g_gain_one, g_gain_two, held, stage, got, home_down,
    home_out, mid_out, parts, seq_parts, sums_own, fsdp_parts, *rest
):
    arrays, rest = rest[:7], rest[7:]
    size = len(reduce_scratch(fsdp, 16, 128))
    sems, part_sems, homes = rest[:2], rest[2:6], (rest[6:9], rest[9:12])
    rows, width = hidden.shape
    g_up, g_qkv, d_packed, w_qkv, hidden, d_middle = loads(
        (g_up, g_qkv, d_packed, w_qkv, hidden, d_middle), arrays[:6], arrays[6]
    )
    me, row = lax.axis_index("seq"), lax.axis_index("fsdp")
    tile = tile_of(width, 512)
    meet(seq, fsdp)
    lines = [
        LineReduce(fsdp, g_up.get(), *rest[12 : 12 + size]),
        LineReduce(fsdp, g_qkv.get(), *rest[12 + size :]),
    ]
    for line in lines:
        line.start()
    moves = [
        Home(seq, fsdp, None, mid_down, home_down, homes[0]),
        Home(seq, fsdp, own_out, mid_out, home_out, homes[1]),
    ]
    moves[1].start_plane()
    d_packed, w_qkv = d_packed.get(), w_qkv.get()
    sums = Scatter(seq, held, stage, got, sems)

    def one(device, at):
        block = pl.ds(pl.multiple_of(device * rows, rows), rows)
        return dot_nt(d_packed[block, :], w_qkv[pl.ds(at, tile), :])

    def term(device, ref):
        def part(at):
            ref[:, pl.ds(at, tile)] = one(device, at).astype(BF16)

        each(width, tile, part)

    sums.send(term, [lines[0].pairs, lines[1].pairs])
    moves[1].finish_plane()
    for move in moves:
        move.start_line()

    def own(at):
        d_input[:, pl.ds(at, tile)] = one(me, at)

    each(width, tile, own)
    hidden, d_middle = hidden.get(), d_middle.get()
    sums.forward()
    lines[0].forward()
    lines[1].forward()
    for move in moves:
        move.finish_line()
    g_down[...] = home_down[...].astype(F32)
    g_out[...] = home_out[...].astype(F32)
    parts[0:1, :] = jnp.zeros((1, width), F32)
    parts[1:2, :] = gain_two[...]
    sums.finish()

    def norm(at):
        part = pl.ds(at, 128)
        values = hidden[part, :].astype(F32)
        grad = d_input[part, :] + sums.terms(part)
        scale = lax.rsqrt(jnp.mean(values * values, axis=-1, keepdims=True) + EPSILON)
        weighted = grad * gain[0:1, :]
        inner = jnp.mean(weighted * values, axis=-1, keepdims=True)
        parts[0:1, :] += jnp.sum(grad * values * scale, axis=0, keepdims=True)
        d_input[part, :] = d_middle[part, :] + scale * (
            weighted - values * (scale * scale) * inner
        )

    each(rows, 128, norm)
    first = [
        push(parts, seq_parts.at[k], part_sems[:2], k, peer)
        for k, peer in enumerate(others(seq))
    ]
    for copy in first:
        copy.start()
    lines[0].finish(own_up)
    lines[1].finish(own_qkv)
    for copy in first:
        copy.wait()
    total = parts[...]
    for k in range(seq - 1):
        total = total + seq_parts[k]
    sums_own[...] = total
    second = [
        push(
            sums_own,
            fsdp_parts.at[step - 1],
            part_sems[2:],
            step - 1,
            lax.rem(row + step, fsdp),
            "fsdp",
        )
        for step in range(1, fsdp)
    ]
    for copy in second:
        copy.start()
    for copy in second:
        copy.wait()
    for step in range(1, fsdp):
        total = total + fsdp_parts[step - 1]
    share = g_gain_one.shape[1]
    turned = pltpu.roll(
        jnp.broadcast_to(total[:, None, :], (2, 8, width)).reshape(16, width),
        lax.rem(width - (row * seq + me) * share, width),
        1,
    )
    g_gain_one[...] = turned[0:1, :share]
    g_gain_two[...] = turned[8:9, :share]


def leave(
    seq, fsdp, g_up, g_qkv, d_packed, w_qkv, hidden, d_middle, own_out, mid_down, gain, gain_two
):
    rows, width = hidden.shape
    dma = pltpu.SemaphoreType.DMA
    share = width // (seq * fsdp)
    return pl.pallas_call(
        functools.partial(leave_kernel, seq, fsdp),
        out_shape=(
            shape((rows, width), F32),
            shape(g_qkv.shape[1:], F32),
            shape(g_up.shape[1:], F32),
            shape(mid_down.shape[1:], F32),
            shape(own_out.shape, F32),
            shape((1, share), F32),
            shape((1, share), F32),
        ),
        in_specs=[ANY] * 8 + [VMEM] * 2,
        out_specs=(VMEM,) * 7,
        scratch_shapes=scatter_scratch(seq, rows, width)[:3]
        + [
            pltpu.VMEM(mid_down.shape[1:], BF16),
            pltpu.VMEM(own_out.shape, BF16),
            pltpu.VMEM((seq,) + own_out.shape, BF16),
            pltpu.VMEM((2, width), F32),
            pltpu.VMEM((seq - 1, 2, width), F32),
            pltpu.VMEM((2, width), F32),
            pltpu.VMEM((fsdp - 1, 2, width), F32),
        ]
        + load_scratch((g_up, g_qkv, d_packed, w_qkv, hidden, d_middle))
        + [dma((n_copies(seq),))] * 2
        + [dma((seq - 1,))] * 2
        + [dma((fsdp - 1,))] * 2
        + home_sems(seq) * 2
        + reduce_scratch(fsdp, *g_up.shape[1:])
        + reduce_scratch(fsdp, *g_qkv.shape[1:]),
        compiler_params=params(3),
        name="leave",
    )(g_up, g_qkv, d_packed, w_qkv, hidden, d_middle, own_out, mid_down, gain, gain_two)


def body(
    hidden_in, cotangent, segment_ids, w_qkv, w_out, w_gate, w_up, w_down, gain_attn, gain_mlp
):
    rows, width = hidden_in.shape
    fsdp = lax.axis_size("fsdp")
    seq = lax.axis_size("seq")
    length = rows * seq

    (
        normed_one, ids_row, ids_col, cosine, sine, gains, packed, attn, lse, middle, normed_two,
        rows_out, cols_qkv, cols_gate, cols_up, _, moved_down, cot_all,
    ) = forward(
        seq, fsdp, hidden_in, w_qkv, w_out, w_gate, w_up, w_down, cotangent, segment_ids,
        gain_attn.reshape(1, -1), gain_mlp.reshape(1, -1),
    )
    d_middle, own_low, part_two, own_down, out_terms, g_gate, g_up = feed(
        seq, fsdp, normed_two, cot_all.reshape(length, width), cols_gate.reshape(width, -1),
        cols_up.reshape(width, -1), middle, moved_down, gains,
    )
    d_packed, output, g_qkv, g_gate, own_out, mid_down = attend_back(
        seq, fsdp, own_low, g_gate.reshape((fsdp,) + w_gate.shape), rows_out, attn, packed, lse,
        cosine, sine, out_terms, normed_one, middle, ids_col, ids_row, own_down,
    )
    d_input, g_qkv, g_up, g_down, g_out, g_gain_one, g_gain_two = leave(
        seq, fsdp, g_up.reshape((fsdp,) + w_up.shape), g_qkv.reshape((fsdp,) + w_qkv.shape),
        d_packed, cols_qkv.reshape(width, -1), hidden_in, d_middle, own_out, mid_down, gains,
        part_two,
    )
    return (
        output, d_input, g_qkv, g_out, g_gate, g_up, g_down, g_gain_one.reshape(-1),
        g_gain_two.reshape(-1),
    )


def solution(mesh):
    both = P(("fsdp", "seq"), None)
    split = P("fsdp", "seq")
    gain = P(("fsdp", "seq"))
    in_specs = (both, both, split, split, split, split, split, split, gain, gain)
    out_specs = (both, both, split, split, split, split, split, gain, gain)
    return jax.shard_map(body, mesh=mesh, in_specs=in_specs, out_specs=out_specs, check_vma=False)
```

```python
import functools
import math

import jax
import jax.numpy as jnp
from jax import lax
from jax.experimental import pallas as pl
from jax.experimental.pallas import tpu as pltpu
from jax.sharding import PartitionSpec as P

HEAD_DIM = 96
EPSILON = 1e-05
ROPE_BASE = 100000.0
NEGATIVE = -1e30
SCALE = 1.0 / math.sqrt(HEAD_DIM)
MESH = pl.DeviceIdType.MESH
BLOCK = 256
F32 = jnp.float32
BF16 = jnp.bfloat16
ANY = pl.BlockSpec(memory_space=pl.ANY)
VMEM = pl.BlockSpec(memory_space=pltpu.VMEM)


def dot(left, right):
    return jnp.dot(left, right, preferred_element_type=F32)


def dot_nt(left, right):
    return lax.dot_general(left, right, (((1,), (1,)), ((), ())), preferred_element_type=F32)


def dot_tn(left, right):
    return lax.dot_general(left, right, (((0,), (0,)), ((), ())), preferred_element_type=F32)


def shape(dims, kind):
    return jax.ShapeDtypeStruct(dims, kind)


def params(collective=None):
    return pltpu.CompilerParams(
        collective_id=collective,
        has_side_effects=collective is not None,
        vmem_limit_bytes=60 << 20,
    )


def cost(flops, moved):
    return pl.CostEstimate(flops=flops, bytes_accessed=moved, transcendentals=0)


def others(size):
    me = lax.axis_index("seq")
    if size == 4:
        low, high = lax.rem(me, 2), me // 2
        return [high * 2 + 1 - low, (1 - high) * 2 + low, (1 - high) * 2 + 1 - low]
    return [lax.rem(me + step, size) for step in range(1, size)]


def meet(seq, fsdp, pairs=(), ends=True):
    barrier = pltpu.get_barrier_semaphore()
    row = lax.axis_index("fsdp")
    for peer in others(seq):
        pl.semaphore_signal(barrier, inc=1, device_id={"seq": peer}, device_id_type=MESH)
    for step in range(1, fsdp):
        peer = lax.rem(row + step, fsdp)
        pl.semaphore_signal(barrier, inc=1, device_id={"fsdp": peer}, device_id_type=MESH)
    for there in pairs:

        @pl.when(away(there))
        def _(there=there):
            pl.semaphore_signal(
                barrier,
                inc=1,
                device_id={"fsdp": there[0], "seq": there[1]},
                device_id_type=MESH,
            )

    if pairs:

        @pl.when(away(pairs[0]))
        def _():
            pl.semaphore_wait(barrier, seq + fsdp - 2 + len(pairs))

        @pl.when(jnp.logical_not(away(pairs[0])))
        def _():
            pl.semaphore_wait(barrier, seq + fsdp - 2)
    elif ends:
        pl.semaphore_wait(barrier, seq + fsdp - 2)


def away(there):
    return jnp.logical_or(
        there[0] != lax.axis_index("fsdp"), there[1] != lax.axis_index("seq")
    )


def flip(one, two):
    return one + two - 2 * one * two


def turn(chip, core, high):
    return flip(chip // 2, core) * 2 + flip(lax.rem(chip, 2), flip(high, core))


def row_owner(seq, fsdp):
    row, me = lax.axis_index("fsdp"), lax.axis_index("seq")
    if seq == 4 and fsdp == 8:
        chip, core = row // 2, lax.rem(row, 2)
        to = (turn(chip, core, me // 2) * 2 + lax.rem(me, 2), chip)
        first = flip(me // 2, chip // 2)
        high = flip(flip(lax.rem(me, 2), lax.rem(chip, 2)), first)
        return to, (me * 2 + first, high * 2 + core)
    ratio = fsdp // seq
    to = (lax.rem(row, ratio) * seq + me, row // ratio)
    source = (me * ratio + row // seq, lax.rem(row, seq))
    return to, source


def line_place(seq, fsdp, down, across):
    if seq == 4 and fsdp == 8:
        return turn(lax.axis_index("seq"), down, across // 2) * 2 + across % 2
    return down * seq + across


def push(src, dst, sems, index, peer, axis="seq", slot=None):
    return pltpu.make_async_remote_copy(
        src_ref=src,
        dst_ref=dst,
        send_sem=sems[0].at[index],
        recv_sem=sems[1].at[index if slot is None else slot],
        device_id={axis: peer},
        device_id_type=MESH,
    )


class Move:
    def __init__(self, src, dst, to, sems, index):
        self.local = pltpu.make_async_copy
        self.src, self.dst, self.to, self.sems, self.index = src, dst, to, sems, index

    def remote(self):
        return pltpu.make_async_remote_copy(
            src_ref=self.src,
            dst_ref=self.dst,
            send_sem=self.sems[0].at[self.index],
            recv_sem=self.sems[1].at[self.index],
            device_id={"fsdp": self.to[0], "seq": self.to[1]},
            device_id_type=MESH,
        )

    def within(self):
        return pltpu.make_async_copy(self.src, self.dst, self.sems[2].at[self.index])

    def start(self):
        @pl.when(away(self.to))
        def _():
            self.remote().start()

        @pl.when(jnp.logical_not(away(self.to)))
        def _():
            self.within().start()

    def finish(self):
        @pl.when(away(self.to))
        def _():
            self.remote().wait()

        @pl.when(jnp.logical_not(away(self.to)))
        def _():
            self.within().wait()


class Home:
    def __init__(self, seq, fsdp, own, mid, out, sems):
        self.seq, self.fsdp = seq, fsdp
        self.own, self.mid, self.out, self.sems = own, mid, out, sems
        me, row = lax.axis_index("seq"), lax.axis_index("fsdp")
        self.me, self.row = me, row
        owner = row_owner(seq, fsdp)[1]
        self.stop = owner[1]
        if seq == 4 and fsdp == 8:
            chip, core = row // 2, lax.rem(row, 2)
            self.slot = lax.rem(owner[0], 2)
            self.takes = lax.rem(me, 2) == core
            self.items = [(turn(chip, k, me // 2), turn(chip, k, me // 2) * 2 + k) for k in (0, 1)]
            self.origin = turn(chip, core, me // 2) * 2 + lax.rem(me, 2)
        else:
            ratio = fsdp // seq
            self.slot = me
            self.takes = me == lax.rem(row, seq)
            self.items = [(k, k * ratio + row // seq) for k in range(seq)]
            self.origin = lax.rem(row, ratio) * seq + me

    def plane(self):
        return push(self.own, self.mid.at[self.slot], self.sems, 0, self.stop, "seq", self.slot)

    def plane_local(self):
        return pltpu.make_async_copy(self.own, self.mid.at[self.slot], self.sems[2].at[0])

    def start_plane(self):
        @pl.when(self.me != self.stop)
        def _():
            self.plane().start()

        @pl.when(self.me == self.stop)
        def _():
            self.plane_local().start()

    def finish_plane(self):
        @pl.when(self.me != self.stop)
        def _():
            self.plane().wait_send()

        @pl.when(self.me == self.stop)
        def _():
            self.plane_local().wait()

        @pl.when(self.takes)
        def _():
            for k, (column, _) in enumerate(self.items):

                @pl.when(column != self.me)
                def _(k=k, column=column):
                    push(self.own, self.mid.at[k], self.sems, 0, column, "seq", k).wait_recv()

    def line(self, k, row):
        return push(self.mid.at[k], self.out, self.sems, k, row, "fsdp", len(self.items))

    def each_line(self, remote, local):
        @pl.when(self.takes)
        def _():
            for k, (_, row) in enumerate(self.items):

                @pl.when(row != self.row)
                def _(k=k, row=row):
                    remote(self.line(k, row))

                @pl.when(row == self.row)
                def _(k=k):
                    local(pltpu.make_async_copy(self.mid.at[k], self.out, self.sems[2].at[0]))

    def start_line(self):
        self.each_line(lambda copy: copy.start(), lambda copy: copy.start())

    def finish_line(self):
        @pl.when(self.origin != self.row)
        def _():
            self.line(0, self.origin).wait_recv()

        self.each_line(lambda copy: copy.wait_send(), lambda copy: copy.wait())


def home_count(seq, fsdp):
    return 2 if seq == 4 and fsdp == 8 else seq


def home_sems(seq, fsdp):
    dma = pltpu.SemaphoreType.DMA
    count = home_count(seq, fsdp)
    return [dma((count,)), dma((count + 1,)), dma((1,))]


def chips(row):
    chip, core = row // 2, lax.rem(row, 2)
    pair = chip // 2
    mate = pair * 2 + 1 - lax.rem(chip, 2)
    first = (1 - pair) * 2
    return chip, core, mate, first, first + 1


def inner_chip(chip):
    return jnp.logical_or(chip == 1, chip == 2)


def line_scratch(fsdp):
    dma = pltpu.SemaphoreType.DMA
    return [dma((max(fsdp, 9),)), dma((max(fsdp, 8),)), dma((1,))]


class LineGather:
    def __init__(self, fsdp, own, whole, sems, part=None):
        self.fsdp, self.own, self.whole, self.sems = fsdp, own, whole, sems
        if part is not None:
            self.own, self.whole = own.at[part], whole.at[:, part]
        self.row = lax.axis_index("fsdp")
        if fsdp == 8:
            self.chip, self.core, self.mate, self.one, self.two = chips(self.row)
            self.near = 2 - self.chip // 2

    def at(self, chip):
        return chip * 2 + self.core

    def send(self, slot, index, peer, own=False):
        src = self.own if own else self.whole.at[slot]
        return push(src, self.whole.at[slot], self.sems, index, peer, "fsdp", slot)

    def arrive(self, slot):
        self.send(slot, 0, self.row).wait_recv()

    def local(self):
        return pltpu.make_async_copy(self.own, self.whole.at[self.row], self.sems[2].at[0])

    def sibling(self, chip, index):
        return self.send(self.at(chip), index, self.chip * 2 + 1 - self.core)

    def start(self):
        if self.fsdp != 8:
            for step in range(1, self.fsdp):
                peer = lax.rem(self.row + step, self.fsdp)
                self.send(self.row, step - 1, peer, own=True).start()
        else:
            self.send(self.row, 1, self.at(self.near), own=True).start()
            self.send(self.row, 0, self.at(self.mate), own=True).start()
            self.send(self.row, 2, self.chip * 2 + 1 - self.core, own=True).start()
        self.local().start()

    def pass_on(self, index, chip):
        self.arrive(self.at(chip))

        @pl.when(inner_chip(self.chip))
        def _():
            self.send(self.at(chip), index, self.at(self.mate)).start()

        self.sibling(chip, index + 3).start()

    def forward(self):
        if self.fsdp == 8:

            @pl.when(inner_chip(self.chip))
            def _():
                self.pass_on(3, self.one)
                self.pass_on(4, self.two)

    def finish(self):
        if self.fsdp != 8:
            for step in range(1, self.fsdp):
                self.arrive(lax.rem(self.row - step + self.fsdp, self.fsdp))
            for step in range(1, self.fsdp):
                self.send(self.row, step - 1, self.row, own=True).wait_send()
            self.local().wait()
            return
        self.arrive(self.at(self.mate))
        self.sibling(self.mate, 5).start()

        @pl.when(jnp.logical_not(inner_chip(self.chip)))
        def _():
            self.pass_on(3, self.one)
            self.pass_on(4, self.two)

        for chip in range(4):
            self.arrive(chip * 2 + 1 - self.core)
        self.local().wait()
        for index in range(3):
            self.send(self.row, index, self.row, own=True).wait_send()
        for index, chip in ((5, self.mate), (6, self.one), (7, self.two)):
            self.sibling(chip, index).wait_send()

        @pl.when(inner_chip(self.chip))
        def _():
            self.send(self.at(self.one), 3, self.row).wait_send()
            self.send(self.at(self.two), 4, self.row).wait_send()


def mine_scratch(fsdp, height, width):
    count = 4 if fsdp == 8 else 1
    return [pltpu.VMEM((count, height, width), BF16), pltpu.SemaphoreType.DMA((count,))]


def reduce_scratch(fsdp, height, width):
    if fsdp == 8:
        bufs = [pltpu.VMEM((4, height, width), BF16)] * 2
    else:
        bufs = [pltpu.VMEM((1, 16, 128), BF16), pltpu.VMEM((fsdp - 1, height, width), BF16)]
    return bufs + line_scratch(fsdp)


class LineReduce:
    def __init__(self, fsdp, grad, pair, got, *sems, mine=None):
        self.fsdp, self.grad, self.pair, self.got, self.sems = fsdp, grad, pair, got, sems
        self.row = lax.axis_index("fsdp")
        if fsdp == 8:
            self.chip, self.core, self.mate, self.one, self.two = chips(self.row)
            self.roles = [self.one, self.two, self.mate, self.chip]
            self.own = [role * 2 + self.core for role in self.roles]
        else:
            self.own = [self.row]
        self.mine = mine

    def fetch(self, role):
        return pltpu.make_async_copy(
            self.grad.at[self.own[role]], self.mine[0].at[role], self.mine[1].at[role]
        )

    def block(self, role, part):
        if self.mine is not None:
            return self.mine[0][role, part].astype(F32)
        return self.grad[self.own[role], part].astype(F32)

    def ready(self, role):
        if self.mine is not None:
            self.fetch(role).wait()

    def rows(self, task):
        height = self.grad.shape[1]
        step = 64
        while height % step:
            step //= 2
        each(height, step, lambda at: task(pl.ds(at, step)))

    def across(self, role):
        other = 1 - self.core
        return push(
            self.grad.at[self.roles[role] * 2 + other],
            self.pair.at[role],
            self.sems,
            role,
            self.chip * 2 + other,
            "fsdp",
        )

    def to_mate(self, role):
        slot = (1, 2, 0)[role]
        return push(
            self.pair.at[role],
            self.got.at[slot],
            self.sems,
            4 + slot,
            self.mate * 2 + self.core,
            "fsdp",
        )

    def to_other(self, role):
        return push(
            self.pair.at[role],
            self.got.at[3],
            self.sems,
            7 + role,
            self.roles[role] * 2 + self.core,
            "fsdp",
            7,
        )

    def direct(self, step):
        peer = lax.rem(self.row + step, self.fsdp)
        return push(
            self.grad.at[peer], self.got.at[step - 1], self.sems, step - 1, peer, "fsdp"
        )

    def start(self):
        if self.fsdp != 8:
            for step in range(1, self.fsdp):
                self.direct(step).start()
        else:
            for role in range(4):
                self.across(role).start()
        if self.mine is not None:
            for role in range(len(self.own)):
                self.fetch(role).start()

    def pairs(self):
        if self.fsdp != 8:
            return
        for role in range(3):
            self.across(role).wait_recv()
            self.ready(role)

            def add(part, role=role):
                self.pair[role, part] = (
                    self.pair[role, part].astype(F32) + self.block(role, part)
                ).astype(BF16)

            self.rows(add)
            if role < 2:

                @pl.when(jnp.logical_not(inner_chip(self.chip)))
                def _(role=role):
                    self.to_mate(role).start()
            else:
                self.to_mate(role).start()

    def forward(self, roles=(0, 1)):
        if self.fsdp != 8:
            return

        @pl.when(inner_chip(self.chip))
        def _():
            for role in roles:
                self.to_mate(role).wait_recv()

                def add(part, role=role):
                    self.pair[role, part] = (
                        self.pair[role, part].astype(F32) + self.got[role + 1, part].astype(F32)
                    ).astype(BF16)

                self.rows(add)
                self.to_other(role).start()

    def finish(self, out, offset=0):
        height = self.grad.shape[1]
        if offset or out.shape[0] != height:
            out = out.at[pl.ds(offset, height)]
        if self.fsdp != 8:
            for step in range(1, self.fsdp):
                self.direct(step).wait_recv()

            self.ready(0)

            def total(part):
                value = self.block(0, part)
                for step in range(1, self.fsdp):
                    value = value + self.got[step - 1, part].astype(F32)
                out[part, :] = value.astype(out.dtype)

            self.rows(total)
            for step in range(1, self.fsdp):
                self.direct(step).wait_send()
            return
        self.across(3).wait_recv()
        self.to_mate(2).wait_recv()
        self.to_other(0).wait_recv()
        self.ready(3)

        def total(part):
            out[part, :] = (
                self.block(3, part)
                + self.pair[3, part].astype(F32)
                + self.got[0, part].astype(F32)
                + self.got[3, part].astype(F32)
            ).astype(out.dtype)

        self.rows(total)
        for role in range(4):
            self.across(role).wait_send()
        self.to_mate(2).wait_send()

        @pl.when(inner_chip(self.chip))
        def _():
            self.to_other(0).wait_send()
            self.to_other(1).wait_send()

        @pl.when(jnp.logical_not(inner_chip(self.chip)))
        def _():
            self.to_mate(0).wait_send()
            self.to_mate(1).wait_send()


def n_copies(size):
    return 6 if size == 4 else size - 1


class Gather:
    def __init__(self, size, own, whole, sems):
        self.size, self.own, self.whole, self.sems = size, own, whole, sems
        self.me = lax.axis_index("seq")
        self.peers = others(size)
        self.rows = own.shape[0]

    def place(self, device, half=None):
        count = self.rows // 2 if half is not None else self.rows
        at = device * self.rows + (count if half else 0)
        return self.whole.at[pl.ds(pl.multiple_of(at, count), count)]

    def copy(self, index):
        me, own, sems = self.me, self.own, self.sems
        if self.size != 4:
            return push(own, self.place(me), sems, index, self.peers[index])
        side, over, _ = self.peers
        count = self.rows // 2
        one, two = pl.ds(0, count), pl.ds(count, count)
        src, dst, peer = [
            (own.at[one], self.place(me, 0), side),
            (own.at[two], self.place(me, 1), side),
            (own.at[two], self.place(me, 1), over),
            (own.at[one], self.place(me, 0), over),
            (self.place(side, 0), self.place(side, 0), over),
            (self.place(over, 1), self.place(over, 1), side),
        ][index]
        return push(src, dst, sems, index, peer)

    def local(self, sem):
        return pltpu.make_async_copy(self.own, self.place(self.me), sem)

    def start(self):
        for index in (0, 2, 1, 3) if self.size == 4 else range(self.size - 1):
            self.copy(index).start()

    def forward(self):
        if self.size == 4:
            for index in (0, 2):
                self.copy(index).wait_recv()
            self.copy(4).start()
            self.copy(5).start()

    def finish(self, task=None):
        if self.size == 4:
            order = [(self.peers[0], (1,)), (self.peers[1], (3,)), (self.peers[2], (4, 5))]
        else:
            order = [
                (lax.rem(self.me - k - 1 + self.size, self.size), (k,))
                for k in range(self.size - 1)
            ]
        for device, parts in order:
            for index in parts:
                self.copy(index).wait_recv()
            if task is not None:
                task(device)
        for index in range(n_copies(self.size)):
            self.copy(index).wait_send()


def scatter_scratch(size, rows, width):
    small = size == 4
    return [
        pltpu.VMEM((size, rows, width), BF16),
        pltpu.VMEM((2, rows // 2, width) if small else (1, 16, 128), BF16),
        pltpu.VMEM((2 if small else size - 1, rows, width), BF16),
    ] + [pltpu.SemaphoreType.DMA((n_copies(size),))] * 2


class Scatter:
    def __init__(self, size, held, stage, got, sems):
        self.size, self.held, self.stage, self.got, self.sems = size, held, stage, got, sems
        self.me = lax.axis_index("seq")
        self.peers = others(size)
        half = held.shape[1] // 2
        self.parts = [pl.ds(0, half), pl.ds(half, half)]

    def copy(self, index):
        held, stage, got, sems = self.held, self.stage, self.got, self.sems
        if self.size != 4:
            peer = self.peers[index]
            return push(held.at[peer], got.at[index], sems, index, peer)
        side, over, far = self.peers
        one, two = self.parts
        src, dst, peer = [
            (held.at[far, one], stage.at[0], side),
            (held.at[far, two], stage.at[1], over),
            (held.at[side, one], got.at[0, one], side),
            (held.at[over, two], got.at[1, two], over),
            (held.at[side, two], got.at[0, two], side),
            (held.at[over, one], got.at[1, one], over),
        ][index]
        return push(src, dst, sems, index, peer)

    def sends(self):
        if self.size == 4:
            return [(2, (0, 1)), (0, (2,)), (1, (3,))]
        return [(k, (k,)) for k in range(self.size - 1)]

    def ready(self, device):
        for place, indices in self.sends():

            @pl.when(self.peers[place] == device)
            def _(indices=indices):
                for index in indices:
                    self.copy(index).start()

    def send(self, make, hooks=()):
        hooks = list(hooks)
        for place, indices in self.sends():
            make(self.peers[place], self.held.at[self.peers[place]])
            for index in indices:
                self.copy(index).start()
            run_hook(hooks)
        while hooks:
            run_hook(hooks)

    def forward(self):
        if self.size == 4:
            side, over, _ = self.peers
            one, two = self.parts
            held, stage = self.held, self.stage
            self.copy(1).wait_recv()
            held[side, two] = (held[side, two].astype(F32) + stage[1].astype(F32)).astype(BF16)
            self.copy(4).start()
            self.copy(0).wait_recv()
            held[over, one] = (held[over, one].astype(F32) + stage[0].astype(F32)).astype(BF16)
            self.copy(5).start()

    def finish(self):
        for index in range(n_copies(self.size)):
            if self.size != 4 or index > 1:
                self.copy(index).wait_recv()
        for index in range(n_copies(self.size)):
            self.copy(index).wait_send()

    def terms(self, rows):
        total = self.got[0, rows].astype(F32)
        for k in range(1, self.got.shape[0]):
            total = total + self.got[k, rows].astype(F32)
        return total


def run_hook(hooks):
    if hooks:
        hook = hooks.pop(0)
        if hook is not None:
            hook()


def each(count, step, task):
    def run(index, carry):
        task(pl.multiple_of(index * step, step))
        return carry

    lax.fori_loop(0, count // step, run, 0)


class Load:
    def __init__(self, src, dst, sem):
        self.dst, self.waited = dst, False
        self.copy = pltpu.make_async_copy(src, dst, sem)
        self.copy.start()

    def get(self):
        if not self.waited:
            self.waited = True
            self.copy.wait()
        return self.dst


def loads(srcs, dsts, sems):
    return [Load(src, dst, sems.at[k]) for k, (src, dst) in enumerate(zip(srcs, dsts))]


def load_scratch(arrays):
    return [pltpu.VMEM(array.shape, array.dtype) for array in arrays] + [
        pltpu.SemaphoreType.DMA((len(arrays),))
    ]


def tile_of(width, most):
    tile = most
    while width % tile:
        tile //= 2
    return tile


def swap_halves(block):
    half = HEAD_DIM // 2
    return jnp.concatenate([block[:, half:], block[:, :half]], axis=1)


def inv_rms(values):
    return lax.rsqrt(jnp.mean(values * values, axis=-1, keepdims=True) + EPSILON)


def mask_bias(ids_col, ids_row, start, low, span):
    query = start + lax.broadcasted_iota(jnp.int32, (BLOCK, span), 0)
    key = low + lax.broadcasted_iota(jnp.int32, (BLOCK, span), 1)
    same = ids_col[pl.ds(start, BLOCK), :] == ids_row[:, pl.ds(low, span)]
    bias = jnp.where(jnp.logical_and(same, key <= query), 0.0, NEGATIVE)
    return jnp.concatenate([bias, bias], axis=0)


def join_blocks(blocks, seq, whole):
    fsdp = blocks.shape[0]
    ratio = fsdp // seq
    height, width = blocks.shape[1:]
    for down in range(ratio):
        for across in range(seq):
            whole[down * height : (down + 1) * height, across * width : (across + 1) * width] = (
                blocks[line_place(seq, fsdp, down, across)]
            )


def forward_kernel(
    seq, fsdp, hidden, w_qkv, w_out, w_gate, w_up, w_down, cot, ids, gain_one, gain_two, normed,
    ids_row, ids_col, cosine, sine, gains, packed, attn, lse, middle, own_normed, rows_out,
    cols_qkv, cols_gate, cols_up, moved_out, moved_down, cot_all, raw, ids_all, gain_own,
    gain_parts, blocks_out, held, stage, got, *sems
):
    def take(count):
        nonlocal sems
        taken, sems = sems[:count], sems[count:]
        return taken

    rows, width = hidden.shape
    length = rows * seq
    groups = w_qkv.shape[1] // (4 * HEAD_DIM)
    me, row = lax.axis_index("seq"), lax.axis_index("fsdp")
    to, source = row_owner(seq, fsdp)
    share = gain_one.shape[1]
    tile = tile_of(width, 512)
    gain_own[0:1, :] = gain_one[...].astype(F32)
    gain_own[1:2, :] = gain_two[...].astype(F32)
    gain_parts[row, me] = gain_own[...]
    ids_all[me] = ids[...]
    meet(seq, fsdp, (to, source))
    local = take(1)[0]
    whole = Gather(seq, hidden, raw, take(2))
    cots = Gather(seq, cot, cot_all, take(2))
    sums = Scatter(seq, held, stage, got, take(2))
    half = w_gate.shape[0] // 2
    one, two = pl.ds(0, half), pl.ds(half, half)
    line_qkv = LineGather(fsdp, w_qkv, cols_qkv, take(3))
    line_out = LineGather(fsdp, moved_out, blocks_out, take(3))
    line_gate = [
        LineGather(fsdp, w_gate, cols_gate, take(3), part) for part in (one, two)
    ]
    line_up = [LineGather(fsdp, w_up, cols_up, take(3), part) for part in (one, two)]
    move_out = Move(w_out, moved_out, to, take(3), 0)
    move_down = Move(w_down, moved_down, to, take(3), 0)
    id_sems, gain_sems, wide_sems = take(2), take(2), take(2)
    id_copies = [
        push(ids, ids_all.at[me], id_sems, k, peer) for k, peer in enumerate(others(seq))
    ]
    gain_copies = [
        push(gain_own, gain_parts.at[row, me], gain_sems, k, peer)
        for k, peer in enumerate(others(seq))
    ]
    for copy in id_copies + gain_copies:
        copy.start()
    line_qkv.start()
    whole.start()
    move_out.start()
    mine = whole.local(local.at[0])
    mine.start()
    for copy in gain_copies:
        copy.wait()
    wide = [
        push(
            gain_parts.at[row],
            gain_parts.at[row],
            wide_sems,
            step - 1,
            lax.rem(row + step, fsdp),
            "fsdp",
        )
        for step in range(1, fsdp)
    ]
    for copy in wide:
        copy.start()
    for copy in id_copies:
        copy.wait()
    for k in range(seq):
        for at in range(0, rows, 128):
            piece = ids_all[k, :, at : at + 128]
            ids_row[:, k * rows + at : k * rows + at + 128] = piece
            turned = jnp.transpose(jnp.broadcast_to(piece, (128, 128)))
            ids_col[k * rows + at : k * rows + at + 128, :] = turned[:, :1]
    whole.forward()
    line_qkv.forward()
    for line in line_gate:
        line.start()
    order = lax.broadcasted_iota(jnp.int32, (1, HEAD_DIM // 2), 1).astype(F32)
    inverse = jnp.exp(order * (-2.0 * math.log(ROPE_BASE) / HEAD_DIM))

    def table(at):
        part = pl.ds(at, BLOCK)
        first = jnp.sum(
            (ids_row[...] < ids_col[part, :]).astype(jnp.int32).astype(F32),
            axis=-1,
            keepdims=True,
        )
        place = (at + lax.broadcasted_iota(jnp.int32, (BLOCK, 1), 0)).astype(F32) - first
        angles = place * inverse
        cos, sin = jnp.cos(angles), jnp.sin(angles)
        cosine[part, :] = jnp.concatenate([cos, cos], axis=1)
        sine[part, :] = jnp.concatenate([-sin, sin], axis=1)

    each(length, BLOCK, table)
    for copy in wide:
        copy.wait()
    for r in range(fsdp):
        for k in range(seq):
            at = (r * seq + k) * share
            gains[:, at : at + share] = gain_parts[r, k]
    mine.wait()

    def norm(device):
        base = pl.multiple_of(device * rows, rows)

        def part(at):
            values = raw[pl.ds(base + at, 128), :].astype(F32)
            normed[pl.ds(base + at, 128), :] = (
                values * inv_rms(values) * gains[0:1, :]
            ).astype(BF16)

        each(rows, 128, part)

    norm(me)
    move_out.finish()
    line_out.start()
    whole.finish(norm)
    cots.start()
    kept = cots.local(local.at[0])
    kept.start()
    move_down.start()
    line_qkv.finish()
    for group in range(groups):

        def project(at, group=group):
            part = pl.ds(at, 512)
            low = group * 4 * HEAD_DIM
            weight = cols_qkv[:, :, low : low + 4 * HEAD_DIM].reshape(width, 4 * HEAD_DIM)
            proj = dot(normed[part, :], weight)
            for slot in range(4):
                piece = proj[:, slot * HEAD_DIM : (slot + 1) * HEAD_DIM]
                if slot < 3:
                    piece = piece * cosine[part, :] + swap_halves(piece) * sine[part, :]
                packed[group * 4 + slot, part, :] = piece.astype(BF16)

        each(length, 512, project)
    line_out.forward()
    hooks = [
        line_gate[0].forward,
        cots.forward,
        line_out.finish,
        line_gate[1].forward,
        line_up[0].start,
        line_up[1].start,
        None,
        line_up[0].forward,
    ]
    for index in range(seq):
        start = index * BLOCK
        low = max(0, start - length // 2)
        span = start + BLOCK - low
        part, keys = pl.ds(start, BLOCK), pl.ds(low, span)
        bias = mask_bias(ids_col, ids_row, start, low, span)
        mixed, logs = [], []
        for group in range(groups):
            queries = jnp.concatenate(
                [packed[group * 4, part, :], packed[group * 4 + 1, part, :]], axis=0
            )
            scores = dot_nt(queries, packed[group * 4 + 2, keys, :]) * SCALE + bias
            most = jnp.max(scores, axis=-1, keepdims=True)
            grown = jnp.exp(scores - most)
            total = jnp.sum(grown, axis=-1, keepdims=True)
            weights = (grown * (1.0 / total)).astype(BF16)
            out = dot(weights, packed[group * 4 + 3, keys, :])
            log_total = most + jnp.log(total)
            mixed += [out[:BLOCK], out[BLOCK:]]
            logs += [log_total[:BLOCK], log_total[BLOCK:]]
            if index:
                run_hook(hooks)
        attn[part, :] = jnp.concatenate(mixed, axis=1).astype(BF16)
        lane = lax.broadcasted_iota(jnp.int32, (BLOCK, 128), 1)
        stats = jnp.zeros((BLOCK, 128), F32)
        for head, log_total in enumerate(logs):
            stats = jnp.where(lane == head, log_total, stats)
        lse[part, :] = stats
        if index == 0:
            run_hook(hooks)
            run_hook(hooks)
            run_hook(hooks)
            join_blocks(blocks_out, seq, rows_out)

        def onward(at, part=part, index=index):
            cols = pl.ds(at, tile)
            term = dot(attn[part, :], rows_out[:, cols])

            @pl.when(me == index)
            def _():
                middle[:, cols] = raw[index * rows : (index + 1) * rows, cols].astype(F32) + term

            @pl.when(me != index)
            def _():
                held[index, :, cols] = term.astype(BF16)

        each(width, tile, onward)
        sums.ready(index)
    while hooks:
        run_hook(hooks)
    sums.forward()
    cots.finish()
    kept.wait()
    line_gate[0].finish()
    line_gate[1].finish()
    line_up[1].forward()
    sums.finish()

    def second(at):
        part = pl.ds(at, 128)
        values = middle[part, :] + sums.terms(part)
        middle[part, :] = values
        own_normed[part, :] = (values * inv_rms(values) * gains[1:2, :]).astype(BF16)

    each(rows, 128, second)
    line_up[0].finish()
    line_up[1].finish()
    move_down.finish()


def forward(seq, fsdp, hidden, w_qkv, w_out, w_gate, w_up, w_down, cot, ids, gain_one, gain_two):
    rows, width = hidden.shape
    length = rows * seq
    dma = pltpu.SemaphoreType.DMA
    share = gain_one.shape[1]
    groups = w_qkv.shape[1] // (4 * HEAD_DIM)
    inner = groups * 2 * HEAD_DIM
    return pl.pallas_call(
        functools.partial(forward_kernel, seq, fsdp),
        out_shape=(
            shape((length, width), BF16),
            shape((1, length), jnp.int32),
            shape((length, 1), jnp.int32),
            shape((length, HEAD_DIM), F32),
            shape((length, HEAD_DIM), F32),
            shape((2, width), F32),
            shape((groups * 4, length, HEAD_DIM), BF16),
            shape((length, inner), BF16),
            shape((length, 128), F32),
            shape((rows, width), F32),
            shape((rows, width), BF16),
            shape((inner, width), BF16),
            shape((fsdp,) + w_qkv.shape, BF16),
            shape((fsdp,) + w_gate.shape, BF16),
            shape((fsdp,) + w_up.shape, BF16),
            shape(w_out.shape, BF16),
            shape(w_down.shape, BF16),
            shape((length, width), BF16),
        ),
        in_specs=[ANY] * 7 + [VMEM] * 3,
        out_specs=(VMEM,) * 13 + (ANY,) * 5,
        scratch_shapes=[
            pltpu.VMEM((length, width), BF16),
            pltpu.VMEM((seq, 1, rows), jnp.int32),
            pltpu.VMEM((2, share), F32),
            pltpu.VMEM((fsdp, seq, 2, share), F32),
            pltpu.VMEM((fsdp,) + w_out.shape, BF16),
        ]
        + scatter_scratch(seq, rows, width)[:3]
        + [dma((1,))]
        + [dma((n_copies(seq),))] * 6
        + line_scratch(fsdp) * 6
        + [dma((1,))] * 6
        + [dma((seq - 1,))] * 4
        + [dma((fsdp - 1,))] * 2,
        compiler_params=params(0),
        name="forward",
    )(hidden, w_qkv, w_out, w_gate, w_up, w_down, cot, ids, gain_one, gain_two)


def feed_kernel(
    seq, fsdp, own_normed, cot_all, w_gate, w_up, middle, w_down, gains, d_middle, own_low, d_gain,
    own_down, out_terms, g_gate, g_up, normed, whole_down, blocks, g_down, gate, up, hid, d_gate,
    d_up, held, stage, got, grad_tiles, *rest
):
    arrays, rest = rest[:5], rest[5:]
    rows, width = middle.shape
    length = rows * seq
    inner = gate.shape[1]
    me = lax.axis_index("seq")
    tile = tile_of(width, 512)
    wide = tile_of(inner, 512)
    w_gate, w_up, cot, middle = loads((w_gate, w_up, cot_all, middle), arrays[:4], arrays[4])
    meet(seq, fsdp)
    local, tile_sems = rest[0], rest[1]
    whole = Gather(seq, own_normed, normed, rest[2:4])
    sums = Scatter(seq, held, stage, got, rest[4:6])
    half = w_down.shape[0] // 2
    line_down = [
        LineGather(fsdp, w_down, blocks, rest[6:9], pl.ds(0, half)),
        LineGather(fsdp, w_down, blocks, rest[9:12], pl.ds(half, half)),
    ]
    early = fsdp == 8
    if not early:
        g_down = blocks
    line = LineReduce(fsdp, g_down, *rest[12:])
    for exchange in line_down:
        exchange.start()
    whole.start()
    mine = whole.local(local.at[0])
    mine.start()
    w_gate, w_up = w_gate.get(), w_up.get()
    mine.wait()

    def block_of(device):
        return pl.ds(pl.multiple_of(device * rows, rows), rows)

    def first(device):
        block = block_of(device)

        def part(at):
            cols = pl.ds(at, wide)
            gate_part = dot(normed[block, :], w_gate[:, cols])
            up_part = dot(normed[block, :], w_up[:, cols])
            gate[block, cols] = gate_part
            up[block, cols] = up_part
            hid[block, cols] = (gate_part / (1.0 + jnp.exp(-gate_part)) * up_part).astype(BF16)

        each(inner, wide, part)

    first(me)
    whole.forward()
    hooks = [line_down[0].forward, line_down[1].forward]

    def arrived(device):
        first(device)
        run_hook(hooks)

    whole.finish(arrived)
    while hooks:
        run_hook(hooks)
    cot, middle = cot.get(), middle.get()
    height, across = g_down.shape[1:]

    def down_grad(k):
        cols = slice(k * across, (k + 1) * across)
        for down in range(fsdp // seq):
            g_down[line_place(seq, fsdp, down, k)] = dot_tn(
                hid[:, down * height : (down + 1) * height], cot[:, cols]
            ).astype(BF16)

    def join_down():
        for exchange in line_down:
            exchange.finish()
        join_blocks(blocks, seq, whole_down)

    if not early:
        join_down()
    for k in range(seq):
        down_grad(k)
    line.start()
    if early:
        join_down()

    def second(device, out):
        block = block_of(device)

        def part(at):
            cols = pl.ds(at, wide)
            d_hid = dot_nt(cot[block, :], whole_down[cols, :])
            gate_part = gate[block, cols]
            sig = 1.0 / (1.0 + jnp.exp(-gate_part))
            d_gate[block, cols] = (
                d_hid * up[block, cols] * sig * (1.0 + gate_part * (1.0 - sig))
            ).astype(BF16)
            d_up[block, cols] = (d_hid * (gate_part * sig)).astype(BF16)

        each(inner, wide, part)

        def term(at):
            cols = pl.ds(at, tile)
            total = dot_nt(d_gate[block, :], w_gate[cols, :]) + dot_nt(
                d_up[block, :], w_up[cols, :]
            )
            out[:, cols] = total.astype(out.dtype)

        each(width, tile, term)

    sums.send(second, [None, line.pairs])
    second(me, d_middle)
    sums.forward()
    line.forward((0,))
    wide_rows = grad_tiles.shape[1]
    for left, grads in ((d_gate, g_gate), (d_up, g_up)):

        def tile_out(index, grads=grads):
            return pltpu.make_async_copy(
                grad_tiles.at[lax.rem(index, 2)],
                grads.at[pl.ds(pl.multiple_of(index * wide_rows, wide_rows), wide_rows)],
                tile_sems.at[lax.rem(index, 2)],
            )

        def job(index, left=left, tile_out=tile_out):
            @pl.when(index >= 2)
            def _():
                tile_out(index - 2).wait()

            at = pl.multiple_of(index * wide_rows, wide_rows)
            grad_tiles[lax.rem(index, 2)] = dot_tn(
                normed[:, pl.ds(at, wide_rows)], left[...]
            ).astype(BF16)
            tile_out(index).start()

        count = width // wide_rows
        each(count, 1, job)
        for index in range(max(0, count - 2), count):
            tile_out(index).wait()
        if left is d_gate:
            line.forward((1,))

    def outward(index):
        block = pl.ds(pl.multiple_of(index * rows, rows), rows)

        def part(at):
            cols = pl.ds(at, tile)
            normed[block, cols] = dot(hid[block, :], whole_down[:, cols]).astype(BF16)

        each(width, tile, part)

    each(seq, 1, outward)
    terms_out = pltpu.make_async_copy(normed, out_terms, local.at[0])
    terms_out.start()
    sums.finish()
    d_gain[...] = jnp.zeros_like(d_gain)
    base = pl.multiple_of(me * rows, rows)

    def norm(at):
        part = pl.ds(at, 128)
        values = middle[part, :]
        grad = d_middle[part, :] + sums.terms(part)
        scale = inv_rms(values)
        weighted = grad * gains[1:2, :]
        mean = jnp.mean(weighted * values, axis=-1, keepdims=True)
        d_gain[...] += jnp.sum(grad * values * scale, axis=0, keepdims=True)
        total = cot[pl.ds(base + at, 128), :].astype(F32) + scale * (
            weighted - values * (scale * scale) * mean
        )
        d_middle[part, :] = total
        own_low[part, :] = total.astype(BF16)

    each(rows, 128, norm)
    line.finish(own_down)
    terms_out.wait()


def feed(seq, fsdp, own_normed, cot_all, w_gate, w_up, middle, w_down, gains):
    rows, width = middle.shape
    length = rows * seq
    inner = w_gate.shape[1]
    dma = pltpu.SemaphoreType.DMA
    return pl.pallas_call(
        functools.partial(feed_kernel, seq, fsdp),
        out_shape=(
            shape((rows, width), F32),
            shape((rows, width), BF16),
            shape((1, width), F32),
            shape(w_down.shape, BF16),
            shape((length, width), BF16),
            shape((width, inner), BF16),
            shape((width, inner), BF16),
        ),
        in_specs=[ANY] * 6 + [VMEM],
        out_specs=(VMEM,) * 4 + (ANY,) * 3,
        scratch_shapes=[
            pltpu.VMEM((length, width), BF16),
            pltpu.VMEM((inner, width), BF16),
            pltpu.VMEM((fsdp,) + w_down.shape, BF16),
            pltpu.VMEM((fsdp,) + w_down.shape if fsdp == 8 else (1, 16, 128), BF16),
            pltpu.VMEM((length, inner), F32),
            pltpu.VMEM((length, inner), F32),
            pltpu.VMEM((length, inner), BF16),
            pltpu.VMEM((length, inner), BF16),
            pltpu.VMEM((length, inner), BF16),
        ]
        + scatter_scratch(seq, rows, width)[:3]
        + [pltpu.VMEM((2, min(512, inner // 2), inner), BF16)]
        + load_scratch((w_gate, w_up, cot_all, middle))
        + [dma((1,)), dma((2,))]
        + [dma((n_copies(seq),))] * 4
        + line_scratch(fsdp) * 2
        + reduce_scratch(fsdp, *w_down.shape),
        compiler_params=params(1),
        name="feed",
    )(own_normed, cot_all, w_gate, w_up, middle, w_down, gains)


def backward_kernel(
    seq, fsdp, own_low, g_gate, g_up, w_out, attn, packed, lse, cosine, sine, w_qkv, hidden,
    d_middle, out_terms, middle, own_down, normed, ids_col, ids_row, gain, gain_two, d_input, output,
    own_qkv, own_gate, own_up, g_down, g_out, g_gain_one, g_gain_two, held_out, stage_out, got_out,
    held, stage, got, d_low, d_keys, d_vals, d_packed, grad_out, grad_qkv, home_down, mid_down,
    home_out, mid_out, own_out, parts, seq_parts, sums_own, fsdp_parts, *rest
):
    def take(count):
        nonlocal rest
        taken, rest = rest[:count], rest[count:]
        return taken

    rows, width = own_low.shape
    length = rows * seq
    groups = packed.shape[0] // 4
    ratio = fsdp // seq
    height, across = grad_out.shape[1:]
    tile, tall = tile_of(width, 512), tile_of(width, 512)
    me, row = lax.axis_index("seq"), lax.axis_index("fsdp")
    arrays = take(10)
    w_out, attn, packed, lse, cosine, sine, w_qkv, hidden, d_middle = loads(
        (w_out, attn, packed, lse, cosine, sine, w_qkv, hidden, d_middle),
        arrays[:9],
        arrays[9],
    )
    local = take(1)[0]
    terms = Load(out_terms, held_out, local.at[1])
    middle = Load(middle, output, local.at[2])
    meet(seq, fsdp)
    whole = Gather(seq, own_low, d_low, take(2))
    outs = Scatter(seq, held_out, stage_out, got_out, take(2))
    early = seq != 4
    if early:
        held = held_out
    sums = Scatter(seq, held, stage, got, take(2))
    part_sems = take(4)
    size = len(reduce_scratch(fsdp, 16, 128))
    line_gate = LineReduce(fsdp, g_gate, *take(size), mine=take(2))
    line_up = LineReduce(fsdp, g_up, *take(size), mine=take(2))
    line_out = LineReduce(fsdp, grad_out, *take(size))
    line_qkv = LineReduce(fsdp, grad_qkv, *take(size))
    moves = [
        Home(seq, fsdp, own_down, mid_down, home_down, take(3)),
        Home(seq, fsdp, own_out, mid_out, home_out, take(3)),
    ]
    whole.start()
    here = whole.local(local.at[0])
    here.start()
    line_gate.start()
    line_up.start()
    w_out, attn, packed, lse = w_out.get(), attn.get(), packed.get(), lse.get()
    cosine, sine = cosine.get(), sine.get()
    d_keys[...] = jnp.zeros_like(d_keys)
    d_vals[...] = jnp.zeros_like(d_vals)
    line_gate.pairs()
    here.wait()
    span = length // 2 + BLOCK

    def send_out():
        outs.send(lambda device, ref: terms.get())

    hooks = [
        whole.forward,
        functools.partial(line_gate.forward, (0,)),
        moves[0].start_plane,
        line_up.pairs,
        functools.partial(line_gate.forward, (1,)),
        send_out,
        functools.partial(line_up.forward, (0,)),
        None,
    ]

    def attend(device):
        start = pl.multiple_of(device * BLOCK, BLOCK)
        low = pl.multiple_of(jnp.maximum(start - length // 2, 0), BLOCK)
        part, keys = pl.ds(start, BLOCK), pl.ds(low, span)
        d_attn = dot_nt(d_low[part, :], w_out[...]).astype(BF16)
        bias = mask_bias(ids_col, ids_row, start, low, span)
        for group in range(groups):
            base = group * 2 * HEAD_DIM
            queries = jnp.concatenate(
                [packed[group * 4, part, :], packed[group * 4 + 1, part, :]], axis=0
            )
            d_wide = d_attn[:, base : base + 2 * HEAD_DIM]
            product = attn[part, base : base + 2 * HEAD_DIM].astype(F32) * d_wide.astype(F32)
            delta = jnp.concatenate(
                [
                    jnp.sum(product[:, :HEAD_DIM], axis=-1, keepdims=True),
                    jnp.sum(product[:, HEAD_DIM:], axis=-1, keepdims=True),
                ],
                axis=0,
            )
            d_out = jnp.concatenate([d_wide[:, :HEAD_DIM], d_wide[:, HEAD_DIM:]], axis=0)
            logs = jnp.concatenate(
                [
                    lse[part, group * 2 : group * 2 + 1],
                    lse[part, group * 2 + 1 : group * 2 + 2],
                ],
                axis=0,
            )
            key_rows = packed[group * 4 + 2, keys, :]
            scores = dot_nt(queries, key_rows) * SCALE + bias
            probs = jnp.exp(scores - logs)
            d_probs = dot_nt(d_out, packed[group * 4 + 3, keys, :])
            d_scores = (probs * (d_probs - delta)).astype(BF16)
            d_vals[group, keys, :] += dot_tn(probs.astype(BF16), d_out)
            d_keys[group, keys, :] += dot_tn(d_scores, queries) * SCALE
            d_query = dot(d_scores, key_rows) * SCALE
            turned = [
                piece * cosine[part, :] - swap_halves(piece) * sine[part, :]
                for piece in (d_query[:BLOCK], d_query[BLOCK:])
            ]
            d_packed[part, group * 4 * HEAD_DIM : group * 4 * HEAD_DIM + 2 * HEAD_DIM] = (
                jnp.concatenate(turned, axis=1).astype(BF16)
            )
            run_hook(hooks)

    def out_grad():
        for k in range(seq):
            part = dot_tn(attn[...], d_low[:, k * across : (k + 1) * across]).astype(BF16)
            for down in range(ratio):
                grad_out[line_place(seq, fsdp, down, k)] = part[
                    down * height : (down + 1) * height
                ]
        line_out.start()

    left = list(range(seq - 1))

    def arrived(device):
        left.pop()
        if not left:
            out_grad()
        attend(device)

    attend(me)
    whole.finish(arrived)
    while hooks:
        run_hook(hooks)
    normed = Load(normed, d_low, local.at[3])
    moves[0].finish_plane()
    moves[0].start_line()

    def last(at):
        part = pl.ds(at, BLOCK)
        for group in range(groups):
            d_key = d_keys[group, part, :]
            turned = d_key * cosine[part, :] - swap_halves(d_key) * sine[part, :]
            base = group * 4 * HEAD_DIM + 2 * HEAD_DIM
            d_packed[part, base : base + 2 * HEAD_DIM] = jnp.concatenate(
                [turned, d_vals[group, part, :]], axis=1
            ).astype(BF16)

    each(length, BLOCK, last)
    line_out.pairs()
    normed = normed.get()
    rows_each = grad_qkv.shape[1]

    per = 128 // math.gcd(128, rows_each)

    def weight(index):
        part = pl.ds(pl.multiple_of(index * per * rows_each, per * rows_each), per * rows_each)
        grad = dot_tn(normed[:, part], d_packed[...]).astype(BF16)
        for k in range(per):
            grad_qkv[index * per + k] = grad[k * rows_each : (k + 1) * rows_each]

    each(fsdp // per, 1, weight)
    line_qkv.start()
    w_qkv = w_qkv.get()

    def one(device, at):
        block = pl.ds(pl.multiple_of(device * rows, rows), rows)
        return dot_nt(d_packed[block, :], w_qkv[pl.ds(at, tile), :])

    def term(device, ref):
        def part(at):
            ref[:, pl.ds(at, tile)] = one(device, at).astype(BF16)

        each(width, tile, part)

    def finish_output():
        middle.get()
        outs.finish()

        def total_of(at):
            part = pl.ds(at, 128)
            output[part, :] = (
                output[part, :] + held_out[me, part, :].astype(F32) + outs.terms(part)
            )

        each(rows, 128, total_of)

    if early:
        finish_output()
    sums.send(
        term,
        [outs.forward, functools.partial(line_up.forward, (1,)), line_qkv.pairs],
    )

    def own(at):
        d_input[:, pl.ds(at, tile)] = one(me, at)

    each(width, tile, own)
    hidden, d_middle = hidden.get(), d_middle.get()
    line_out.forward()
    line_gate.finish(own_gate)
    sums.forward()
    line_qkv.forward((0,))
    line_up.finish(own_up)
    if not early:
        finish_output()
    line_out.finish(own_out)
    moves[1].start_plane()
    line_qkv.forward((1,))
    parts[0:1, :] = jnp.zeros((1, width), F32)
    parts[1:2, :] = gain_two[...]
    moves[1].finish_plane()
    moves[1].start_line()
    sums.finish()

    def norm(at):
        part = pl.ds(at, 128)
        values = hidden[part, :].astype(F32)
        grad = d_input[part, :] + sums.terms(part)
        scale = inv_rms(values)
        weighted = grad * gain[0:1, :]
        mean = jnp.mean(weighted * values, axis=-1, keepdims=True)
        parts[0:1, :] += jnp.sum(grad * values * scale, axis=0, keepdims=True)
        d_input[part, :] = d_middle[part, :] + scale * (
            weighted - values * (scale * scale) * mean
        )

    each(rows, 128, norm)
    first = [
        push(parts, seq_parts.at[k], part_sems[:2], k, peer)
        for k, peer in enumerate(others(seq))
    ]
    for copy in first:
        copy.start()
    moves[0].finish_line()
    g_down[...] = home_down[...].astype(F32)
    for copy in first:
        copy.wait()
    total = parts[...]
    for k in range(seq - 1):
        total = total + seq_parts[k]
    sums_own[...] = total
    second = [
        push(
            sums_own,
            fsdp_parts.at[step - 1],
            part_sems[2:],
            step - 1,
            lax.rem(row + step, fsdp),
            "fsdp",
        )
        for step in range(1, fsdp)
    ]
    for copy in second:
        copy.start()
    moves[1].finish_line()
    g_out[...] = home_out[...].astype(F32)
    line_qkv.finish(own_qkv)
    for copy in second:
        copy.wait()
    for step in range(1, fsdp):
        total = total + fsdp_parts[step - 1]
    share = g_gain_one.shape[1]
    turned = pltpu.roll(
        jnp.broadcast_to(total[:, None, :], (2, 8, width)).reshape(16, width),
        lax.rem(width - (row * seq + me) * share, width),
        1,
    )
    g_gain_one[...] = turned[0:1, :share]
    g_gain_two[...] = turned[8:9, :share]


def backward(
    seq, fsdp, own_low, g_gate, g_up, w_out, attn, packed, lse, cosine, sine, normed, w_qkv, hidden,
    d_middle, out_terms, middle, own_down, ids_col, ids_row, gain, gain_two
):
    rows, width = own_low.shape
    length = rows * seq
    inner = attn.shape[1]
    groups = packed.shape[0] // 4
    height, across = inner // (fsdp // seq), width // seq
    share = width // (seq * fsdp)
    shard = (width // fsdp, w_qkv.shape[1])
    count = home_count(seq, fsdp)
    dma = pltpu.SemaphoreType.DMA
    big = (w_out, attn, packed, lse, cosine, sine, w_qkv, hidden, d_middle)
    return pl.pallas_call(
        functools.partial(backward_kernel, seq, fsdp),
        out_shape=(
            shape((rows, width), F32),
            shape((rows, width), F32),
            shape(shard, F32),
            shape(g_gate.shape[1:], F32),
            shape(g_up.shape[1:], F32),
            shape(own_down.shape, F32),
            shape((height, across), F32),
            shape((1, share), F32),
            shape((1, share), F32),
        ),
        in_specs=[ANY] * 16 + [VMEM] * 4,
        out_specs=(VMEM,) * 9,
        scratch_shapes=scatter_scratch(seq, rows, width)[:3]
        + [pltpu.VMEM((seq, rows, width) if seq == 4 else (1, 16, 128), BF16)]
        + scatter_scratch(seq, rows, width)[1:3]
        + [pltpu.VMEM((length, width), BF16)]
        + [pltpu.VMEM((groups, length, HEAD_DIM), F32)] * 2
        + [
            pltpu.VMEM((length, groups * 4 * HEAD_DIM), BF16),
            pltpu.VMEM((fsdp, height, across), BF16),
            pltpu.VMEM((fsdp,) + shard, BF16),
            pltpu.VMEM(own_down.shape, BF16),
            pltpu.VMEM((count,) + own_down.shape, BF16),
            pltpu.VMEM((height, across), BF16),
            pltpu.VMEM((count, height, across), BF16),
            pltpu.VMEM((height, across), BF16),
            pltpu.VMEM((2, width), F32),
            pltpu.VMEM((seq - 1, 2, width), F32),
            pltpu.VMEM((2, width), F32),
            pltpu.VMEM((fsdp - 1, 2, width), F32),
        ]
        + load_scratch(big)
        + [dma((4,))]
        + [dma((n_copies(seq),))] * 6
        + [dma((seq - 1,))] * 2
        + [dma((fsdp - 1,))] * 2
        + (reduce_scratch(fsdp, *g_gate.shape[1:]) + mine_scratch(fsdp, *g_gate.shape[1:]))
        + (reduce_scratch(fsdp, *g_up.shape[1:]) + mine_scratch(fsdp, *g_up.shape[1:]))
        + reduce_scratch(fsdp, height, across)
        + reduce_scratch(fsdp, *shard)
        + home_sems(seq, fsdp) * 2,
        compiler_params=params(2),
        name="backward",
    )(
        own_low, g_gate, g_up, *big, out_terms, middle, own_down, normed, ids_col, ids_row, gain,
        gain_two,
    )


def body(
    hidden_in, cotangent, segment_ids, w_qkv, w_out, w_gate, w_up, w_down, gain_attn, gain_mlp
):
    rows, width = hidden_in.shape
    fsdp = lax.axis_size("fsdp")
    seq = lax.axis_size("seq")
    length = rows * seq

    (
        normed_one, ids_row, ids_col, cosine, sine, gains, packed, attn, lse, middle, normed_two,
        rows_out, cols_qkv, cols_gate, cols_up, _, moved_down, cot_all,
    ) = forward(
        seq, fsdp, hidden_in, w_qkv, w_out, w_gate, w_up, w_down, cotangent, segment_ids,
        gain_attn.reshape(1, -1), gain_mlp.reshape(1, -1),
    )
    d_middle, own_low, part_two, own_down, out_terms, g_gate, g_up = feed(
        seq, fsdp, normed_two, cot_all, cols_gate.reshape(width, -1), cols_up.reshape(width, -1),
        middle, moved_down, gains,
    )
    out_terms = out_terms.reshape(seq, rows, width)
    g_up = g_up.reshape((fsdp,) + w_up.shape)
    d_input, output, g_qkv, g_gate, g_up, g_down, g_out, g_gain_one, g_gain_two = backward(
        seq, fsdp, own_low, g_gate.reshape((fsdp,) + w_gate.shape), g_up, rows_out, attn, packed,
        lse, cosine, sine, normed_one, cols_qkv.reshape(width, -1), hidden_in, d_middle, out_terms,
        middle, own_down, ids_col, ids_row, gains, part_two,
    )
    return (
        output, d_input, g_qkv, g_out, g_gate, g_up, g_down, g_gain_one.reshape(-1),
        g_gain_two.reshape(-1),
    )


def solution(mesh):
    both = P(("fsdp", "seq"), None)
    split = P("fsdp", "seq")
    gain = P(("fsdp", "seq"))
    in_specs = (both, both, split, split, split, split, split, split, gain, gain)
    out_specs = (both, both, split, split, split, split, split, gain, gain)
    return jax.shard_map(body, mesh=mesh, in_specs=in_specs, out_specs=out_specs, check_vma=False)
```

```python
import functools
import math

import jax
import jax.numpy as jnp
from jax import lax
from jax.experimental import pallas as pl
from jax.experimental.pallas import tpu as pltpu
from jax.sharding import PartitionSpec as P

HEAD_DIM = 96
EPSILON = 1e-05
ROPE_BASE = 100000.0
NEGATIVE = -1e30
SCALE = 1.0 / math.sqrt(HEAD_DIM)
SCALE_TWO = SCALE * math.log2(math.e)
MESH = pl.DeviceIdType.MESH
BLOCK = 256
F32 = jnp.float32
BF16 = jnp.bfloat16
ANY = pl.BlockSpec(memory_space=pl.ANY)
VMEM = pl.BlockSpec(memory_space=pltpu.VMEM)


def dot(left, right):
    return jnp.dot(left, right, preferred_element_type=F32)


def dot_nt(left, right):
    return lax.dot_general(left, right, (((1,), (1,)), ((), ())), preferred_element_type=F32)


def dot_tn(left, right):
    return lax.dot_general(left, right, (((0,), (0,)), ((), ())), preferred_element_type=F32)


def shape(dims, kind):
    return jax.ShapeDtypeStruct(dims, kind)


def params(collective=None):
    return pltpu.CompilerParams(
        collective_id=collective,
        has_side_effects=collective is not None,
        vmem_limit_bytes=60 << 20,
    )


def cost(flops, moved):
    return pl.CostEstimate(flops=flops, bytes_accessed=moved, transcendentals=0)


def others(size):
    me = lax.axis_index("seq")
    if size == 4:
        low, high = lax.rem(me, 2), me // 2
        return [high * 2 + 1 - low, (1 - high) * 2 + low, (1 - high) * 2 + 1 - low]
    return [lax.rem(me + step, size) for step in range(1, size)]


def meet(seq, fsdp, pairs=(), ends=True):
    barrier = pltpu.get_barrier_semaphore()
    row = lax.axis_index("fsdp")
    for peer in others(seq):
        pl.semaphore_signal(barrier, inc=1, device_id={"seq": peer}, device_id_type=MESH)
    for step in range(1, fsdp):
        peer = lax.rem(row + step, fsdp)
        pl.semaphore_signal(barrier, inc=1, device_id={"fsdp": peer}, device_id_type=MESH)
    for there in pairs:

        @pl.when(away(there))
        def _(there=there):
            pl.semaphore_signal(
                barrier,
                inc=1,
                device_id={"fsdp": there[0], "seq": there[1]},
                device_id_type=MESH,
            )

    if pairs:

        @pl.when(away(pairs[0]))
        def _():
            pl.semaphore_wait(barrier, seq + fsdp - 2 + len(pairs))

        @pl.when(jnp.logical_not(away(pairs[0])))
        def _():
            pl.semaphore_wait(barrier, seq + fsdp - 2)
    elif ends:
        pl.semaphore_wait(barrier, seq + fsdp - 2)


def away(there):
    return jnp.logical_or(
        there[0] != lax.axis_index("fsdp"), there[1] != lax.axis_index("seq")
    )


def flip(one, two):
    return one + two - 2 * one * two


def turn(chip, core, high):
    return flip(chip // 2, core) * 2 + flip(lax.rem(chip, 2), flip(high, core))


def row_owner(seq, fsdp):
    row, me = lax.axis_index("fsdp"), lax.axis_index("seq")
    if seq == 4 and fsdp == 8:
        chip, core = row // 2, lax.rem(row, 2)
        to = (turn(chip, core, me // 2) * 2 + lax.rem(me, 2), chip)
        first = flip(me // 2, chip // 2)
        high = flip(flip(lax.rem(me, 2), lax.rem(chip, 2)), first)
        return to, (me * 2 + first, high * 2 + core)
    ratio = fsdp // seq
    to = (lax.rem(row, ratio) * seq + me, row // ratio)
    source = (me * ratio + row // seq, lax.rem(row, seq))
    return to, source


def line_place(seq, fsdp, down, across):
    if seq == 4 and fsdp == 8:
        return turn(lax.axis_index("seq"), down, across // 2) * 2 + across % 2
    return down * seq + across


def push(src, dst, sems, index, peer, axis="seq", slot=None):
    return pltpu.make_async_remote_copy(
        src_ref=src,
        dst_ref=dst,
        send_sem=sems[0].at[index],
        recv_sem=sems[1].at[index if slot is None else slot],
        device_id={axis: peer},
        device_id_type=MESH,
    )


class Move:
    def __init__(self, src, dst, to, sems, bounce):
        self.src, self.dst, self.to, self.sems, self.bounce = src, dst, to, sems, bounce
        self.index = 0

    def remote(self):
        return pltpu.make_async_remote_copy(
            src_ref=self.src,
            dst_ref=self.dst,
            send_sem=self.sems[0].at[self.index],
            recv_sem=self.sems[1].at[self.index],
            device_id={"fsdp": self.to[0], "seq": self.to[1]},
            device_id_type=MESH,
        )

    def within(self, last):
        src, dst = (self.bounce, self.dst) if last else (self.src, self.bounce)
        return pltpu.make_async_copy(src, dst, self.sems[2].at[0])

    def start(self):
        @pl.when(away(self.to))
        def _():
            self.remote().start()

        @pl.when(jnp.logical_not(away(self.to)))
        def _():
            self.within(False).start()

    def finish(self):
        @pl.when(away(self.to))
        def _():
            self.remote().wait()

        @pl.when(jnp.logical_not(away(self.to)))
        def _():
            self.within(False).wait()
            self.within(True).start()
            self.within(True).wait()


class Home:
    def __init__(self, seq, fsdp, own, mid, out, sems):
        self.seq, self.fsdp = seq, fsdp
        self.own, self.mid, self.out, self.sems = own, mid, out, sems
        me, row = lax.axis_index("seq"), lax.axis_index("fsdp")
        self.me, self.row = me, row
        owner = row_owner(seq, fsdp)[1]
        self.stop = owner[1]
        if seq == 4 and fsdp == 8:
            chip, core = row // 2, lax.rem(row, 2)
            self.slot = lax.rem(owner[0], 2)
            self.takes = lax.rem(me, 2) == core
            self.items = [(turn(chip, k, me // 2), turn(chip, k, me // 2) * 2 + k) for k in (0, 1)]
            self.origin = turn(chip, core, me // 2) * 2 + lax.rem(me, 2)
        else:
            ratio = fsdp // seq
            self.slot = me
            self.takes = me == lax.rem(row, seq)
            self.items = [(k, k * ratio + row // seq) for k in range(seq)]
            self.origin = lax.rem(row, ratio) * seq + me

    def plane(self):
        return push(self.own, self.mid.at[self.slot], self.sems, 0, self.stop, "seq", self.slot)

    def plane_local(self):
        return pltpu.make_async_copy(self.own, self.mid.at[self.slot], self.sems[2].at[0])

    def start_plane(self):
        @pl.when(self.me != self.stop)
        def _():
            self.plane().start()

        @pl.when(self.me == self.stop)
        def _():
            self.plane_local().start()

    def finish_plane(self):
        @pl.when(self.me != self.stop)
        def _():
            self.plane().wait_send()

        @pl.when(self.me == self.stop)
        def _():
            self.plane_local().wait()

        @pl.when(self.takes)
        def _():
            for k, (column, _) in enumerate(self.items):

                @pl.when(column != self.me)
                def _(k=k, column=column):
                    push(self.own, self.mid.at[k], self.sems, 0, column, "seq", k).wait_recv()

    def line(self, k, row):
        return push(self.mid.at[k], self.out, self.sems, k, row, "fsdp", len(self.items))

    def each_line(self, remote, local):
        @pl.when(self.takes)
        def _():
            for k, (_, row) in enumerate(self.items):

                @pl.when(row != self.row)
                def _(k=k, row=row):
                    remote(self.line(k, row))

                @pl.when(row == self.row)
                def _(k=k):
                    local(pltpu.make_async_copy(self.mid.at[k], self.out, self.sems[2].at[0]))

    def start_line(self):
        self.each_line(lambda copy: copy.start(), lambda copy: copy.start())

    def finish_line(self):
        @pl.when(self.origin != self.row)
        def _():
            self.line(0, self.origin).wait_recv()

        self.each_line(lambda copy: copy.wait_send(), lambda copy: copy.wait())


def home_count(seq, fsdp):
    return 2 if seq == 4 and fsdp == 8 else seq


def home_sems(seq, fsdp):
    dma = pltpu.SemaphoreType.DMA
    count = home_count(seq, fsdp)
    return [dma((count,)), dma((count + 1,)), dma((1,))]


def chips(row):
    chip, core = row // 2, lax.rem(row, 2)
    pair = chip // 2
    mate = pair * 2 + 1 - lax.rem(chip, 2)
    first = (1 - pair) * 2
    return chip, core, mate, first, first + 1


def inner_chip(chip):
    return jnp.logical_or(chip == 1, chip == 2)


def line_scratch(fsdp):
    dma = pltpu.SemaphoreType.DMA
    return [dma((max(fsdp, 9),)), dma((max(fsdp, 8),)), dma((1,))]


class LineGather:
    def __init__(self, fsdp, own, whole, sems, part=None, bounce=None):
        self.fsdp, self.own, self.whole, self.sems = fsdp, own, whole, sems
        self.bounce = bounce
        if part is not None:
            self.own, self.whole = own.at[part], whole.at[:, part]
        self.row = lax.axis_index("fsdp")
        if fsdp == 8:
            self.chip, self.core, self.mate, self.one, self.two = chips(self.row)
            self.near = 2 - self.chip // 2

    def at(self, chip):
        return chip * 2 + self.core

    def send(self, slot, index, peer, own=False):
        src = self.own if own else self.whole.at[slot]
        return push(src, self.whole.at[slot], self.sems, index, peer, "fsdp", slot)

    def arrive(self, slot):
        self.send(slot, 0, self.row).wait_recv()

    def local(self):
        src = self.own if self.bounce is None else self.bounce
        return pltpu.make_async_copy(src, self.whole.at[self.row], self.sems[2].at[0])

    def start_local(self):
        if self.bounce is None:
            self.local().start()
        else:
            pltpu.make_async_copy(self.own, self.bounce, self.sems[2].at[0]).start()

    def settle(self):
        if self.bounce is not None:
            pltpu.make_async_copy(self.own, self.bounce, self.sems[2].at[0]).wait()
            self.local().start()

    def sibling(self, chip, index):
        return self.send(self.at(chip), index, self.chip * 2 + 1 - self.core)

    def start(self):
        if self.fsdp != 8:
            for step in range(1, self.fsdp):
                peer = lax.rem(self.row + step, self.fsdp)
                self.send(self.row, step - 1, peer, own=True).start()
        else:
            self.send(self.row, 1, self.at(self.near), own=True).start()
            self.send(self.row, 0, self.at(self.mate), own=True).start()
            self.send(self.row, 2, self.chip * 2 + 1 - self.core, own=True).start()
        self.start_local()

    def pass_on(self, index, chip):
        self.arrive(self.at(chip))

        @pl.when(inner_chip(self.chip))
        def _():
            self.send(self.at(chip), index, self.at(self.mate)).start()

        self.sibling(chip, index + 3).start()

    def forward(self):
        self.settle()
        if self.fsdp == 8:

            @pl.when(inner_chip(self.chip))
            def _():
                self.pass_on(3, self.one)
                self.pass_on(4, self.two)

    def finish(self):
        if self.fsdp != 8:
            for step in range(1, self.fsdp):
                self.arrive(lax.rem(self.row - step + self.fsdp, self.fsdp))
            for step in range(1, self.fsdp):
                self.send(self.row, step - 1, self.row, own=True).wait_send()
            self.local().wait()
            return
        self.arrive(self.at(self.mate))
        self.sibling(self.mate, 5).start()

        @pl.when(jnp.logical_not(inner_chip(self.chip)))
        def _():
            self.pass_on(3, self.one)
            self.pass_on(4, self.two)

        for chip in range(4):
            self.arrive(chip * 2 + 1 - self.core)
        self.local().wait()
        for index in range(3):
            self.send(self.row, index, self.row, own=True).wait_send()
        for index, chip in ((5, self.mate), (6, self.one), (7, self.two)):
            self.sibling(chip, index).wait_send()

        @pl.when(inner_chip(self.chip))
        def _():
            self.send(self.at(self.one), 3, self.row).wait_send()
            self.send(self.at(self.two), 4, self.row).wait_send()


def mine_scratch(fsdp, height, width):
    count = 4 if fsdp == 8 else 1
    return [pltpu.VMEM((count, height, width), BF16), pltpu.SemaphoreType.DMA((count,))]


def reduce_scratch(fsdp, height, width):
    if fsdp == 8:
        bufs = [pltpu.VMEM((4, height, width), BF16)] * 2
    else:
        bufs = [pltpu.VMEM((1, 16, 128), BF16), pltpu.VMEM((fsdp - 1, height, width), BF16)]
    return bufs + line_scratch(fsdp)


class LineReduce:
    def __init__(self, fsdp, grad, pair, got, *sems, mine=None):
        self.fsdp, self.grad, self.pair, self.got, self.sems = fsdp, grad, pair, got, sems
        self.row = lax.axis_index("fsdp")
        if fsdp == 8:
            self.chip, self.core, self.mate, self.one, self.two = chips(self.row)
            self.roles = [self.one, self.two, self.mate, self.chip]
            self.own = [role * 2 + self.core for role in self.roles]
        else:
            self.own = [self.row]
        self.mine = mine

    def fetch(self, role):
        return pltpu.make_async_copy(
            self.grad.at[self.own[role]], self.mine[0].at[role], self.mine[1].at[role]
        )

    def block(self, role, part):
        if self.mine is not None:
            return self.mine[0][role, part].astype(F32)
        return self.grad[self.own[role], part].astype(F32)

    def ready(self, role):
        if self.mine is not None:
            self.fetch(role).wait()

    def rows(self, task):
        height = self.grad.shape[1]
        step = 64
        while height % step:
            step //= 2
        each(height, step, lambda at: task(pl.ds(at, step)))

    def across(self, role):
        other = 1 - self.core
        return push(
            self.grad.at[self.roles[role] * 2 + other],
            self.pair.at[role],
            self.sems,
            role,
            self.chip * 2 + other,
            "fsdp",
        )

    def to_mate(self, role):
        slot = (1, 2, 0)[role]
        return push(
            self.pair.at[role],
            self.got.at[slot],
            self.sems,
            4 + slot,
            self.mate * 2 + self.core,
            "fsdp",
        )

    def to_other(self, role):
        return push(
            self.pair.at[role],
            self.got.at[3],
            self.sems,
            7 + role,
            self.roles[role] * 2 + self.core,
            "fsdp",
            7,
        )

    def direct(self, step):
        peer = lax.rem(self.row + step, self.fsdp)
        return push(
            self.grad.at[peer], self.got.at[step - 1], self.sems, step - 1, peer, "fsdp"
        )

    def start(self):
        if self.fsdp != 8:
            for step in range(1, self.fsdp):
                self.direct(step).start()
        else:
            for role in range(4):
                self.across(role).start()
        if self.mine is not None:
            for role in range(len(self.own)):
                self.fetch(role).start()

    def pairs(self):
        if self.fsdp != 8:
            return
        for role in range(3):
            self.across(role).wait_recv()
            self.ready(role)

            def add(part, role=role):
                self.pair[role, part] = (
                    self.pair[role, part].astype(F32) + self.block(role, part)
                ).astype(BF16)

            self.rows(add)
            if role < 2:

                @pl.when(jnp.logical_not(inner_chip(self.chip)))
                def _(role=role):
                    self.to_mate(role).start()
            else:
                self.to_mate(role).start()

    def forward(self, roles=(0, 1)):
        if self.fsdp != 8:
            return

        @pl.when(inner_chip(self.chip))
        def _():
            for role in roles:
                self.to_mate(role).wait_recv()

                def add(part, role=role):
                    self.pair[role, part] = (
                        self.pair[role, part].astype(F32) + self.got[role + 1, part].astype(F32)
                    ).astype(BF16)

                self.rows(add)
                self.to_other(role).start()

    def finish(self, out, offset=0):
        height = self.grad.shape[1]
        if offset or out.shape[0] != height:
            out = out.at[pl.ds(offset, height)]
        if self.fsdp != 8:
            for step in range(1, self.fsdp):
                self.direct(step).wait_recv()

            self.ready(0)

            def total(part):
                value = self.block(0, part)
                for step in range(1, self.fsdp):
                    value = value + self.got[step - 1, part].astype(F32)
                out[part, :] = value.astype(out.dtype)

            self.rows(total)
            for step in range(1, self.fsdp):
                self.direct(step).wait_send()
            return
        self.across(3).wait_recv()
        self.to_mate(2).wait_recv()
        self.to_other(0).wait_recv()
        self.ready(3)

        def total(part):
            out[part, :] = (
                self.block(3, part)
                + self.pair[3, part].astype(F32)
                + self.got[0, part].astype(F32)
                + self.got[3, part].astype(F32)
            ).astype(out.dtype)

        self.rows(total)
        for role in range(4):
            self.across(role).wait_send()
        self.to_mate(2).wait_send()

        @pl.when(inner_chip(self.chip))
        def _():
            self.to_other(0).wait_send()
            self.to_other(1).wait_send()

        @pl.when(jnp.logical_not(inner_chip(self.chip)))
        def _():
            self.to_mate(0).wait_send()
            self.to_mate(1).wait_send()


def n_copies(size):
    return 6 if size == 4 else size - 1


class Gather:
    def __init__(self, size, own, whole, sems):
        self.size, self.own, self.whole, self.sems = size, own, whole, sems
        self.me = lax.axis_index("seq")
        self.peers = others(size)
        self.rows = own.shape[0]

    def place(self, device, half=None):
        count = self.rows // 2 if half is not None else self.rows
        at = device * self.rows + (count if half else 0)
        return self.whole.at[pl.ds(pl.multiple_of(at, count), count)]

    def copy(self, index):
        me, own, sems = self.me, self.own, self.sems
        if self.size != 4:
            return push(own, self.place(me), sems, index, self.peers[index])
        side, over, _ = self.peers
        count = self.rows // 2
        one, two = pl.ds(0, count), pl.ds(count, count)
        src, dst, peer = [
            (own.at[one], self.place(me, 0), side),
            (own.at[two], self.place(me, 1), side),
            (own.at[two], self.place(me, 1), over),
            (own.at[one], self.place(me, 0), over),
            (self.place(side, 0), self.place(side, 0), over),
            (self.place(over, 1), self.place(over, 1), side),
        ][index]
        return push(src, dst, sems, index, peer)

    def local(self, sem):
        return pltpu.make_async_copy(self.own, self.place(self.me), sem)

    def start(self):
        for index in (0, 2, 1, 3) if self.size == 4 else range(self.size - 1):
            self.copy(index).start()

    def forward(self):
        if self.size == 4:
            for index in (0, 2):
                self.copy(index).wait_recv()
            self.copy(4).start()
            self.copy(5).start()

    def order(self):
        if self.size == 4:
            return [(self.peers[0], (1,)), (self.peers[1], (3,)), (self.peers[2], (4, 5))]
        return [
            (lax.rem(self.me - k - 1 + self.size, self.size), (k,)) for k in range(self.size - 1)
        ]

    def coming(self, index):
        if self.size == 4:
            return flip(self.me // 2, index // 2) * 2 + flip(
                lax.rem(self.me, 2), lax.rem(index, 2)
            )
        return lax.rem(self.me - index + self.size, self.size)

    def arrive(self, number):
        for index in self.order()[number - 1][1]:
            self.copy(index).wait_recv()

    def sent(self):
        for index in range(n_copies(self.size)):
            self.copy(index).wait_send()

    def finish(self, task=None):
        for number, (device, _) in enumerate(self.order()):
            self.arrive(number + 1)
            if task is not None:
                task(device)
        self.sent()


def scatter_scratch(size, rows, width):
    small = size == 4
    return [
        pltpu.VMEM((size, rows, width), BF16),
        pltpu.VMEM((2, rows // 2, width) if small else (1, 16, 128), BF16),
        pltpu.VMEM((2 if small else size - 1, rows, width), BF16),
    ] + [pltpu.SemaphoreType.DMA((n_copies(size),))] * 2


class Scatter:
    def __init__(self, size, held, stage, got, sems):
        self.size, self.held, self.stage, self.got, self.sems = size, held, stage, got, sems
        self.me = lax.axis_index("seq")
        self.peers = others(size)
        half = held.shape[1] // 2
        self.parts = [pl.ds(0, half), pl.ds(half, half)]

    def copy(self, index):
        held, stage, got, sems = self.held, self.stage, self.got, self.sems
        if self.size != 4:
            peer = self.peers[index]
            return push(held.at[peer], got.at[index], sems, index, peer)
        side, over, far = self.peers
        one, two = self.parts
        src, dst, peer = [
            (held.at[far, one], stage.at[0], side),
            (held.at[far, two], stage.at[1], over),
            (held.at[side, one], got.at[0, one], side),
            (held.at[over, two], got.at[1, two], over),
            (held.at[side, two], got.at[0, two], side),
            (held.at[over, one], got.at[1, one], over),
        ][index]
        return push(src, dst, sems, index, peer)

    def sends(self):
        if self.size == 4:
            return [(2, (0, 1)), (0, (2,)), (1, (3,))]
        return [(k, (k,)) for k in range(self.size - 1)]

    def units(self):
        rows = self.held.shape[1]
        return (8, rows // 2) if self.size == 4 else (self.size, rows)

    def unit(self, index):
        if self.size != 4:
            return lax.rem(self.me + index + 1, self.size), 0
        half, k = index // 4, lax.rem(index, 4)
        one, two = 1 - k // 2, 1 - lax.rem(k, 2)
        low, high = one + half * (two - one), two + half * (one - two)
        return flip(self.me // 2, high) * 2 + flip(lax.rem(self.me, 2), low), half

    def unit_made(self, index):
        starts = {0: 0, 1: 2, 4: 1, 5: 3}
        if self.size != 4:
            starts = {k: k for k in range(self.size - 1)}
        for number, copy in starts.items():

            @pl.when(index == number)
            def _(copy=copy):
                self.copy(copy).start()

    def send(self, make, hooks=()):
        hooks = list(hooks)
        for place, indices in self.sends():
            make(self.peers[place], self.held.at[self.peers[place]])
            for index in indices:
                self.copy(index).start()
            run_hook(hooks)
        while hooks:
            run_hook(hooks)

    def forward_one(self, stage, device, half, index):
        if self.size == 4:
            self.copy(stage).wait_recv()
            spot = (device, self.parts[half])
            total = self.held[spot].astype(F32) + self.stage[stage].astype(F32)
            self.held[spot] = total.astype(BF16)
            self.copy(index).start()

    def forward_side(self):
        self.forward_one(1, self.peers[0], 1, 4)

    def forward_over(self):
        self.forward_one(0, self.peers[1], 0, 5)

    def forward(self):
        self.forward_side()
        self.forward_over()

    def finish(self):
        for index in range(n_copies(self.size)):
            if self.size != 4 or index > 1:
                self.copy(index).wait_recv()
        for index in range(n_copies(self.size)):
            self.copy(index).wait_send()

    def terms(self, rows):
        total = self.got[0, rows].astype(F32)
        for k in range(1, self.got.shape[0]):
            total = total + self.got[k, rows].astype(F32)
        return total


def run_hook(hooks):
    if hooks:
        hook = hooks.pop(0)
        if hook is not None:
            hook()


def at_step(index, tasks):
    for number, task in tasks.items():

        @pl.when(index == number)
        def _(task=task):
            task()


def each(count, step, task):
    def run(index, carry):
        task(pl.multiple_of(index * step, step))
        return carry

    lax.fori_loop(0, count // step, run, 0)


class Load:
    def __init__(self, src, dst, sem):
        self.dst, self.waited = dst, False
        self.copy = pltpu.make_async_copy(src, dst, sem)
        self.copy.start()

    def get(self):
        if not self.waited:
            self.waited = True
            self.copy.wait()
        return self.dst


def loads(srcs, dsts, sems):
    return [Load(src, dst, sems.at[k]) for k, (src, dst) in enumerate(zip(srcs, dsts))]


def load_scratch(arrays):
    return [pltpu.VMEM(array.shape, array.dtype) for array in arrays] + [
        pltpu.SemaphoreType.DMA((len(arrays),))
    ]


def tile_of(width, most):
    tile = most
    while width % tile:
        tile //= 2
    return tile


def swap_halves(block):
    half = HEAD_DIM // 2
    return jnp.concatenate([block[:, half:], block[:, :half]], axis=1)


def inv_rms(values):
    return lax.rsqrt(jnp.mean(values * values, axis=-1, keepdims=True) + EPSILON)


def mask_bias(ids_col, ids_row, start, low, rows, span):
    query = start + lax.broadcasted_iota(jnp.int32, (rows, span), 0)
    key = low + lax.broadcasted_iota(jnp.int32, (rows, span), 1)
    same = ids_col[pl.ds(start, rows), :] == ids_row[:, pl.ds(low, span)]
    bias = jnp.where(jnp.logical_and(same, key <= query), 0.0, NEGATIVE)
    return jnp.concatenate([bias, bias], axis=0)


def join_blocks(blocks, seq, whole):
    fsdp = blocks.shape[0]
    ratio = fsdp // seq
    height, width = blocks.shape[1:]
    for down in range(ratio):
        for across in range(seq):
            whole[down * height : (down + 1) * height, across * width : (across + 1) * width] = (
                blocks[line_place(seq, fsdp, down, across)]
            )


def forward_kernel(
    seq, fsdp, hidden, w_qkv, w_out, w_gate, w_up, w_down, cot, ids, gain_one, gain_two, ids_row,
    ids_col, gains, attn, lse, middle, own_normed, normed_out, cosine_out, sine_out, packed_out,
    rows_out_out, cols_qkv_out, cols_gate, cols_up, moved_out, moved_down, cot_all, raw, ids_all,
    gain_own, gain_parts, blocks_out, held, stage, got, normed, cosine, sine, packed, rows_out,
    cols_qkv, own_cot, own_gate, own_up, own_out, own_down, *sems
):
    def take(count):
        nonlocal sems
        taken, sems = sems[:count], sems[count:]
        return taken

    rows, width = hidden.shape
    length = rows * seq
    groups = w_qkv.shape[1] // (4 * HEAD_DIM)
    me, row = lax.axis_index("seq"), lax.axis_index("fsdp")
    to, source = row_owner(seq, fsdp)
    share = gain_one.shape[1]
    tile = tile_of(width, 512)
    gain_own[0:1, :] = gain_one[...].astype(F32)
    gain_own[1:2, :] = gain_two[...].astype(F32)
    gain_parts[row, me] = gain_own[...]
    ids_all[me] = ids[...]
    meet(seq, fsdp, (to, source))
    local, out_sems = take(2)
    stores = []

    def store(src, dst):
        stores.append(pltpu.make_async_copy(src, dst, out_sems.at[len(stores)]))
        stores[-1].start()

    whole = Gather(seq, hidden, raw, take(2))
    cots = Gather(seq, cot, cot_all, take(2))
    sums = Scatter(seq, held, stage, got, take(2))
    half = w_gate.shape[0] // 2
    one, two = pl.ds(0, half), pl.ds(half, half)
    line_qkv = LineGather(fsdp, w_qkv, cols_qkv, take(3))
    line_out = LineGather(fsdp, moved_out, blocks_out, take(3))
    line_gate = [
        LineGather(fsdp, w_gate, cols_gate, take(3), part, own_gate.at[part])
        for part in (one, two)
    ]
    line_up = [
        LineGather(fsdp, w_up, cols_up, take(3), part, own_up.at[part]) for part in (one, two)
    ]
    move_out = Move(w_out, moved_out, to, take(3), own_out)
    move_down = Move(w_down, moved_down, to, take(3), own_down)
    id_sems, gain_sems, wide_sems = take(2), take(2), take(2)
    id_copies = [
        push(ids, ids_all.at[me], id_sems, k, peer) for k, peer in enumerate(others(seq))
    ]
    gain_copies = [
        push(gain_own, gain_parts.at[row, me], gain_sems, k, peer)
        for k, peer in enumerate(others(seq))
    ]
    for copy in id_copies + gain_copies:
        copy.start()
    line_qkv.start()
    whole.start()
    move_out.start()
    mine = whole.local(local.at[0])
    mine.start()
    cot_in = pltpu.make_async_copy(cot, own_cot, local.at[1])
    cot_in.start()
    for copy in gain_copies:
        copy.wait()
    wide = [
        push(
            gain_parts.at[row],
            gain_parts.at[row],
            wide_sems,
            step - 1,
            lax.rem(row + step, fsdp),
            "fsdp",
        )
        for step in range(1, fsdp)
    ]
    for copy in wide:
        copy.start()
    for copy in id_copies:
        copy.wait()
    for k in range(seq):
        for at in range(0, rows, 128):
            piece = ids_all[k, :, at : at + 128]
            ids_row[:, k * rows + at : k * rows + at + 128] = piece
            turned = jnp.transpose(jnp.broadcast_to(piece, (128, 128)))
            ids_col[k * rows + at : k * rows + at + 128, :] = turned[:, :1]
    whole.forward()
    line_qkv.forward()
    for line in line_gate:
        line.start()
    order = lax.broadcasted_iota(jnp.int32, (1, HEAD_DIM // 2), 1).astype(F32)
    inverse = jnp.exp(order * (-2.0 * math.log(ROPE_BASE) / HEAD_DIM))

    def table(at):
        part = pl.ds(at, BLOCK)
        first = jnp.sum(
            (ids_row[...] < ids_col[part, :]).astype(jnp.int32).astype(F32),
            axis=-1,
            keepdims=True,
        )
        place = (at + lax.broadcasted_iota(jnp.int32, (BLOCK, 1), 0)).astype(F32) - first
        angles = place * inverse
        cos, sin = jnp.cos(angles), jnp.sin(angles)
        cosine[part, :] = jnp.concatenate([cos, cos], axis=1)
        sine[part, :] = jnp.concatenate([-sin, sin], axis=1)

    each(length, BLOCK, table)
    for copy in wide:
        copy.wait()
    for r in range(fsdp):
        for k in range(seq):
            at = (r * seq + k) * share
            gains[:, at : at + share] = gain_parts[r, k]
    mine.wait()

    def norm(device):
        base = pl.multiple_of(device * rows, rows)

        def part(at):
            values = raw[pl.ds(base + at, 128), :].astype(F32)
            normed[pl.ds(base + at, 128), :] = (
                values * inv_rms(values) * gains[0:1, :]
            ).astype(BF16)

        each(rows, 128, part)

    norm(me)
    move_out.finish()
    line_out.start()
    whole.finish(norm)
    cots.start()
    cot_in.wait()
    kept = pltpu.make_async_copy(own_cot, cots.place(me), local.at[0])
    kept.start()
    line_out.forward()
    line_gate[0].forward()
    for line in line_up:
        line.start()
    move_down.start()
    store(normed, normed_out)
    store(cosine, cosine_out)
    store(sine, sine_out)
    line_qkv.finish()
    store(cols_qkv, cols_qkv_out)
    for group in range(groups):

        def project(at, group=group):
            part = pl.ds(at, 512)
            low = group * 4 * HEAD_DIM
            weight = cols_qkv[:, :, low : low + 4 * HEAD_DIM].reshape(width, 4 * HEAD_DIM)
            proj = dot(normed[part, :], weight)
            for slot in range(4):
                piece = proj[:, slot * HEAD_DIM : (slot + 1) * HEAD_DIM]
                if slot < 3:
                    piece = piece * cosine[part, :] + swap_halves(piece) * sine[part, :]
                packed[group * 4 + slot, part, :] = piece.astype(BF16)

        each(length, 512, project)
    store(packed, packed_out)
    line_out.finish()
    join_blocks(blocks_out, seq, rows_out)
    store(rows_out, rows_out_out)
    hooks = {
        0: line_gate[1].forward,
        1: cots.forward,
        3: line_up[0].forward,
        5: sums.forward_over,
        6: line_up[1].forward,
    }
    count, unit_rows = sums.units()
    span = length // 2 + unit_rows

    def unit(index):
        device, half = sums.unit(index)
        start = pl.multiple_of(device * rows + half * unit_rows, unit_rows)
        low = pl.multiple_of(jnp.maximum(start - length // 2, 0), unit_rows)
        part, keys = pl.ds(start, unit_rows), pl.ds(low, span)
        spot = pl.ds(pl.multiple_of(half * unit_rows, unit_rows), unit_rows)
        bias = mask_bias(ids_col, ids_row, start, low, unit_rows, span)
        mixed, logs = [], []
        for group in range(groups):
            queries = jnp.concatenate(
                [packed[group * 4, part, :], packed[group * 4 + 1, part, :]], axis=0
            )
            scores = dot_nt(queries, packed[group * 4 + 2, keys, :]) * SCALE_TWO + bias
            most = jnp.max(scores, axis=-1, keepdims=True)
            grown = jnp.exp2(scores - most)
            total = jnp.sum(grown, axis=-1, keepdims=True)
            weights = (grown * (1.0 / total)).astype(BF16)
            out = dot(weights, packed[group * 4 + 3, keys, :])
            log_total = most + jnp.log2(total)
            mixed += [out[:unit_rows], out[unit_rows:]]
            logs += [log_total[:unit_rows], log_total[unit_rows:]]
        attn[part, :] = jnp.concatenate(mixed, axis=1).astype(BF16)
        lane = lax.broadcasted_iota(jnp.int32, (unit_rows, 128), 1)
        stats = jnp.zeros((unit_rows, 128), F32)
        for head, log_total in enumerate(logs):
            stats = jnp.where(lane == head, log_total, stats)
        lse[part, :] = stats

        def onward(at):
            cols = pl.ds(at, tile)
            term = dot(attn[part, :], rows_out[:, cols])

            @pl.when(device == me)
            def _():
                middle[spot, cols] = raw[part, cols].astype(F32) + term

            @pl.when(device != me)
            def _():
                held[device, spot, cols] = term.astype(BF16)

        each(width, tile, onward)
        sums.unit_made(index)
        for number, hook in hooks.items():

            @pl.when(index == number)
            def _(hook=hook):
                hook()

    each(count, 1, unit)
    sums.forward_side()
    cots.finish()
    kept.wait()
    line_gate[0].finish()
    line_gate[1].finish()
    line_up[0].finish()
    sums.finish()

    def second(at):
        part = pl.ds(at, 128)
        values = middle[part, :] + sums.terms(part)
        middle[part, :] = values
        own_normed[part, :] = (values * inv_rms(values) * gains[1:2, :]).astype(BF16)

    each(rows, 128, second)
    line_up[1].finish()
    move_down.finish()
    for copy in stores:
        copy.wait()


def forward(seq, fsdp, hidden, w_qkv, w_out, w_gate, w_up, w_down, cot, ids, gain_one, gain_two):
    rows, width = hidden.shape
    length = rows * seq
    dma = pltpu.SemaphoreType.DMA
    share = gain_one.shape[1]
    groups = w_qkv.shape[1] // (4 * HEAD_DIM)
    inner = groups * 2 * HEAD_DIM
    return pl.pallas_call(
        functools.partial(forward_kernel, seq, fsdp),
        out_shape=(
            shape((1, length), jnp.int32),
            shape((length, 1), jnp.int32),
            shape((2, width), F32),
            shape((length, inner), BF16),
            shape((length, 128), F32),
            shape((rows, width), F32),
            shape((rows, width), BF16),
            shape((length, width), BF16),
            shape((length, HEAD_DIM), F32),
            shape((length, HEAD_DIM), F32),
            shape((groups * 4, length, HEAD_DIM), BF16),
            shape((inner, width), BF16),
            shape((fsdp,) + w_qkv.shape, BF16),
            shape((fsdp,) + w_gate.shape, BF16),
            shape((fsdp,) + w_up.shape, BF16),
            shape(w_out.shape, BF16),
            shape(w_down.shape, BF16),
            shape((length, width), BF16),
        ),
        in_specs=[ANY] * 7 + [VMEM] * 3,
        out_specs=(VMEM,) * 7 + (ANY,) * 11,
        scratch_shapes=[
            pltpu.VMEM((length, width), BF16),
            pltpu.VMEM((seq, 1, rows), jnp.int32),
            pltpu.VMEM((2, share), F32),
            pltpu.VMEM((fsdp, seq, 2, share), F32),
            pltpu.VMEM((fsdp,) + w_out.shape, BF16),
        ]
        + scatter_scratch(seq, rows, width)[:3]
        + [
            pltpu.VMEM((length, width), BF16),
            pltpu.VMEM((length, HEAD_DIM), F32),
            pltpu.VMEM((length, HEAD_DIM), F32),
            pltpu.VMEM((groups * 4, length, HEAD_DIM), BF16),
            pltpu.VMEM((inner, width), BF16),
            pltpu.VMEM((fsdp,) + w_qkv.shape, BF16),
            pltpu.VMEM(cot.shape, BF16),
            pltpu.VMEM(w_gate.shape, BF16),
            pltpu.VMEM(w_up.shape, BF16),
            pltpu.VMEM(w_out.shape, BF16),
            pltpu.VMEM(w_down.shape, BF16),
        ]
        + [dma((2,)), dma((6,))]
        + [dma((n_copies(seq),))] * 6
        + line_scratch(fsdp) * 6
        + [dma((1,))] * 6
        + [dma((seq - 1,))] * 4
        + [dma((fsdp - 1,))] * 2,
        compiler_params=params(0),
        name="forward",
    )(hidden, w_qkv, w_out, w_gate, w_up, w_down, cot, ids, gain_one, gain_two)


def feed_kernel(
    seq, fsdp, own_normed, cot_all, w_gate, w_up, middle, w_down, gains, d_middle, own_low, d_gain,
    own_down, out_terms, g_gate, g_up, normed, whole_down, blocks, g_down, gate, up, hid, d_gate,
    d_up, held, stage, got, grad_tiles, *rest
):
    arrays, rest = rest[:5], rest[5:]
    rows, width = middle.shape
    length = rows * seq
    inner = gate.shape[1]
    me = lax.axis_index("seq")
    tile = tile_of(width, 512)
    wide = tile_of(inner, 512)
    w_gate, w_up, cot, middle = loads((w_gate, w_up, cot_all, middle), arrays[:4], arrays[4])
    meet(seq, fsdp)
    local, tile_sems = rest[0], rest[1]
    whole = Gather(seq, own_normed, normed, rest[2:4])
    sums = Scatter(seq, held, stage, got, rest[4:6])
    half = w_down.shape[0] // 2
    line_down = [
        LineGather(fsdp, w_down, blocks, rest[6:9], pl.ds(0, half)),
        LineGather(fsdp, w_down, blocks, rest[9:12], pl.ds(half, half)),
    ]
    early = fsdp == 8
    if not early:
        g_down = blocks
    line = LineReduce(fsdp, g_down, *rest[12:])
    for exchange in line_down:
        exchange.start()
    whole.start()
    mine = whole.local(local.at[0])
    mine.start()
    w_gate, w_up = w_gate.get(), w_up.get()
    mine.wait()

    def block_of(device):
        return pl.ds(pl.multiple_of(device * rows, rows), rows)

    def first(device):
        block = block_of(device)

        def part(at):
            cols = pl.ds(at, wide)
            gate_part = dot(normed[block, :], w_gate[:, cols])
            up_part = dot(normed[block, :], w_up[:, cols])
            gate[block, cols] = gate_part
            up[block, cols] = up_part
            hid[block, cols] = (gate_part / (1.0 + jnp.exp(-gate_part)) * up_part).astype(BF16)

        each(inner, wide, part)

    first(me)
    whole.forward()
    hooks = [line_down[0].forward, line_down[1].forward]

    def arrived(device):
        first(device)
        run_hook(hooks)

    whole.finish(arrived)
    while hooks:
        run_hook(hooks)
    cot, middle = cot.get(), middle.get()
    height, across = g_down.shape[1:]

    def down_grad(k):
        cols = slice(k * across, (k + 1) * across)
        for down in range(fsdp // seq):
            g_down[line_place(seq, fsdp, down, k)] = dot_tn(
                hid[:, down * height : (down + 1) * height], cot[:, cols]
            ).astype(BF16)

    def join_down():
        for exchange in line_down:
            exchange.finish()
        join_blocks(blocks, seq, whole_down)

    if not early:
        join_down()
    for k in range(seq):
        down_grad(k)
    line.start()
    if early:
        join_down()

    def second(device, out):
        block = block_of(device)

        def part(at):
            cols = pl.ds(at, wide)
            d_hid = dot_nt(cot[block, :], whole_down[cols, :])
            gate_part = gate[block, cols]
            sig = 1.0 / (1.0 + jnp.exp(-gate_part))
            d_gate[block, cols] = (
                d_hid * up[block, cols] * sig * (1.0 + gate_part * (1.0 - sig))
            ).astype(BF16)
            d_up[block, cols] = (d_hid * (gate_part * sig)).astype(BF16)

        each(inner, wide, part)

        def term(at):
            cols = pl.ds(at, tile)
            total = dot_nt(d_gate[block, :], w_gate[cols, :]) + dot_nt(
                d_up[block, :], w_up[cols, :]
            )
            out[:, cols] = total.astype(out.dtype)

        each(width, tile, term)

    sums.send(second, [None, line.pairs])
    second(me, d_middle)
    sums.forward()
    line.forward((0,))
    wide_rows = grad_tiles.shape[1]
    for left, grads in ((d_gate, g_gate), (d_up, g_up)):

        def tile_out(index, grads=grads):
            return pltpu.make_async_copy(
                grad_tiles.at[lax.rem(index, 2)],
                grads.at[pl.ds(pl.multiple_of(index * wide_rows, wide_rows), wide_rows)],
                tile_sems.at[lax.rem(index, 2)],
            )

        def job(index, left=left, tile_out=tile_out):
            @pl.when(index >= 2)
            def _():
                tile_out(index - 2).wait()

            at = pl.multiple_of(index * wide_rows, wide_rows)
            grad_tiles[lax.rem(index, 2)] = dot_tn(
                normed[:, pl.ds(at, wide_rows)], left[...]
            ).astype(BF16)
            tile_out(index).start()

        count = width // wide_rows
        each(count, 1, job)
        for index in range(max(0, count - 2), count):
            tile_out(index).wait()
        if left is d_gate:
            line.forward((1,))

    def outward(index):
        block = pl.ds(pl.multiple_of(index * rows, rows), rows)

        def part(at):
            cols = pl.ds(at, tile)
            normed[block, cols] = dot(hid[block, :], whole_down[:, cols]).astype(BF16)

        each(width, tile, part)

    each(seq, 1, outward)
    terms_out = pltpu.make_async_copy(normed, out_terms, local.at[0])
    terms_out.start()
    sums.finish()
    d_gain[...] = jnp.zeros_like(d_gain)
    base = pl.multiple_of(me * rows, rows)

    def norm(at):
        part = pl.ds(at, 128)
        values = middle[part, :]
        grad = d_middle[part, :] + sums.terms(part)
        scale = inv_rms(values)
        weighted = grad * gains[1:2, :]
        mean = jnp.mean(weighted * values, axis=-1, keepdims=True)
        d_gain[...] += jnp.sum(grad * values * scale, axis=0, keepdims=True)
        total = cot[pl.ds(base + at, 128), :].astype(F32) + scale * (
            weighted - values * (scale * scale) * mean
        )
        d_middle[part, :] = total
        own_low[part, :] = total.astype(BF16)

    each(rows, 128, norm)
    line.finish(own_down)
    terms_out.wait()


def feed(seq, fsdp, own_normed, cot_all, w_gate, w_up, middle, w_down, gains):
    rows, width = middle.shape
    length = rows * seq
    inner = w_gate.shape[1]
    dma = pltpu.SemaphoreType.DMA
    return pl.pallas_call(
        functools.partial(feed_kernel, seq, fsdp),
        out_shape=(
            shape((rows, width), F32),
            shape((rows, width), BF16),
            shape((1, width), F32),
            shape(w_down.shape, BF16),
            shape((length, width), BF16),
            shape((width, inner), BF16),
            shape((width, inner), BF16),
        ),
        in_specs=[ANY] * 6 + [VMEM],
        out_specs=(VMEM,) * 4 + (ANY,) * 3,
        scratch_shapes=[
            pltpu.VMEM((length, width), BF16),
            pltpu.VMEM((inner, width), BF16),
            pltpu.VMEM((fsdp,) + w_down.shape, BF16),
            pltpu.VMEM((fsdp,) + w_down.shape if fsdp == 8 else (1, 16, 128), BF16),
            pltpu.VMEM((length, inner), F32),
            pltpu.VMEM((length, inner), F32),
            pltpu.VMEM((length, inner), BF16),
            pltpu.VMEM((length, inner), BF16),
            pltpu.VMEM((length, inner), BF16),
        ]
        + scatter_scratch(seq, rows, width)[:3]
        + [pltpu.VMEM((2, min(512, inner // 2), inner), BF16)]
        + load_scratch((w_gate, w_up, cot_all, middle))
        + [dma((1,)), dma((2,))]
        + [dma((n_copies(seq),))] * 4
        + line_scratch(fsdp) * 2
        + reduce_scratch(fsdp, *w_down.shape),
        compiler_params=params(1),
        name="feed",
    )(own_normed, cot_all, w_gate, w_up, middle, w_down, gains)


def backward_kernel(
    seq, fsdp, own_low, g_gate, g_up, w_out, attn, packed, lse, cosine, sine, w_qkv, hidden,
    d_middle, out_terms, middle, own_down, normed, ids_col, ids_row, gain, gain_two, d_input, output,
    own_qkv, own_gate, own_up, home_down, home_out, g_gain_one, g_gain_two, held_out, stage_out,
    got_out, held, stage, got, d_low, d_keys, d_vals, d_packed, grad_out, grad_qkv, mid_down,
    mid_out, own_out, parts, seq_parts, sums_own, fsdp_parts, *rest
):
    def take(count):
        nonlocal rest
        taken, rest = rest[:count], rest[count:]
        return taken

    rows, width = own_low.shape
    length = rows * seq
    groups = packed.shape[0] // 4
    ratio = fsdp // seq
    height, across = grad_out.shape[1:]
    tile, tall = tile_of(width, 512), tile_of(width, 512)
    me, row = lax.axis_index("seq"), lax.axis_index("fsdp")
    arrays = take(10)
    w_out, attn, packed, lse, cosine, sine, w_qkv, hidden, d_middle = loads(
        (w_out, attn, packed, lse, cosine, sine, w_qkv, hidden, d_middle),
        arrays[:9],
        arrays[9],
    )
    local = take(1)[0]
    terms = Load(out_terms, held_out, local.at[1])
    middle = Load(middle, output, local.at[2])
    meet(seq, fsdp)
    whole = Gather(seq, own_low, d_low, take(2))
    outs = Scatter(seq, held_out, stage_out, got_out, take(2))
    early = seq != 4
    if early:
        held = held_out
    sums = Scatter(seq, held, stage, got, take(2))
    part_sems = take(4)
    size = len(reduce_scratch(fsdp, 16, 128))
    line_gate = LineReduce(fsdp, g_gate, *take(size), mine=take(2))
    line_up = LineReduce(fsdp, g_up, *take(size), mine=take(2))
    line_out = LineReduce(fsdp, grad_out, *take(size))
    line_qkv = LineReduce(fsdp, grad_qkv, *take(size))
    moves = [
        Home(seq, fsdp, own_down, mid_down, home_down, take(3)),
        Home(seq, fsdp, own_out, mid_out, home_out, take(3)),
    ]
    whole.start()
    here = whole.local(local.at[0])
    here.start()
    line_gate.start()
    line_up.start()
    w_out, attn, packed, lse = w_out.get(), attn.get(), packed.get(), lse.get()
    cosine, sine = cosine.get(), sine.get()
    d_keys[...] = jnp.zeros_like(d_keys)
    d_vals[...] = jnp.zeros_like(d_vals)
    line_gate.pairs()
    here.wait()
    span = length // 2 + BLOCK

    def send_out():
        outs.send(lambda device, ref: terms.get())

    def out_grad():
        for k in range(seq):
            part = dot_tn(attn[...], d_low[:, k * across : (k + 1) * across]).astype(BF16)
            for down in range(ratio):
                grad_out[line_place(seq, fsdp, down, k)] = part[
                    down * height : (down + 1) * height
                ]
        line_out.start()

    def attend(index):
        steps = {k: functools.partial(whole.arrive, k) for k in range(1, seq)}
        at_step(index, steps)
        at_step(index, {seq - 1: out_grad})
        start = pl.multiple_of(whole.coming(index) * BLOCK, BLOCK)
        low = pl.multiple_of(jnp.maximum(start - length // 2, 0), BLOCK)
        part, keys = pl.ds(start, BLOCK), pl.ds(low, span)
        d_attn = dot_nt(d_low[part, :], w_out[...]).astype(BF16)
        bias = mask_bias(ids_col, ids_row, start, low, BLOCK, span)
        for group in range(groups):
            base = group * 2 * HEAD_DIM
            queries = jnp.concatenate(
                [packed[group * 4, part, :], packed[group * 4 + 1, part, :]], axis=0
            )
            d_wide = d_attn[:, base : base + 2 * HEAD_DIM]
            product = attn[part, base : base + 2 * HEAD_DIM].astype(F32) * d_wide.astype(F32)
            delta = jnp.concatenate(
                [
                    jnp.sum(product[:, :HEAD_DIM], axis=-1, keepdims=True),
                    jnp.sum(product[:, HEAD_DIM:], axis=-1, keepdims=True),
                ],
                axis=0,
            )
            d_out = jnp.concatenate([d_wide[:, :HEAD_DIM], d_wide[:, HEAD_DIM:]], axis=0)
            logs = jnp.concatenate(
                [
                    lse[part, group * 2 : group * 2 + 1],
                    lse[part, group * 2 + 1 : group * 2 + 2],
                ],
                axis=0,
            )
            key_rows = packed[group * 4 + 2, keys, :]
            scores = dot_nt(queries, key_rows) * SCALE_TWO + bias
            probs = jnp.exp2(scores - logs)
            d_probs = dot_nt(d_out, packed[group * 4 + 3, keys, :])
            d_scores = (probs * (d_probs - delta)).astype(BF16)
            d_vals[group, keys, :] += dot_tn(probs.astype(BF16), d_out)
            d_keys[group, keys, :] += dot_tn(d_scores, queries) * SCALE
            d_query = dot(d_scores, key_rows) * SCALE
            turned = [
                piece * cosine[part, :] - swap_halves(piece) * sine[part, :]
                for piece in (d_query[:BLOCK], d_query[BLOCK:])
            ]
            d_packed[part, group * 4 * HEAD_DIM : group * 4 * HEAD_DIM + 2 * HEAD_DIM] = (
                jnp.concatenate(turned, axis=1).astype(BF16)
            )
            if group == 0:
                at_step(index, {0: whole.forward})

    def passing(index):
        attend(index)
        at_step(
            index,
            {
                0: functools.partial(line_gate.forward, (0,)),
                1: second_step,
                2: third_step,
            },
        )

    def second_step():
        moves[0].start_plane()
        line_up.pairs()
        line_gate.forward((1,))

    def third_step():
        send_out()
        line_up.forward((0,))

    each(seq, 1, passing)
    whole.sent()
    normed = Load(normed, d_low, local.at[3])
    moves[0].finish_plane()
    moves[0].start_line()

    def last(at):
        part = pl.ds(at, BLOCK)
        for group in range(groups):
            d_key = d_keys[group, part, :]
            turned = d_key * cosine[part, :] - swap_halves(d_key) * sine[part, :]
            base = group * 4 * HEAD_DIM + 2 * HEAD_DIM
            d_packed[part, base : base + 2 * HEAD_DIM] = jnp.concatenate(
                [turned, d_vals[group, part, :]], axis=1
            ).astype(BF16)

    each(length, BLOCK, last)
    line_out.pairs()
    normed = normed.get()
    rows_each = grad_qkv.shape[1]

    per = 128 // math.gcd(128, rows_each)

    def weight(index):
        part = pl.ds(pl.multiple_of(index * per * rows_each, per * rows_each), per * rows_each)
        grad = dot_tn(normed[:, part], d_packed[...]).astype(BF16)
        for k in range(per):
            grad_qkv[index * per + k] = grad[k * rows_each : (k + 1) * rows_each]

    each(fsdp // per, 1, weight)
    line_qkv.start()
    w_qkv = w_qkv.get()

    def one(device, at):
        block = pl.ds(pl.multiple_of(device * rows, rows), rows)
        return dot_nt(d_packed[block, :], w_qkv[pl.ds(at, tile), :])

    def term(device, ref):
        def part(at):
            ref[:, pl.ds(at, tile)] = one(device, at).astype(BF16)

        each(width, tile, part)

    def finish_output():
        middle.get()
        outs.finish()

        def total_of(at):
            part = pl.ds(at, 128)
            output[part, :] = (
                output[part, :] + held_out[me, part, :].astype(F32) + outs.terms(part)
            )

        each(rows, 128, total_of)

    if early:
        finish_output()
    sums.send(
        term,
        [outs.forward, functools.partial(line_up.forward, (1,)), line_qkv.pairs],
    )

    def own(at):
        d_input[:, pl.ds(at, tile)] = one(me, at)

    each(width, tile, own)
    hidden, d_middle = hidden.get(), d_middle.get()
    line_out.forward()
    line_gate.finish(own_gate)
    sums.forward()
    line_qkv.forward((0,))
    line_up.finish(own_up)
    if not early:
        finish_output()
    line_out.finish(own_out)
    moves[1].start_plane()
    line_qkv.forward((1,))
    parts[0:1, :] = jnp.zeros((1, width), F32)
    parts[1:2, :] = gain_two[...]
    moves[1].finish_plane()
    moves[1].start_line()
    sums.finish()

    def norm(at):
        part = pl.ds(at, 128)
        values = hidden[part, :].astype(F32)
        grad = d_input[part, :] + sums.terms(part)
        scale = inv_rms(values)
        weighted = grad * gain[0:1, :]
        mean = jnp.mean(weighted * values, axis=-1, keepdims=True)
        parts[0:1, :] += jnp.sum(grad * values * scale, axis=0, keepdims=True)
        d_input[part, :] = d_middle[part, :] + scale * (
            weighted - values * (scale * scale) * mean
        )

    each(rows, 128, norm)
    first = [
        push(parts, seq_parts.at[k], part_sems[:2], k, peer)
        for k, peer in enumerate(others(seq))
    ]
    for copy in first:
        copy.start()
    moves[0].finish_line()
    for copy in first:
        copy.wait()
    total = parts[...]
    for k in range(seq - 1):
        total = total + seq_parts[k]
    sums_own[...] = total
    second = [
        push(
            sums_own,
            fsdp_parts.at[step - 1],
            part_sems[2:],
            step - 1,
            lax.rem(row + step, fsdp),
            "fsdp",
        )
        for step in range(1, fsdp)
    ]
    for copy in second:
        copy.start()
    moves[1].finish_line()
    line_qkv.finish(own_qkv)
    for copy in second:
        copy.wait()
    for step in range(1, fsdp):
        total = total + fsdp_parts[step - 1]
    share = g_gain_one.shape[1]
    turned = pltpu.roll(
        jnp.broadcast_to(total[:, None, :], (2, 8, width)).reshape(16, width),
        lax.rem(width - (row * seq + me) * share, width),
        1,
    )
    g_gain_one[...] = turned[0:1, :share]
    g_gain_two[...] = turned[8:9, :share]


def backward(
    seq, fsdp, own_low, g_gate, g_up, w_out, attn, packed, lse, cosine, sine, normed, w_qkv, hidden,
    d_middle, out_terms, middle, own_down, ids_col, ids_row, gain, gain_two
):
    rows, width = own_low.shape
    length = rows * seq
    inner = attn.shape[1]
    groups = packed.shape[0] // 4
    height, across = inner // (fsdp // seq), width // seq
    share = width // (seq * fsdp)
    shard = (width // fsdp, w_qkv.shape[1])
    count = home_count(seq, fsdp)
    dma = pltpu.SemaphoreType.DMA
    big = (w_out, attn, packed, lse, cosine, sine, w_qkv, hidden, d_middle)
    return pl.pallas_call(
        functools.partial(backward_kernel, seq, fsdp),
        out_shape=(
            shape((rows, width), F32),
            shape((rows, width), F32),
            shape(shard, BF16),
            shape(g_gate.shape[1:], BF16),
            shape(g_up.shape[1:], BF16),
            shape(own_down.shape, BF16),
            shape((height, across), BF16),
            shape((1, share), F32),
            shape((1, share), F32),
        ),
        in_specs=[ANY] * 16 + [VMEM] * 4,
        out_specs=(VMEM,) * 9,
        scratch_shapes=scatter_scratch(seq, rows, width)[:3]
        + [pltpu.VMEM((seq, rows, width) if seq == 4 else (1, 16, 128), BF16)]
        + scatter_scratch(seq, rows, width)[1:3]
        + [pltpu.VMEM((length, width), BF16)]
        + [pltpu.VMEM((groups, length, HEAD_DIM), F32)] * 2
        + [
            pltpu.VMEM((length, groups * 4 * HEAD_DIM), BF16),
            pltpu.VMEM((fsdp, height, across), BF16),
            pltpu.VMEM((fsdp,) + shard, BF16),
            pltpu.VMEM((count,) + own_down.shape, BF16),
            pltpu.VMEM((count, height, across), BF16),
            pltpu.VMEM((height, across), BF16),
            pltpu.VMEM((2, width), F32),
            pltpu.VMEM((seq - 1, 2, width), F32),
            pltpu.VMEM((2, width), F32),
            pltpu.VMEM((fsdp - 1, 2, width), F32),
        ]
        + load_scratch(big)
        + [dma((4,))]
        + [dma((n_copies(seq),))] * 6
        + [dma((seq - 1,))] * 2
        + [dma((fsdp - 1,))] * 2
        + (reduce_scratch(fsdp, *g_gate.shape[1:]) + mine_scratch(fsdp, *g_gate.shape[1:]))
        + (reduce_scratch(fsdp, *g_up.shape[1:]) + mine_scratch(fsdp, *g_up.shape[1:]))
        + reduce_scratch(fsdp, height, across)
        + reduce_scratch(fsdp, *shard)
        + home_sems(seq, fsdp) * 2,
        compiler_params=params(2),
        name="backward",
    )(
        own_low, g_gate, g_up, *big, out_terms, middle, own_down, normed, ids_col, ids_row, gain,
        gain_two,
    )


def widen_kernel(*refs):
    half = len(refs) // 2
    for src, dst in zip(refs[:half], refs[half:]):
        dst[...] = src[...].astype(F32)


def widen(*arrays):
    steps = 4 if all(array.shape[0] % 64 == 0 for array in arrays if array.shape[0] > 1) else 2
    specs = [
        pl.BlockSpec((array.shape[0] // steps, array.shape[1]), lambda i: (i, 0))
        if array.shape[0] > 1
        else pl.BlockSpec(array.shape, lambda i: (0, 0))
        for array in arrays
    ]
    return pl.pallas_call(
        widen_kernel,
        grid=(steps,),
        out_shape=tuple(shape(array.shape, F32) for array in arrays),
        in_specs=specs,
        out_specs=tuple(specs),
        compiler_params=params(),
        name="widen",
    )(*arrays)


def body(
    hidden_in, cotangent, segment_ids, w_qkv, w_out, w_gate, w_up, w_down, gain_attn, gain_mlp
):
    rows, width = hidden_in.shape
    fsdp = lax.axis_size("fsdp")
    seq = lax.axis_size("seq")
    length = rows * seq

    (
        ids_row, ids_col, gains, attn, lse, middle, normed_two, normed_one, cosine, sine, packed,
        rows_out, cols_qkv, cols_gate, cols_up, _, moved_down, cot_all,
    ) = forward(
        seq, fsdp, hidden_in, w_qkv, w_out, w_gate, w_up, w_down, cotangent, segment_ids,
        gain_attn.reshape(1, -1), gain_mlp.reshape(1, -1),
    )
    d_middle, own_low, part_two, own_down, out_terms, g_gate, g_up = feed(
        seq, fsdp, normed_two, cot_all, cols_gate.reshape(width, -1), cols_up.reshape(width, -1),
        middle, moved_down, gains,
    )
    out_terms = out_terms.reshape(seq, rows, width)
    g_up = g_up.reshape((fsdp,) + w_up.shape)
    results = backward(
        seq, fsdp, own_low, g_gate.reshape((fsdp,) + w_gate.shape), g_up, rows_out, attn, packed,
        lse, cosine, sine, normed_one, cols_qkv.reshape(width, -1), hidden_in, d_middle, out_terms,
        middle, own_down, ids_col, ids_row, gains, part_two,
    )
    d_input, output, g_qkv, g_gate, g_up, g_down, g_out, g_gain_one, g_gain_two = widen(*results)
    return (
        output, d_input, g_qkv, g_out, g_gate, g_up, g_down, g_gain_one.reshape(-1),
        g_gain_two.reshape(-1),
    )


def solution(mesh):
    both = P(("fsdp", "seq"), None)
    split = P("fsdp", "seq")
    gain = P(("fsdp", "seq"))
    in_specs = (both, both, split, split, split, split, split, split, gain, gain)
    out_specs = (both, both, split, split, split, split, split, gain, gain)
    return jax.shard_map(body, mesh=mesh, in_specs=in_specs, out_specs=out_specs, check_vma=False)
```

```python
import functools
import math

import jax
import jax.numpy as jnp
from jax import lax
from jax.experimental import pallas as pl
from jax.experimental.pallas import tpu as pltpu
from jax.sharding import PartitionSpec as P

HEAD_DIM = 96
EPSILON = 1e-05
ROPE_BASE = 100000.0
NEGATIVE = -1e30
SCALE = 1.0 / math.sqrt(HEAD_DIM)
SCALE_TWO = SCALE * math.log2(math.e)
MESH = pl.DeviceIdType.MESH
BLOCK = 256
F32 = jnp.float32
BF16 = jnp.bfloat16
ANY = pl.BlockSpec(memory_space=pl.ANY)
VMEM = pl.BlockSpec(memory_space=pltpu.VMEM)


def dot(left, right):
    return jnp.dot(left, right, preferred_element_type=F32)


def dot_nt(left, right):
    return lax.dot_general(left, right, (((1,), (1,)), ((), ())), preferred_element_type=F32)


def dot_tn(left, right):
    return lax.dot_general(left, right, (((0,), (0,)), ((), ())), preferred_element_type=F32)


def shape(dims, kind):
    return jax.ShapeDtypeStruct(dims, kind)


def params(collective=None):
    return pltpu.CompilerParams(
        collective_id=collective,
        has_side_effects=collective is not None,
        vmem_limit_bytes=60 << 20,
    )


def cost(flops, moved):
    return pl.CostEstimate(flops=flops, bytes_accessed=moved, transcendentals=0)


def others(size):
    me = lax.axis_index("seq")
    if size == 4:
        low, high = lax.rem(me, 2), me // 2
        return [high * 2 + 1 - low, (1 - high) * 2 + low, (1 - high) * 2 + 1 - low]
    return [lax.rem(me + step, size) for step in range(1, size)]


def meet(seq, fsdp, pairs=(), ends=True):
    barrier = pltpu.get_barrier_semaphore()
    row = lax.axis_index("fsdp")
    for peer in others(seq):
        pl.semaphore_signal(barrier, inc=1, device_id={"seq": peer}, device_id_type=MESH)
    for step in range(1, fsdp):
        peer = lax.rem(row + step, fsdp)
        pl.semaphore_signal(barrier, inc=1, device_id={"fsdp": peer}, device_id_type=MESH)
    for there in pairs:

        @pl.when(away(there))
        def _(there=there):
            pl.semaphore_signal(
                barrier,
                inc=1,
                device_id={"fsdp": there[0], "seq": there[1]},
                device_id_type=MESH,
            )

    if pairs:

        @pl.when(away(pairs[0]))
        def _():
            pl.semaphore_wait(barrier, seq + fsdp - 2 + len(pairs))

        @pl.when(jnp.logical_not(away(pairs[0])))
        def _():
            pl.semaphore_wait(barrier, seq + fsdp - 2)
    elif ends:
        pl.semaphore_wait(barrier, seq + fsdp - 2)


def away(there):
    return jnp.logical_or(
        there[0] != lax.axis_index("fsdp"), there[1] != lax.axis_index("seq")
    )


def flip(one, two):
    return one + two - 2 * one * two


def turn(chip, core, high):
    return flip(chip // 2, core) * 2 + flip(lax.rem(chip, 2), flip(high, core))


def row_owner(seq, fsdp):
    row, me = lax.axis_index("fsdp"), lax.axis_index("seq")
    if seq == 4 and fsdp == 8:
        chip, core = row // 2, lax.rem(row, 2)
        to = (turn(chip, core, me // 2) * 2 + lax.rem(me, 2), chip)
        first = flip(me // 2, chip // 2)
        high = flip(flip(lax.rem(me, 2), lax.rem(chip, 2)), first)
        return to, (me * 2 + first, high * 2 + core)
    ratio = fsdp // seq
    to = (lax.rem(row, ratio) * seq + me, row // ratio)
    source = (me * ratio + row // seq, lax.rem(row, seq))
    return to, source


def line_place(seq, fsdp, down, across):
    if seq == 4 and fsdp == 8:
        return turn(lax.axis_index("seq"), down, across // 2) * 2 + across % 2
    return down * seq + across


def push(src, dst, sems, index, peer, axis="seq", slot=None):
    return pltpu.make_async_remote_copy(
        src_ref=src,
        dst_ref=dst,
        send_sem=sems[0].at[index],
        recv_sem=sems[1].at[index if slot is None else slot],
        device_id={axis: peer},
        device_id_type=MESH,
    )


class Move:
    def __init__(self, src, dst, to, sems, bounce):
        self.src, self.dst, self.to, self.sems, self.bounce = src, dst, to, sems, bounce
        self.index = 0

    def remote(self):
        return pltpu.make_async_remote_copy(
            src_ref=self.src,
            dst_ref=self.dst,
            send_sem=self.sems[0].at[self.index],
            recv_sem=self.sems[1].at[self.index],
            device_id={"fsdp": self.to[0], "seq": self.to[1]},
            device_id_type=MESH,
        )

    def within(self, last):
        src, dst = (self.bounce, self.dst) if last else (self.src, self.bounce)
        return pltpu.make_async_copy(src, dst, self.sems[2].at[0])

    def start(self):
        @pl.when(away(self.to))
        def _():
            self.remote().start()

        @pl.when(jnp.logical_not(away(self.to)))
        def _():
            self.within(False).start()

    def finish(self):
        @pl.when(away(self.to))
        def _():
            self.remote().wait()

        @pl.when(jnp.logical_not(away(self.to)))
        def _():
            self.within(False).wait()
            self.within(True).start()
            self.within(True).wait()


class Home:
    def __init__(self, seq, fsdp, own, mid, out, sems):
        self.seq, self.fsdp = seq, fsdp
        self.own, self.mid, self.out, self.sems = own, mid, out, sems
        me, row = lax.axis_index("seq"), lax.axis_index("fsdp")
        self.me, self.row = me, row
        owner = row_owner(seq, fsdp)[1]
        self.stop = owner[1]
        if seq == 4 and fsdp == 8:
            chip, core = row // 2, lax.rem(row, 2)
            self.slot = lax.rem(owner[0], 2)
            self.takes = lax.rem(me, 2) == core
            self.items = [(turn(chip, k, me // 2), turn(chip, k, me // 2) * 2 + k) for k in (0, 1)]
            self.origin = turn(chip, core, me // 2) * 2 + lax.rem(me, 2)
        else:
            ratio = fsdp // seq
            self.slot = me
            self.takes = me == lax.rem(row, seq)
            self.items = [(k, k * ratio + row // seq) for k in range(seq)]
            self.origin = lax.rem(row, ratio) * seq + me

    def plane(self):
        return push(self.own, self.mid.at[self.slot], self.sems, 0, self.stop, "seq", self.slot)

    def plane_local(self):
        return pltpu.make_async_copy(self.own, self.mid.at[self.slot], self.sems[2].at[0])

    def start_plane(self):
        @pl.when(self.me != self.stop)
        def _():
            self.plane().start()

        @pl.when(self.me == self.stop)
        def _():
            self.plane_local().start()

    def finish_plane(self):
        @pl.when(self.me != self.stop)
        def _():
            self.plane().wait_send()

        @pl.when(self.me == self.stop)
        def _():
            self.plane_local().wait()

        @pl.when(self.takes)
        def _():
            for k, (column, _) in enumerate(self.items):

                @pl.when(column != self.me)
                def _(k=k, column=column):
                    push(self.own, self.mid.at[k], self.sems, 0, column, "seq", k).wait_recv()

    def line(self, k, row):
        return push(self.mid.at[k], self.out, self.sems, k, row, "fsdp", len(self.items))

    def each_line(self, remote, local):
        @pl.when(self.takes)
        def _():
            for k, (_, row) in enumerate(self.items):

                @pl.when(row != self.row)
                def _(k=k, row=row):
                    remote(self.line(k, row))

                @pl.when(row == self.row)
                def _(k=k):
                    local(pltpu.make_async_copy(self.mid.at[k], self.out, self.sems[2].at[0]))

    def start_line(self):
        self.each_line(lambda copy: copy.start(), lambda copy: copy.start())

    def finish_line(self):
        @pl.when(self.origin != self.row)
        def _():
            self.line(0, self.origin).wait_recv()

        self.each_line(lambda copy: copy.wait_send(), lambda copy: copy.wait())


def home_count(seq, fsdp):
    return 2 if seq == 4 and fsdp == 8 else seq


def home_sems(seq, fsdp):
    dma = pltpu.SemaphoreType.DMA
    count = home_count(seq, fsdp)
    return [dma((count,)), dma((count + 1,)), dma((1,))]


def chips(row):
    chip, core = row // 2, lax.rem(row, 2)
    pair = chip // 2
    mate = pair * 2 + 1 - lax.rem(chip, 2)
    first = (1 - pair) * 2
    return chip, core, mate, first, first + 1


def inner_chip(chip):
    return jnp.logical_or(chip == 1, chip == 2)


def line_scratch(fsdp):
    dma = pltpu.SemaphoreType.DMA
    return [dma((max(fsdp, 9),)), dma((max(fsdp, 8),)), dma((1,))]


class LineGather:
    def __init__(self, fsdp, own, whole, sems, part=None, bounce=None):
        self.fsdp, self.own, self.whole, self.sems = fsdp, own, whole, sems
        self.bounce = bounce
        if part is not None:
            self.own, self.whole = own.at[part], whole.at[:, part]
        self.row = lax.axis_index("fsdp")
        if fsdp == 8:
            self.chip, self.core, self.mate, self.one, self.two = chips(self.row)
            self.near = 2 - self.chip // 2

    def at(self, chip):
        return chip * 2 + self.core

    def send(self, slot, index, peer, own=False):
        src = self.own if own else self.whole.at[slot]
        return push(src, self.whole.at[slot], self.sems, index, peer, "fsdp", slot)

    def arrive(self, slot):
        self.send(slot, 0, self.row).wait_recv()

    def local(self):
        src = self.own if self.bounce is None else self.bounce
        return pltpu.make_async_copy(src, self.whole.at[self.row], self.sems[2].at[0])

    def start_local(self):
        if self.bounce is None:
            self.local().start()
        else:
            pltpu.make_async_copy(self.own, self.bounce, self.sems[2].at[0]).start()

    def settle(self):
        if self.bounce is not None:
            pltpu.make_async_copy(self.own, self.bounce, self.sems[2].at[0]).wait()
            self.local().start()

    def sibling(self, chip, index):
        return self.send(self.at(chip), index, self.chip * 2 + 1 - self.core)

    def start(self):
        if self.fsdp != 8:
            for step in range(1, self.fsdp):
                peer = lax.rem(self.row + step, self.fsdp)
                self.send(self.row, step - 1, peer, own=True).start()
        else:
            self.send(self.row, 1, self.at(self.near), own=True).start()
            self.send(self.row, 0, self.at(self.mate), own=True).start()
            self.send(self.row, 2, self.chip * 2 + 1 - self.core, own=True).start()
        self.start_local()

    def pass_on(self, index, chip):
        self.arrive(self.at(chip))

        @pl.when(inner_chip(self.chip))
        def _():
            self.send(self.at(chip), index, self.at(self.mate)).start()

        self.sibling(chip, index + 3).start()

    def forward(self):
        self.settle()
        if self.fsdp == 8:

            @pl.when(inner_chip(self.chip))
            def _():
                self.pass_on(3, self.one)
                self.pass_on(4, self.two)

    def finish(self):
        if self.fsdp != 8:
            for step in range(1, self.fsdp):
                self.arrive(lax.rem(self.row - step + self.fsdp, self.fsdp))
            for step in range(1, self.fsdp):
                self.send(self.row, step - 1, self.row, own=True).wait_send()
            self.local().wait()
            return
        self.arrive(self.at(self.mate))
        self.sibling(self.mate, 5).start()

        @pl.when(jnp.logical_not(inner_chip(self.chip)))
        def _():
            self.pass_on(3, self.one)
            self.pass_on(4, self.two)

        for chip in range(4):
            self.arrive(chip * 2 + 1 - self.core)
        self.local().wait()
        for index in range(3):
            self.send(self.row, index, self.row, own=True).wait_send()
        for index, chip in ((5, self.mate), (6, self.one), (7, self.two)):
            self.sibling(chip, index).wait_send()

        @pl.when(inner_chip(self.chip))
        def _():
            self.send(self.at(self.one), 3, self.row).wait_send()
            self.send(self.at(self.two), 4, self.row).wait_send()


def mine_scratch(fsdp, height, width):
    count = 4 if fsdp == 8 else 1
    return [pltpu.VMEM((count, height, width), BF16), pltpu.SemaphoreType.DMA((count,))]


def reduce_scratch(fsdp, height, width):
    if fsdp == 8:
        bufs = [pltpu.VMEM((4, height, width), BF16)] * 2
    else:
        bufs = [pltpu.VMEM((1, 16, 128), BF16), pltpu.VMEM((fsdp - 1, height, width), BF16)]
    return bufs + line_scratch(fsdp)


class LineReduce:
    def __init__(self, fsdp, grad, pair, got, *sems, mine=None):
        self.fsdp, self.grad, self.pair, self.got, self.sems = fsdp, grad, pair, got, sems
        self.row = lax.axis_index("fsdp")
        if fsdp == 8:
            self.chip, self.core, self.mate, self.one, self.two = chips(self.row)
            self.roles = [self.one, self.two, self.mate, self.chip]
            self.own = [role * 2 + self.core for role in self.roles]
        else:
            self.own = [self.row]
        self.mine = mine

    def fetch(self, role):
        return pltpu.make_async_copy(
            self.grad.at[self.own[role]], self.mine[0].at[role], self.mine[1].at[role]
        )

    def block(self, role, part):
        if self.mine is not None:
            return self.mine[0][role, part].astype(F32)
        return self.grad[self.own[role], part].astype(F32)

    def ready(self, role):
        if self.mine is not None:
            self.fetch(role).wait()

    def rows(self, task):
        height = self.grad.shape[1]
        step = 64
        while height % step:
            step //= 2
        each(height, step, lambda at: task(pl.ds(at, step)))

    def across(self, role):
        other = 1 - self.core
        return push(
            self.grad.at[self.roles[role] * 2 + other],
            self.pair.at[role],
            self.sems,
            role,
            self.chip * 2 + other,
            "fsdp",
        )

    def to_mate(self, role):
        slot = (1, 2, 0)[role]
        return push(
            self.pair.at[role],
            self.got.at[slot],
            self.sems,
            4 + slot,
            self.mate * 2 + self.core,
            "fsdp",
        )

    def to_other(self, role):
        return push(
            self.pair.at[role],
            self.got.at[3],
            self.sems,
            7 + role,
            self.roles[role] * 2 + self.core,
            "fsdp",
            7,
        )

    def direct(self, step):
        peer = lax.rem(self.row + step, self.fsdp)
        return push(
            self.grad.at[peer], self.got.at[step - 1], self.sems, step - 1, peer, "fsdp"
        )

    def start(self):
        if self.fsdp != 8:
            for step in range(1, self.fsdp):
                self.direct(step).start()
        else:
            for role in range(4):
                self.across(role).start()
        if self.mine is not None:
            for role in range(len(self.own)):
                self.fetch(role).start()

    def pairs(self):
        if self.fsdp != 8:
            return
        for role in range(3):
            self.across(role).wait_recv()
            self.ready(role)

            def add(part, role=role):
                self.pair[role, part] = (
                    self.pair[role, part].astype(F32) + self.block(role, part)
                ).astype(BF16)

            self.rows(add)
            if role < 2:

                @pl.when(jnp.logical_not(inner_chip(self.chip)))
                def _(role=role):
                    self.to_mate(role).start()
            else:
                self.to_mate(role).start()

    def forward(self, roles=(0, 1)):
        if self.fsdp != 8:
            return

        @pl.when(inner_chip(self.chip))
        def _():
            for role in roles:
                self.to_mate(role).wait_recv()

                def add(part, role=role):
                    self.pair[role, part] = (
                        self.pair[role, part].astype(F32) + self.got[role + 1, part].astype(F32)
                    ).astype(BF16)

                self.rows(add)
                self.to_other(role).start()

    def finish(self, out, offset=0):
        height = self.grad.shape[1]
        if offset or out.shape[0] != height:
            out = out.at[pl.ds(offset, height)]
        if self.fsdp != 8:
            for step in range(1, self.fsdp):
                self.direct(step).wait_recv()

            self.ready(0)

            def total(part):
                value = self.block(0, part)
                for step in range(1, self.fsdp):
                    value = value + self.got[step - 1, part].astype(F32)
                out[part, :] = value.astype(out.dtype)

            self.rows(total)
            for step in range(1, self.fsdp):
                self.direct(step).wait_send()
            return
        self.across(3).wait_recv()
        self.to_mate(2).wait_recv()
        self.to_other(0).wait_recv()
        self.ready(3)

        def total(part):
            out[part, :] = (
                self.block(3, part)
                + self.pair[3, part].astype(F32)
                + self.got[0, part].astype(F32)
                + self.got[3, part].astype(F32)
            ).astype(out.dtype)

        self.rows(total)
        for role in range(4):
            self.across(role).wait_send()
        self.to_mate(2).wait_send()

        @pl.when(inner_chip(self.chip))
        def _():
            self.to_other(0).wait_send()
            self.to_other(1).wait_send()

        @pl.when(jnp.logical_not(inner_chip(self.chip)))
        def _():
            self.to_mate(0).wait_send()
            self.to_mate(1).wait_send()


def n_copies(size):
    return 6 if size == 4 else size - 1


class Gather:
    def __init__(self, size, own, whole, sems):
        self.size, self.own, self.whole, self.sems = size, own, whole, sems
        self.me = lax.axis_index("seq")
        self.peers = others(size)
        self.rows = own.shape[0]

    def place(self, device, half=None):
        count = self.rows // 2 if half is not None else self.rows
        at = device * self.rows + (count if half else 0)
        return self.whole.at[pl.ds(pl.multiple_of(at, count), count)]

    def copy(self, index):
        me, own, sems = self.me, self.own, self.sems
        if self.size != 4:
            return push(own, self.place(me), sems, index, self.peers[index])
        side, over, _ = self.peers
        count = self.rows // 2
        one, two = pl.ds(0, count), pl.ds(count, count)
        src, dst, peer = [
            (own.at[one], self.place(me, 0), side),
            (own.at[two], self.place(me, 1), side),
            (own.at[two], self.place(me, 1), over),
            (own.at[one], self.place(me, 0), over),
            (self.place(side, 0), self.place(side, 0), over),
            (self.place(over, 1), self.place(over, 1), side),
        ][index]
        return push(src, dst, sems, index, peer)

    def local(self, sem):
        return pltpu.make_async_copy(self.own, self.place(self.me), sem)

    def start(self):
        for index in (0, 2, 1, 3) if self.size == 4 else range(self.size - 1):
            self.copy(index).start()

    def forward(self):
        if self.size == 4:
            for index in (0, 2):
                self.copy(index).wait_recv()
            self.copy(4).start()
            self.copy(5).start()

    def order(self):
        if self.size == 4:
            return [(self.peers[0], (1,)), (self.peers[1], (3,)), (self.peers[2], (4, 5))]
        return [
            (lax.rem(self.me - k - 1 + self.size, self.size), (k,)) for k in range(self.size - 1)
        ]

    def coming(self, index):
        if self.size == 4:
            return flip(self.me // 2, index // 2) * 2 + flip(
                lax.rem(self.me, 2), lax.rem(index, 2)
            )
        return lax.rem(self.me - index + self.size, self.size)

    def arrive(self, number):
        for index in self.order()[number - 1][1]:
            self.copy(index).wait_recv()

    def sent(self):
        for index in range(n_copies(self.size)):
            self.copy(index).wait_send()

    def finish(self, task=None):
        for number, (device, _) in enumerate(self.order()):
            self.arrive(number + 1)
            if task is not None:
                task(device)
        self.sent()


def scatter_scratch(size, rows, width):
    small = size == 4
    return [
        pltpu.VMEM((size, rows, width), BF16),
        pltpu.VMEM((2, rows // 2, width) if small else (1, 16, 128), BF16),
        pltpu.VMEM((2 if small else size - 1, rows, width), BF16),
    ] + [pltpu.SemaphoreType.DMA((n_copies(size),))] * 2


class Scatter:
    def __init__(self, size, held, stage, got, sems):
        self.size, self.held, self.stage, self.got, self.sems = size, held, stage, got, sems
        self.me = lax.axis_index("seq")
        self.peers = others(size)
        half = held.shape[1] // 2
        self.parts = [pl.ds(0, half), pl.ds(half, half)]

    def copy(self, index):
        held, stage, got, sems = self.held, self.stage, self.got, self.sems
        if self.size != 4:
            peer = self.peers[index]
            return push(held.at[peer], got.at[index], sems, index, peer)
        side, over, far = self.peers
        one, two = self.parts
        src, dst, peer = [
            (held.at[far, one], stage.at[0], side),
            (held.at[far, two], stage.at[1], over),
            (held.at[side, one], got.at[0, one], side),
            (held.at[over, two], got.at[1, two], over),
            (held.at[side, two], got.at[0, two], side),
            (held.at[over, one], got.at[1, one], over),
        ][index]
        return push(src, dst, sems, index, peer)

    def sends(self):
        if self.size == 4:
            return [(2, (0, 1)), (0, (2,)), (1, (3,))]
        return [(k, (k,)) for k in range(self.size - 1)]

    def units(self):
        rows = self.held.shape[1]
        return (8, rows // 2) if self.size == 4 else (self.size, rows)

    def unit(self, index):
        if self.size != 4:
            return lax.rem(self.me + index + 1, self.size), 0
        half, k = index // 4, lax.rem(index, 4)
        one, two = 1 - k // 2, 1 - lax.rem(k, 2)
        low, high = one + half * (two - one), two + half * (one - two)
        return flip(self.me // 2, high) * 2 + flip(lax.rem(self.me, 2), low), half

    def unit_made(self, index):
        starts = {0: 0, 1: 2, 4: 1, 5: 3}
        if self.size != 4:
            starts = {k: k for k in range(self.size - 1)}
        for number, copy in starts.items():

            @pl.when(index == number)
            def _(copy=copy):
                self.copy(copy).start()

    def send(self, make, hooks=()):
        hooks = list(hooks)
        for place, indices in self.sends():
            make(self.peers[place], self.held.at[self.peers[place]])
            for index in indices:
                self.copy(index).start()
            run_hook(hooks)
        while hooks:
            run_hook(hooks)

    def forward_one(self, stage, device, half, index):
        if self.size == 4:
            self.copy(stage).wait_recv()
            spot = (device, self.parts[half])
            total = self.held[spot].astype(F32) + self.stage[stage].astype(F32)
            self.held[spot] = total.astype(BF16)
            self.copy(index).start()

    def forward_side(self):
        self.forward_one(1, self.peers[0], 1, 4)

    def forward_over(self):
        self.forward_one(0, self.peers[1], 0, 5)

    def forward(self):
        self.forward_side()
        self.forward_over()

    def finish(self):
        for index in range(n_copies(self.size)):
            if self.size != 4 or index > 1:
                self.copy(index).wait_recv()
        for index in range(n_copies(self.size)):
            self.copy(index).wait_send()

    def terms(self, rows):
        total = self.got[0, rows].astype(F32)
        for k in range(1, self.got.shape[0]):
            total = total + self.got[k, rows].astype(F32)
        return total


def run_hook(hooks):
    if hooks:
        hook = hooks.pop(0)
        if hook is not None:
            hook()


def at_step(index, tasks):
    for number, task in tasks.items():

        @pl.when(index == number)
        def _(task=task):
            task()


def each(count, step, task):
    def run(index, carry):
        task(pl.multiple_of(index * step, step))
        return carry

    lax.fori_loop(0, count // step, run, 0)


class Load:
    def __init__(self, src, dst, sem):
        self.dst, self.waited = dst, False
        self.copy = pltpu.make_async_copy(src, dst, sem)
        self.copy.start()

    def get(self):
        if not self.waited:
            self.waited = True
            self.copy.wait()
        return self.dst


def loads(srcs, dsts, sems):
    return [Load(src, dst, sems.at[k]) for k, (src, dst) in enumerate(zip(srcs, dsts))]


def load_scratch(arrays):
    return [pltpu.VMEM(array.shape, array.dtype) for array in arrays] + [
        pltpu.SemaphoreType.DMA((len(arrays),))
    ]


def tile_of(width, most):
    tile = most
    while width % tile:
        tile //= 2
    return tile


def swap_halves(block):
    half = HEAD_DIM // 2
    return jnp.concatenate([block[:, half:], block[:, :half]], axis=1)


def inv_rms(values):
    return lax.rsqrt(jnp.mean(values * values, axis=-1, keepdims=True) + EPSILON)


def mask_bias(ids_col, ids_row, start, low, rows, span):
    query = start + lax.broadcasted_iota(jnp.int32, (rows, span), 0)
    key = low + lax.broadcasted_iota(jnp.int32, (rows, span), 1)
    same = ids_col[pl.ds(start, rows), :] == ids_row[:, pl.ds(low, span)]
    bias = jnp.where(jnp.logical_and(same, key <= query), 0.0, NEGATIVE)
    return jnp.concatenate([bias, bias], axis=0)


def join_blocks(blocks, seq, whole):
    fsdp = blocks.shape[0]
    ratio = fsdp // seq
    height, width = blocks.shape[1:]
    for down in range(ratio):
        for across in range(seq):
            whole[down * height : (down + 1) * height, across * width : (across + 1) * width] = (
                blocks[line_place(seq, fsdp, down, across)]
            )


def forward_kernel(
    seq, fsdp, hidden, w_qkv, w_out, w_gate, w_up, w_down, cot, ids, gain_one, gain_two, ids_row,
    ids_col, gains, attn, lse, middle, own_normed, normed_out, cosine_out, sine_out, packed_out,
    rows_out_out, cols_qkv_out, cols_gate, cols_up, moved_out, moved_down, cot_all, raw, ids_all,
    gain_own, gain_parts, blocks_out, held, stage, got, normed, cosine, sine, packed, rows_out,
    cols_qkv, own_cot, own_gate, own_up, own_out, own_down, *sems
):
    def take(count):
        nonlocal sems
        taken, sems = sems[:count], sems[count:]
        return taken

    rows, width = hidden.shape
    length = rows * seq
    groups = w_qkv.shape[1] // (4 * HEAD_DIM)
    me, row = lax.axis_index("seq"), lax.axis_index("fsdp")
    to, source = row_owner(seq, fsdp)
    share = gain_one.shape[1]
    tile = tile_of(width, 512)
    gain_own[0:1, :] = gain_one[...].astype(F32)
    gain_own[1:2, :] = gain_two[...].astype(F32)
    gain_parts[row, me] = gain_own[...]
    ids_all[me] = ids[...]
    meet(seq, fsdp, (to, source))
    local, out_sems = take(2)
    stores = []

    def store(src, dst):
        stores.append(pltpu.make_async_copy(src, dst, out_sems.at[len(stores)]))
        stores[-1].start()

    whole = Gather(seq, hidden, raw, take(2))
    cots = Gather(seq, cot, cot_all, take(2))
    sums = Scatter(seq, held, stage, got, take(2))
    half = w_gate.shape[0] // 2
    one, two = pl.ds(0, half), pl.ds(half, half)
    line_qkv = LineGather(fsdp, w_qkv, cols_qkv, take(3))
    line_out = LineGather(fsdp, moved_out, blocks_out, take(3))
    line_gate = [
        LineGather(fsdp, w_gate, cols_gate, take(3), part, own_gate.at[part])
        for part in (one, two)
    ]
    line_up = [
        LineGather(fsdp, w_up, cols_up, take(3), part, own_up.at[part]) for part in (one, two)
    ]
    move_out = Move(w_out, moved_out, to, take(3), own_out)
    move_down = Move(w_down, moved_down, to, take(3), own_down)
    id_sems, gain_sems, wide_sems = take(2), take(2), take(2)
    id_copies = [
        push(ids, ids_all.at[me], id_sems, k, peer) for k, peer in enumerate(others(seq))
    ]
    gain_copies = [
        push(gain_own, gain_parts.at[row, me], gain_sems, k, peer)
        for k, peer in enumerate(others(seq))
    ]
    for copy in id_copies + gain_copies:
        copy.start()
    line_qkv.start()
    whole.start()
    move_out.start()
    mine = whole.local(local.at[0])
    mine.start()
    cot_in = pltpu.make_async_copy(cot, own_cot, local.at[1])
    cot_in.start()
    for copy in gain_copies:
        copy.wait()
    wide = [
        push(
            gain_parts.at[row],
            gain_parts.at[row],
            wide_sems,
            step - 1,
            lax.rem(row + step, fsdp),
            "fsdp",
        )
        for step in range(1, fsdp)
    ]
    for copy in wide:
        copy.start()
    for copy in id_copies:
        copy.wait()
    for k in range(seq):
        for at in range(0, rows, 128):
            piece = ids_all[k, :, at : at + 128]
            ids_row[:, k * rows + at : k * rows + at + 128] = piece
            turned = jnp.transpose(jnp.broadcast_to(piece, (128, 128)))
            ids_col[k * rows + at : k * rows + at + 128, :] = turned[:, :1]
    whole.forward()
    line_qkv.forward()
    for line in line_gate:
        line.start()
    order = lax.broadcasted_iota(jnp.int32, (1, HEAD_DIM // 2), 1).astype(F32)
    inverse = jnp.exp(order * (-2.0 * math.log(ROPE_BASE) / HEAD_DIM))

    def table(at):
        part = pl.ds(at, BLOCK)
        first = jnp.sum(
            (ids_row[...] < ids_col[part, :]).astype(jnp.int32).astype(F32),
            axis=-1,
            keepdims=True,
        )
        place = (at + lax.broadcasted_iota(jnp.int32, (BLOCK, 1), 0)).astype(F32) - first
        angles = place * inverse
        cos, sin = jnp.cos(angles), jnp.sin(angles)
        cosine[part, :] = jnp.concatenate([cos, cos], axis=1)
        sine[part, :] = jnp.concatenate([-sin, sin], axis=1)

    each(length, BLOCK, table)
    for copy in wide:
        copy.wait()
    for r in range(fsdp):
        for k in range(seq):
            at = (r * seq + k) * share
            gains[:, at : at + share] = gain_parts[r, k]
    mine.wait()

    def norm(device):
        base = pl.multiple_of(device * rows, rows)

        def part(at):
            values = raw[pl.ds(base + at, 128), :].astype(F32)
            normed[pl.ds(base + at, 128), :] = (
                values * inv_rms(values) * gains[0:1, :]
            ).astype(BF16)

        each(rows, 128, part)

    norm(me)
    move_out.finish()
    line_out.start()
    whole.finish(norm)
    cots.start()
    cot_in.wait()
    kept = pltpu.make_async_copy(own_cot, cots.place(me), local.at[0])
    kept.start()
    line_out.forward()
    line_gate[0].forward()
    for line in line_up:
        line.start()
    move_down.start()
    store(normed, normed_out)
    store(cosine, cosine_out)
    store(sine, sine_out)
    line_qkv.finish()
    store(cols_qkv, cols_qkv_out)
    for group in range(groups):

        def project(at, group=group):
            part = pl.ds(at, 512)
            low = group * 4 * HEAD_DIM
            weight = cols_qkv[:, :, low : low + 4 * HEAD_DIM].reshape(width, 4 * HEAD_DIM)
            proj = dot(normed[part, :], weight)
            for slot in range(4):
                piece = proj[:, slot * HEAD_DIM : (slot + 1) * HEAD_DIM]
                if slot < 3:
                    piece = piece * cosine[part, :] + swap_halves(piece) * sine[part, :]
                packed[group * 4 + slot, part, :] = piece.astype(BF16)

        each(length, 512, project)
    store(packed, packed_out)
    line_out.finish()
    join_blocks(blocks_out, seq, rows_out)
    store(rows_out, rows_out_out)
    hooks = {
        0: line_gate[1].forward,
        1: cots.forward,
        3: line_up[0].forward,
        5: sums.forward_over,
        6: line_up[1].forward,
    }
    count, unit_rows = sums.units()
    span = length // 2 + unit_rows

    def unit(index):
        device, half = sums.unit(index)
        start = pl.multiple_of(device * rows + half * unit_rows, unit_rows)
        low = pl.multiple_of(jnp.maximum(start - length // 2, 0), unit_rows)
        part, keys = pl.ds(start, unit_rows), pl.ds(low, span)
        spot = pl.ds(pl.multiple_of(half * unit_rows, unit_rows), unit_rows)
        bias = mask_bias(ids_col, ids_row, start, low, unit_rows, span)
        mixed, logs = [], []
        for group in range(groups):
            queries = jnp.concatenate(
                [packed[group * 4, part, :], packed[group * 4 + 1, part, :]], axis=0
            )
            scores = dot_nt(queries, packed[group * 4 + 2, keys, :]) * SCALE_TWO + bias
            most = jnp.max(scores, axis=-1, keepdims=True)
            grown = jnp.exp2(scores - most)
            total = jnp.sum(grown, axis=-1, keepdims=True)
            weights = (grown * (1.0 / total)).astype(BF16)
            out = dot(weights, packed[group * 4 + 3, keys, :])
            log_total = most + jnp.log2(total)
            mixed += [out[:unit_rows], out[unit_rows:]]
            logs += [log_total[:unit_rows], log_total[unit_rows:]]
        attn[part, :] = jnp.concatenate(mixed, axis=1).astype(BF16)
        lane = lax.broadcasted_iota(jnp.int32, (unit_rows, 128), 1)
        stats = jnp.zeros((unit_rows, 128), F32)
        for head, log_total in enumerate(logs):
            stats = jnp.where(lane == head, log_total, stats)
        lse[part, :] = stats

        def onward(at):
            cols = pl.ds(at, tile)
            term = dot(attn[part, :], rows_out[:, cols])

            @pl.when(device == me)
            def _():
                middle[spot, cols] = raw[part, cols].astype(F32) + term

            @pl.when(device != me)
            def _():
                held[device, spot, cols] = term.astype(BF16)

        each(width, tile, onward)
        sums.unit_made(index)
        for number, hook in hooks.items():

            @pl.when(index == number)
            def _(hook=hook):
                hook()

    each(count, 1, unit)
    sums.forward_side()
    cots.finish()
    kept.wait()
    line_gate[0].finish()
    line_gate[1].finish()
    line_up[0].finish()
    sums.finish()

    def second(at):
        part = pl.ds(at, 128)
        values = middle[part, :] + sums.terms(part)
        middle[part, :] = values
        own_normed[part, :] = (values * inv_rms(values) * gains[1:2, :]).astype(BF16)

    each(rows, 128, second)
    line_up[1].finish()
    move_down.finish()
    for copy in stores:
        copy.wait()


def forward(seq, fsdp, hidden, w_qkv, w_out, w_gate, w_up, w_down, cot, ids, gain_one, gain_two):
    rows, width = hidden.shape
    length = rows * seq
    dma = pltpu.SemaphoreType.DMA
    share = gain_one.shape[1]
    groups = w_qkv.shape[1] // (4 * HEAD_DIM)
    inner = groups * 2 * HEAD_DIM
    return pl.pallas_call(
        functools.partial(forward_kernel, seq, fsdp),
        out_shape=(
            shape((1, length), jnp.int32),
            shape((length, 1), jnp.int32),
            shape((2, width), F32),
            shape((length, inner), BF16),
            shape((length, 128), F32),
            shape((rows, width), F32),
            shape((rows, width), BF16),
            shape((length, width), BF16),
            shape((length, HEAD_DIM), F32),
            shape((length, HEAD_DIM), F32),
            shape((groups * 4, length, HEAD_DIM), BF16),
            shape((inner, width), BF16),
            shape((fsdp,) + w_qkv.shape, BF16),
            shape((fsdp,) + w_gate.shape, BF16),
            shape((fsdp,) + w_up.shape, BF16),
            shape(w_out.shape, BF16),
            shape(w_down.shape, BF16),
            shape((length, width), BF16),
        ),
        in_specs=[ANY] * 7 + [VMEM] * 3,
        out_specs=(VMEM,) * 7 + (ANY,) * 11,
        scratch_shapes=[
            pltpu.VMEM((length, width), BF16),
            pltpu.VMEM((seq, 1, rows), jnp.int32),
            pltpu.VMEM((2, share), F32),
            pltpu.VMEM((fsdp, seq, 2, share), F32),
            pltpu.VMEM((fsdp,) + w_out.shape, BF16),
        ]
        + scatter_scratch(seq, rows, width)[:3]
        + [
            pltpu.VMEM((length, width), BF16),
            pltpu.VMEM((length, HEAD_DIM), F32),
            pltpu.VMEM((length, HEAD_DIM), F32),
            pltpu.VMEM((groups * 4, length, HEAD_DIM), BF16),
            pltpu.VMEM((inner, width), BF16),
            pltpu.VMEM((fsdp,) + w_qkv.shape, BF16),
            pltpu.VMEM(cot.shape, BF16),
            pltpu.VMEM(w_gate.shape, BF16),
            pltpu.VMEM(w_up.shape, BF16),
            pltpu.VMEM(w_out.shape, BF16),
            pltpu.VMEM(w_down.shape, BF16),
        ]
        + [dma((2,)), dma((6,))]
        + [dma((n_copies(seq),))] * 6
        + line_scratch(fsdp) * 6
        + [dma((1,))] * 6
        + [dma((seq - 1,))] * 4
        + [dma((fsdp - 1,))] * 2,
        compiler_params=params(0),
        name="forward",
    )(hidden, w_qkv, w_out, w_gate, w_up, w_down, cot, ids, gain_one, gain_two)


def feed_kernel(
    seq, fsdp, own_normed, cot_all, w_gate, w_up, middle, w_down, gains, d_middle, own_low, d_gain,
    own_down, out_terms, down_out, g_gate, g_up, normed, whole_down, blocks, g_down, gate, up, hid, d_gate,
    d_up, held, stage, got, grad_tiles, *rest
):
    arrays, rest = rest[:5], rest[5:]
    rows, width = middle.shape
    length = rows * seq
    inner = gate.shape[1]
    me = lax.axis_index("seq")
    tile = tile_of(width, 512)
    wide = tile_of(inner, 512)
    w_gate, w_up, cot, middle = loads((w_gate, w_up, cot_all, middle), arrays[:4], arrays[4])
    meet(seq, fsdp)
    local, tile_sems = rest[0], rest[1]
    whole = Gather(seq, own_normed, normed, rest[2:4])
    sums = Scatter(seq, held, stage, got, rest[4:6])
    half = w_down.shape[0] // 2
    line_down = [
        LineGather(fsdp, w_down, blocks, rest[6:9], pl.ds(0, half)),
        LineGather(fsdp, w_down, blocks, rest[9:12], pl.ds(half, half)),
    ]
    early = fsdp == 8
    if not early:
        g_down = blocks
    line = LineReduce(fsdp, g_down, *rest[12:])
    for exchange in line_down:
        exchange.start()
    whole.start()
    mine = whole.local(local.at[0])
    mine.start()
    w_gate, w_up = w_gate.get(), w_up.get()
    mine.wait()

    def block_of(device):
        return pl.ds(pl.multiple_of(device * rows, rows), rows)

    def first(device):
        block = block_of(device)

        def part(at):
            cols = pl.ds(at, wide)
            gate_part = dot(normed[block, :], w_gate[:, cols])
            up_part = dot(normed[block, :], w_up[:, cols])
            gate[block, cols] = gate_part
            up[block, cols] = up_part
            hid[block, cols] = (gate_part / (1.0 + jnp.exp(-gate_part)) * up_part).astype(BF16)

        each(inner, wide, part)

    first(me)
    whole.forward()
    hooks = [line_down[0].forward, line_down[1].forward]

    def arrived(device):
        first(device)
        run_hook(hooks)

    whole.finish(arrived)
    while hooks:
        run_hook(hooks)
    cot, middle = cot.get(), middle.get()
    height, across = g_down.shape[1:]

    def down_grad(k):
        cols = slice(k * across, (k + 1) * across)
        for down in range(fsdp // seq):
            g_down[line_place(seq, fsdp, down, k)] = dot_tn(
                hid[:, down * height : (down + 1) * height], cot[:, cols]
            ).astype(BF16)

    def join_down():
        for exchange in line_down:
            exchange.finish()
        join_blocks(blocks, seq, whole_down)

    if not early:
        join_down()
    for k in range(seq):
        down_grad(k)
    line.start()
    if early:
        join_down()

    def second(device, out):
        block = block_of(device)

        def part(at):
            cols = pl.ds(at, wide)
            d_hid = dot_nt(cot[block, :], whole_down[cols, :])
            gate_part = gate[block, cols]
            sig = 1.0 / (1.0 + jnp.exp(-gate_part))
            d_gate[block, cols] = (
                d_hid * up[block, cols] * sig * (1.0 + gate_part * (1.0 - sig))
            ).astype(BF16)
            d_up[block, cols] = (d_hid * (gate_part * sig)).astype(BF16)

        each(inner, wide, part)

        def term(at):
            cols = pl.ds(at, tile)
            total = dot_nt(d_gate[block, :], w_gate[cols, :]) + dot_nt(
                d_up[block, :], w_up[cols, :]
            )
            out[:, cols] = total.astype(out.dtype)

        each(width, tile, term)

    sums.send(second, [None, line.pairs])
    second(me, d_middle)
    sums.forward()
    line.forward((0,))
    wide_rows = grad_tiles.shape[1]
    for left, grads in ((d_gate, g_gate), (d_up, g_up)):

        def tile_out(index, grads=grads):
            return pltpu.make_async_copy(
                grad_tiles.at[lax.rem(index, 2)],
                grads.at[pl.ds(pl.multiple_of(index * wide_rows, wide_rows), wide_rows)],
                tile_sems.at[lax.rem(index, 2)],
            )

        def job(index, left=left, tile_out=tile_out):
            @pl.when(index >= 2)
            def _():
                tile_out(index - 2).wait()

            at = pl.multiple_of(index * wide_rows, wide_rows)
            grad_tiles[lax.rem(index, 2)] = dot_tn(
                normed[:, pl.ds(at, wide_rows)], left[...]
            ).astype(BF16)
            tile_out(index).start()

        count = width // wide_rows
        each(count, 1, job)
        for index in range(max(0, count - 2), count):
            tile_out(index).wait()
        if left is d_gate:
            line.forward((1,))

    terms_out = pltpu.make_async_copy(hid if seq == 4 else normed, out_terms, local.at[0])
    down_copy = pltpu.make_async_copy(whole_down, down_out, local.at[1])

    def outward(index):
        block = pl.ds(pl.multiple_of(index * rows, rows), rows)

        def part(at):
            cols = pl.ds(at, tile)
            normed[block, cols] = dot(hid[block, :], whole_down[:, cols]).astype(BF16)

        each(width, tile, part)

    if seq == 4:
        down_copy.start()
    else:
        each(seq, 1, outward)
    terms_out.start()
    sums.finish()
    d_gain[...] = jnp.zeros_like(d_gain)
    base = pl.multiple_of(me * rows, rows)

    def norm(at):
        part = pl.ds(at, 128)
        values = middle[part, :]
        grad = d_middle[part, :] + sums.terms(part)
        scale = inv_rms(values)
        weighted = grad * gains[1:2, :]
        mean = jnp.mean(weighted * values, axis=-1, keepdims=True)
        d_gain[...] += jnp.sum(grad * values * scale, axis=0, keepdims=True)
        total = cot[pl.ds(base + at, 128), :].astype(F32) + scale * (
            weighted - values * (scale * scale) * mean
        )
        d_middle[part, :] = total
        own_low[part, :] = total.astype(BF16)

    each(rows, 128, norm)
    line.finish(own_down)
    terms_out.wait()
    if seq == 4:
        down_copy.wait()


def feed(seq, fsdp, own_normed, cot_all, w_gate, w_up, middle, w_down, gains):
    rows, width = middle.shape
    length = rows * seq
    inner = w_gate.shape[1]
    dma = pltpu.SemaphoreType.DMA
    return pl.pallas_call(
        functools.partial(feed_kernel, seq, fsdp),
        out_shape=(
            shape((rows, width), F32),
            shape((rows, width), BF16),
            shape((1, width), F32),
            shape(w_down.shape, BF16),
            shape((length, inner if seq == 4 else width), BF16),
            shape((inner, width) if seq == 4 else (16, 128), BF16),
            shape((width, inner), BF16),
            shape((width, inner), BF16),
        ),
        in_specs=[ANY] * 6 + [VMEM],
        out_specs=(VMEM,) * 4 + (ANY,) * 4,
        scratch_shapes=[
            pltpu.VMEM((length, width), BF16),
            pltpu.VMEM((inner, width), BF16),
            pltpu.VMEM((fsdp,) + w_down.shape, BF16),
            pltpu.VMEM((fsdp,) + w_down.shape if fsdp == 8 else (1, 16, 128), BF16),
            pltpu.VMEM((length, inner), F32),
            pltpu.VMEM((length, inner), F32),
            pltpu.VMEM((length, inner), BF16),
            pltpu.VMEM((length, inner), BF16),
            pltpu.VMEM((length, inner), BF16),
        ]
        + scatter_scratch(seq, rows, width)[:3]
        + [pltpu.VMEM((2, min(512, inner // 2), inner), BF16)]
        + load_scratch((w_gate, w_up, cot_all, middle))
        + [dma((2,)), dma((2,))]
        + [dma((n_copies(seq),))] * 4
        + line_scratch(fsdp) * 2
        + reduce_scratch(fsdp, *w_down.shape),
        compiler_params=params(1),
        name="feed",
    )(own_normed, cot_all, w_gate, w_up, middle, w_down, gains)


def backward_kernel(
    seq, fsdp, own_low, g_gate, g_up, w_out, attn, packed, lse, cosine, sine, w_qkv, hidden,
    d_middle, out_terms, w_down, middle, own_down, normed, ids_col, ids_row, gain, gain_two, d_input, output,
    own_qkv, own_gate, own_up, home_down, home_out, g_gain_one, g_gain_two, held_out, stage_out,
    got_out, held, stage, got, d_low, d_keys, d_vals, d_packed, grad_out, grad_qkv, mid_down,
    mid_out, own_out, parts, seq_parts, sums_own, fsdp_parts, hid, *rest
):
    def take(count):
        nonlocal rest
        taken, rest = rest[:count], rest[count:]
        return taken

    rows, width = own_low.shape
    length = rows * seq
    groups = packed.shape[0] // 4
    ratio = fsdp // seq
    height, across = grad_out.shape[1:]
    tile, tall = tile_of(width, 512), tile_of(width, 512)
    me, row = lax.axis_index("seq"), lax.axis_index("fsdp")
    arrays = take(10)
    w_out, attn, packed, lse, cosine, sine, w_qkv, hidden, d_middle = loads(
        (w_out, attn, packed, lse, cosine, sine, w_qkv, hidden, d_middle),
        arrays[:9],
        arrays[9],
    )
    local = take(1)[0]
    if seq == 4:
        terms = Load(out_terms, hid, local.at[1])
        w_down = Load(w_down, held, local.at[4])
    else:
        terms = Load(out_terms, held_out, local.at[1])
    middle = Load(middle, output, local.at[2])
    meet(seq, fsdp)
    whole = Gather(seq, own_low, d_low, take(2))
    outs = Scatter(seq, held_out, stage_out, got_out, take(2))
    early = seq != 4
    if early:
        held = held_out
    sums = Scatter(seq, held, stage, got, take(2))
    part_sems = take(4)
    size = len(reduce_scratch(fsdp, 16, 128))
    line_gate = LineReduce(fsdp, g_gate, *take(size), mine=take(2))
    line_up = LineReduce(fsdp, g_up, *take(size), mine=take(2))
    line_out = LineReduce(fsdp, grad_out, *take(size))
    line_qkv = LineReduce(fsdp, grad_qkv, *take(size))
    moves = [
        Home(seq, fsdp, own_down, mid_down, home_down, take(3)),
        Home(seq, fsdp, own_out, mid_out, home_out, take(3)),
    ]
    whole.start()
    here = whole.local(local.at[0])
    here.start()
    line_gate.start()
    line_up.start()
    w_out, attn, packed, lse = w_out.get(), attn.get(), packed.get(), lse.get()
    cosine, sine = cosine.get(), sine.get()
    d_keys[...] = jnp.zeros_like(d_keys)
    d_vals[...] = jnp.zeros_like(d_vals)
    line_gate.pairs()
    here.wait()
    if seq == 4:
        w_down.get()
        terms.get()

        def outward(index):
            block = pl.ds(pl.multiple_of(index * rows, rows), rows)

            def part(at):
                cols = pl.ds(at, tile)
                weight = held[:, :, cols].reshape(hid.shape[1], tile)
                held_out[index, :, cols] = dot(hid[block, :], weight).astype(BF16)

            each(width, tile, part)

        each(seq, 1, outward)
    span = length // 2 + BLOCK

    def send_out():
        if seq != 4:
            terms.get()
        outs.send(lambda device, ref: None)

    def out_grad():
        for k in range(seq):
            part = dot_tn(attn[...], d_low[:, k * across : (k + 1) * across]).astype(BF16)
            for down in range(ratio):
                grad_out[line_place(seq, fsdp, down, k)] = part[
                    down * height : (down + 1) * height
                ]
        line_out.start()

    def attend(index):
        steps = {k: functools.partial(whole.arrive, k) for k in range(1, seq)}
        at_step(index, steps)
        at_step(index, {seq - 1: out_grad})
        start = pl.multiple_of(whole.coming(index) * BLOCK, BLOCK)
        low = pl.multiple_of(jnp.maximum(start - length // 2, 0), BLOCK)
        part, keys = pl.ds(start, BLOCK), pl.ds(low, span)
        d_attn = dot_nt(d_low[part, :], w_out[...]).astype(BF16)
        bias = mask_bias(ids_col, ids_row, start, low, BLOCK, span)
        for group in range(groups):
            base = group * 2 * HEAD_DIM
            queries = jnp.concatenate(
                [packed[group * 4, part, :], packed[group * 4 + 1, part, :]], axis=0
            )
            d_wide = d_attn[:, base : base + 2 * HEAD_DIM]
            product = attn[part, base : base + 2 * HEAD_DIM].astype(F32) * d_wide.astype(F32)
            delta = jnp.concatenate(
                [
                    jnp.sum(product[:, :HEAD_DIM], axis=-1, keepdims=True),
                    jnp.sum(product[:, HEAD_DIM:], axis=-1, keepdims=True),
                ],
                axis=0,
            )
            d_out = jnp.concatenate([d_wide[:, :HEAD_DIM], d_wide[:, HEAD_DIM:]], axis=0)
            logs = jnp.concatenate(
                [
                    lse[part, group * 2 : group * 2 + 1],
                    lse[part, group * 2 + 1 : group * 2 + 2],
                ],
                axis=0,
            )
            key_rows = packed[group * 4 + 2, keys, :]
            scores = dot_nt(queries, key_rows) * SCALE_TWO + bias
            probs = jnp.exp2(scores - logs)
            d_probs = dot_nt(d_out, packed[group * 4 + 3, keys, :])
            d_scores = (probs * (d_probs - delta)).astype(BF16)
            d_vals[group, keys, :] += dot_tn(probs.astype(BF16), d_out)
            d_keys[group, keys, :] += dot_tn(d_scores, queries) * SCALE
            d_query = dot(d_scores, key_rows) * SCALE
            turned = [
                piece * cosine[part, :] - swap_halves(piece) * sine[part, :]
                for piece in (d_query[:BLOCK], d_query[BLOCK:])
            ]
            d_packed[part, group * 4 * HEAD_DIM : group * 4 * HEAD_DIM + 2 * HEAD_DIM] = (
                jnp.concatenate(turned, axis=1).astype(BF16)
            )
            if group == 0:
                at_step(index, {0: whole.forward})

    def passing(index):
        attend(index)
        at_step(
            index,
            {
                0: functools.partial(line_gate.forward, (0,)),
                1: second_step,
                2: third_step,
            },
        )

    def second_step():
        moves[0].start_plane()
        line_up.pairs()
        line_gate.forward((1,))

    def third_step():
        send_out()
        line_up.forward((0,))

    each(seq, 1, passing)
    whole.sent()
    normed = Load(normed, d_low, local.at[3])
    moves[0].finish_plane()
    moves[0].start_line()

    def last(at):
        part = pl.ds(at, BLOCK)
        for group in range(groups):
            d_key = d_keys[group, part, :]
            turned = d_key * cosine[part, :] - swap_halves(d_key) * sine[part, :]
            base = group * 4 * HEAD_DIM + 2 * HEAD_DIM
            d_packed[part, base : base + 2 * HEAD_DIM] = jnp.concatenate(
                [turned, d_vals[group, part, :]], axis=1
            ).astype(BF16)

    each(length, BLOCK, last)
    line_out.pairs()
    normed = normed.get()
    rows_each = grad_qkv.shape[1]

    per = 128 // math.gcd(128, rows_each)

    def weight(index):
        part = pl.ds(pl.multiple_of(index * per * rows_each, per * rows_each), per * rows_each)
        grad = dot_tn(normed[:, part], d_packed[...]).astype(BF16)
        for k in range(per):
            grad_qkv[index * per + k] = grad[k * rows_each : (k + 1) * rows_each]

    each(fsdp // per, 1, weight)
    line_qkv.start()
    w_qkv = w_qkv.get()

    def one(device, at):
        block = pl.ds(pl.multiple_of(device * rows, rows), rows)
        return dot_nt(d_packed[block, :], w_qkv[pl.ds(at, tile), :])

    def term(device, ref):
        def part(at):
            ref[:, pl.ds(at, tile)] = one(device, at).astype(BF16)

        each(width, tile, part)

    def finish_output():
        middle.get()
        outs.finish()

        def total_of(at):
            part = pl.ds(at, 128)
            output[part, :] = (
                output[part, :] + held_out[me, part, :].astype(F32) + outs.terms(part)
            )

        each(rows, 128, total_of)

    if early:
        finish_output()
    sums.send(
        term,
        [outs.forward, functools.partial(line_up.forward, (1,)), line_qkv.pairs],
    )

    def own(at):
        d_input[:, pl.ds(at, tile)] = one(me, at)

    each(width, tile, own)
    hidden, d_middle = hidden.get(), d_middle.get()
    line_out.forward()
    line_gate.finish(own_gate)
    sums.forward()
    line_qkv.forward((0,))
    line_up.finish(own_up)
    if not early:
        finish_output()
    line_out.finish(own_out)
    moves[1].start_plane()
    line_qkv.forward((1,))
    parts[0:1, :] = jnp.zeros((1, width), F32)
    parts[1:2, :] = gain_two[...]
    moves[1].finish_plane()
    moves[1].start_line()
    sums.finish()

    def norm(at):
        part = pl.ds(at, 128)
        values = hidden[part, :].astype(F32)
        grad = d_input[part, :] + sums.terms(part)
        scale = inv_rms(values)
        weighted = grad * gain[0:1, :]
        mean = jnp.mean(weighted * values, axis=-1, keepdims=True)
        parts[0:1, :] += jnp.sum(grad * values * scale, axis=0, keepdims=True)
        d_input[part, :] = d_middle[part, :] + scale * (
            weighted - values * (scale * scale) * mean
        )

    each(rows, 128, norm)
    first = [
        push(parts, seq_parts.at[k], part_sems[:2], k, peer)
        for k, peer in enumerate(others(seq))
    ]
    for copy in first:
        copy.start()
    moves[0].finish_line()
    for copy in first:
        copy.wait()
    total = parts[...]
    for k in range(seq - 1):
        total = total + seq_parts[k]
    sums_own[...] = total
    second = [
        push(
            sums_own,
            fsdp_parts.at[step - 1],
            part_sems[2:],
            step - 1,
            lax.rem(row + step, fsdp),
            "fsdp",
        )
        for step in range(1, fsdp)
    ]
    for copy in second:
        copy.start()
    moves[1].finish_line()
    line_qkv.finish(own_qkv)
    for copy in second:
        copy.wait()
    for step in range(1, fsdp):
        total = total + fsdp_parts[step - 1]
    share = g_gain_one.shape[1]
    turned = pltpu.roll(
        jnp.broadcast_to(total[:, None, :], (2, 8, width)).reshape(16, width),
        lax.rem(width - (row * seq + me) * share, width),
        1,
    )
    g_gain_one[...] = turned[0:1, :share]
    g_gain_two[...] = turned[8:9, :share]


def backward(
    seq, fsdp, own_low, g_gate, g_up, w_out, attn, packed, lse, cosine, sine, normed, w_qkv, hidden,
    d_middle, out_terms, w_down, middle, own_down, ids_col, ids_row, gain, gain_two
):
    rows, width = own_low.shape
    length = rows * seq
    inner = attn.shape[1]
    groups = packed.shape[0] // 4
    height, across = inner // (fsdp // seq), width // seq
    share = width // (seq * fsdp)
    shard = (width // fsdp, w_qkv.shape[1])
    count = home_count(seq, fsdp)
    dma = pltpu.SemaphoreType.DMA
    big = (w_out, attn, packed, lse, cosine, sine, w_qkv, hidden, d_middle)
    return pl.pallas_call(
        functools.partial(backward_kernel, seq, fsdp),
        out_shape=(
            shape((rows, width), F32),
            shape((rows, width), F32),
            shape(shard, BF16),
            shape(g_gate.shape[1:], BF16),
            shape(g_up.shape[1:], BF16),
            shape(own_down.shape, BF16),
            shape((height, across), BF16),
            shape((1, share), F32),
            shape((1, share), F32),
        ),
        in_specs=[ANY] * 17 + [VMEM] * 4,
        out_specs=(VMEM,) * 9,
        scratch_shapes=scatter_scratch(seq, rows, width)[:3]
        + [pltpu.VMEM((seq, rows, width) if seq == 4 else (1, 16, 128), BF16)]
        + scatter_scratch(seq, rows, width)[1:3]
        + [pltpu.VMEM((length, width), BF16)]
        + [pltpu.VMEM((groups, length, HEAD_DIM), F32)] * 2
        + [
            pltpu.VMEM((length, groups * 4 * HEAD_DIM), BF16),
            pltpu.VMEM((fsdp, height, across), BF16),
            pltpu.VMEM((fsdp,) + shard, BF16),
            pltpu.VMEM((count,) + own_down.shape, BF16),
            pltpu.VMEM((count, height, across), BF16),
            pltpu.VMEM((height, across), BF16),
            pltpu.VMEM((2, width), F32),
            pltpu.VMEM((seq - 1, 2, width), F32),
            pltpu.VMEM((2, width), F32),
            pltpu.VMEM((fsdp - 1, 2, width), F32),
            pltpu.VMEM(out_terms.shape if seq == 4 else (16, 128), BF16),
        ]
        + load_scratch(big)
        + [dma((5,))]
        + [dma((n_copies(seq),))] * 6
        + [dma((seq - 1,))] * 2
        + [dma((fsdp - 1,))] * 2
        + (reduce_scratch(fsdp, *g_gate.shape[1:]) + mine_scratch(fsdp, *g_gate.shape[1:]))
        + (reduce_scratch(fsdp, *g_up.shape[1:]) + mine_scratch(fsdp, *g_up.shape[1:]))
        + reduce_scratch(fsdp, height, across)
        + reduce_scratch(fsdp, *shard)
        + home_sems(seq, fsdp) * 2,
        compiler_params=params(2),
        name="backward",
    )(
        own_low, g_gate, g_up, *big, out_terms, w_down, middle, own_down, normed, ids_col, ids_row, gain,
        gain_two,
    )


def widen_kernel(*refs):
    half = len(refs) // 2
    for src, dst in zip(refs[:half], refs[half:]):
        dst[...] = src[...].astype(F32)


def widen(*arrays):
    steps = 2
    specs = [
        pl.BlockSpec((array.shape[0] // steps, array.shape[1]), lambda i: (i, 0))
        if array.shape[0] > 1
        else pl.BlockSpec(array.shape, lambda i: (0, 0))
        for array in arrays
    ]
    return pl.pallas_call(
        widen_kernel,
        grid=(steps,),
        out_shape=tuple(shape(array.shape, F32) for array in arrays),
        in_specs=specs,
        out_specs=tuple(specs),
        compiler_params=params(),
        name="widen",
    )(*arrays)


def body(
    hidden_in, cotangent, segment_ids, w_qkv, w_out, w_gate, w_up, w_down, gain_attn, gain_mlp
):
    rows, width = hidden_in.shape
    fsdp = lax.axis_size("fsdp")
    seq = lax.axis_size("seq")
    length = rows * seq

    (
        ids_row, ids_col, gains, attn, lse, middle, normed_two, normed_one, cosine, sine, packed,
        rows_out, cols_qkv, cols_gate, cols_up, _, moved_down, cot_all,
    ) = forward(
        seq, fsdp, hidden_in, w_qkv, w_out, w_gate, w_up, w_down, cotangent, segment_ids,
        gain_attn.reshape(1, -1), gain_mlp.reshape(1, -1),
    )
    d_middle, own_low, part_two, own_down, out_terms, rows_down, g_gate, g_up = feed(
        seq, fsdp, normed_two, cot_all, cols_gate.reshape(width, -1), cols_up.reshape(width, -1),
        middle, moved_down, gains,
    )
    if seq == 4:
        rows_down = rows_down.reshape(seq, rows, width)
    else:
        out_terms = out_terms.reshape(seq, rows, width)
    g_up = g_up.reshape((fsdp,) + w_up.shape)
    results = backward(
        seq, fsdp, own_low, g_gate.reshape((fsdp,) + w_gate.shape), g_up, rows_out, attn, packed,
        lse, cosine, sine, normed_one, cols_qkv.reshape(width, -1), hidden_in, d_middle, out_terms, rows_down,
        middle, own_down, ids_col, ids_row, gains, part_two,
    )
    d_input, output, g_qkv, g_gate, g_up, g_down, g_out, g_gain_one, g_gain_two = widen(*results)
    return (
        output, d_input, g_qkv, g_out, g_gate, g_up, g_down, g_gain_one.reshape(-1),
        g_gain_two.reshape(-1),
    )


def solution(mesh):
    both = P(("fsdp", "seq"), None)
    split = P("fsdp", "seq")
    gain = P(("fsdp", "seq"))
    in_specs = (both, both, split, split, split, split, split, split, gain, gain)
    out_specs = (both, both, split, split, split, split, split, gain, gain)
    return jax.shard_map(body, mesh=mesh, in_specs=in_specs, out_specs=out_specs, check_vma=False)
```
